32 devices in a mesh: seq: 32 (over z, y, x, core).
Axes of the slice: x: 2, y: 2, z: 4, core: 2. Of those that a mesh axis runs over, the one named last changes fastest.
Arguments:
- tokens: bfloat16 [4, 2048, 768], P(None, 'seq'), may hold values from -6 to 6
- doc_lengths: int32 [4, 16], replicated, may hold values from 1 to 512, 2048 in all within a row
- first_gain: float32 [768], replicated, may hold values from 0.5 to 1.5
- first_shift: float32 [768], replicated, may hold values from -1.75 to 1.75
- input_weight: bfloat16 [768, 2304], replicated, may hold values from -0.21875 to 0.21875
- input_bias: float32 [2304], replicated, may hold values from -1.75 to 1.75
- short_kernel: float32 [3, 2304], replicated, may hold values from -3.5 to 3.5
- short_bias: float32 [2304], replicated, may hold values from -1.75 to 1.75
- embed_weight: float32 [33, 64], replicated, may hold values from -2 to 2
- embed_bias: float32 [64], replicated, may hold values from -3.140625 to 3.140625
- inner_weight: float32 [64, 64], replicated, may hold values from -1.5 to 1.5
- inner_bias: float32 [64], replicated, may hold values from -3.140625 to 3.140625
- filter_weight: float32 [64, 768], replicated, may hold values from -0.03125 to 0.03125
- decay_rates: float32 [768], replicated, may hold values from 3.07 to 15.35
- filter_bias: float32 [768], replicated, may hold values from -3 to 3
- output_weight: bfloat16 [768, 768], replicated, may hold values from -0.21875 to 0.21875
- output_bias: float32 [768], replicated, may hold values from -1.75 to 1.75
- second_gain: float32 [768], replicated, may hold values from 0.5 to 1.5
- second_shift: float32 [768], replicated, may hold values from -1.75 to 1.75
- up_weight: bfloat16 [768, 3072], replicated, may hold values from -0.21875 to 0.21875
- up_bias: float32 [3072], replicated, may hold values from -1.75 to 1.75
- down_weight: bfloat16 [3072, 768], replicated, may hold values from -0.109375 to 0.109375
- down_bias: float32 [768], replicated, may hold values from -1.75 to 1.75
- cotangent: bfloat16 [4, 2048, 768], P(None, 'seq'), may hold values from -6 to 6
Outputs:
- output: bfloat16 [4, 2048, 768], P(None, 'seq')
- grad_tokens: bfloat16 [4, 2048, 768], P(None, 'seq')
- grad_first_gain: float32 [768], replicated
- grad_first_shift: float32 [768], replicated
- grad_input_weight: float32 [768, 2304], replicated
- grad_input_bias: float32 [2304], replicated
- grad_short_kernel: float32 [3, 2304], replicated
- grad_short_bias: float32 [2304], replicated
- grad_embed_weight: float32 [33, 64], replicated
- grad_embed_bias: float32 [64], replicated
- grad_inner_weight: float32 [64, 64], replicated
- grad_inner_bias: float32 [64], replicated
- grad_filter_weight: float32 [64, 768], replicated
- grad_decay_rates: float32 [768], replicated
- grad_filter_bias: float32 [768], replicated
- grad_output_weight: float32 [768, 768], replicated
- grad_output_bias: float32 [768], replicated
- grad_second_gain: float32 [768], replicated
- grad_second_shift: float32 [768], replicated
- grad_up_weight: float32 [768, 3072], replicated
- grad_up_bias: float32 [3072], replicated
- grad_down_weight: float32 [3072, 768], replicated
- grad_down_bias: float32 [768], replicated
The draws below stay inside these ranges and needn't reach their ends.
Inputs may be any that keep to these rules, and one draw needn't show every extreme that they name: `doc_lengths`: the lengths of one sequence add up to 2048, and the longest document of each sequence has exactly 512 positions.
All inputs are finite; a program needn't handle non-finite values.
Results may differ from the reference program's by a relative error of at most 0.014.
Values may be sent and summed in bfloat16 or wider, within the bound.
A program may use at most 192 MiB of HBM per device.

```python
import functools
import math
import jax
import jax.numpy as jnp
import numpy as np
from jax import lax

D = 768
FF = 3072
FILT = 64
EMB = 33
ROWS = 4
DOCS = 16
LENGTH = 2048


def block_levels(key, extent, cuts, low, high):
    loudness, own = 1.0, jax.random.fold_in(key, 6)
    for dim, blocks in cuts:
        draws = jnp.exp(jax.random.uniform(jax.random.fold_in(own, dim), (blocks,), jnp.float32, low / len(cuts), high / len(cuts)))
        loudness = loudness * jnp.repeat(draws, extent[dim] // blocks).reshape([-1 if axis == dim else 1 for axis in range(len(extent))])
    return loudness


def split_up(count, total, reach, lean):
    weights = [(1 << 20) // math.isqrt(grade ** lean) + 1 for grade in range(2, count + 1)]
    rest, given = total - reach - (count - 1), [1] * (count - 1)
    while rest > 0:
        free = [i for i in range(count - 1) if given[i] < reach]
        whole, left = sum([weights[i] for i in free]), rest
        for i in free:
            extra = min(reach - given[i], max(1, left * weights[i] // whole), rest)
            given[i] = given[i] + extra
            rest = rest - extra
    return np.array([reach] + given)


def ragged(key, number_of, total, reach, lean):
    if number_of == 2:
        one = jax.random.randint(key, (), max(1, total - reach), min(reach, total - 1) + 1)
        return jnp.stack([one, total - one])
    sizes = jnp.asarray(split_up(number_of, total, reach, lean), jnp.int32)
    twos = (number_of - 1) // 2
    donor, sink = sizes[1:1 + 2 * twos:2], sizes[2:2 + 2 * twos:2]
    slack = jnp.minimum(donor - 1, reach - sink)
    moved = jax.random.randint(jax.random.fold_in(key, 1), (twos,), 0, 1 << 20) % (slack + 1)
    sizes = sizes.at[1:1 + 2 * twos:2].set(donor - moved).at[2:2 + 2 * twos:2].set(sink + moved)
    return sizes[jax.random.permutation(jax.random.fold_in(key, 2), number_of)]


def bell_draw(own_key, extent, scale, most, pieces=(), kind=jnp.bfloat16):
    drawn = scale * jax.random.normal(own_key, extent, jnp.float32)
    if pieces:
        drawn = drawn * block_levels(own_key, extent, pieces, -0.22, 0.18)
    return jnp.clip(drawn, -most, most).astype(kind)


def setup_inputs(seed: int = 0) -> dict:
    streams_of = jax.random.split(jax.random.key(seed), 25)
    tokens = bell_draw(streams_of[0], (ROWS, LENGTH, D), 1.0, 6.0, ((1, 32),))
    doc_lengths = jax.vmap(lambda own: ragged(own, DOCS, LENGTH, LENGTH // 4, 2))(jax.random.split(streams_of[1], ROWS)).reshape((ROWS, DOCS)).astype(jnp.int32)
    first_gain = jnp.clip(1.0 + 0.1 * jax.random.normal(streams_of[2], (D,), jnp.float32), 0.5, 1.5)
    first_shift = bell_draw(streams_of[3], (D,), 0.3, 1.75, (), jnp.float32)
    input_weight = bell_draw(streams_of[4], (D, 3 * D), D ** -0.5, 0.21875)
    input_bias = bell_draw(streams_of[5], (3 * D,), 0.3, 1.75, (), jnp.float32)
    short_kernel = bell_draw(streams_of[6], (3, 3 * D), 0.6, 3.5, (), jnp.float32)
    short_bias = bell_draw(streams_of[7], (3 * D,), 0.3, 1.75, (), jnp.float32)
    embed_weight = bell_draw(streams_of[8], (EMB, FILT), (EMB // 4) ** -0.5, 2.0, (), jnp.float32)
    embed_bias = jnp.clip(jax.random.uniform(streams_of[9], (FILT,), jnp.float32, -3.140625, 3.140625), -3.140625, 3.140625)
    inner_weight = bell_draw(streams_of[10], (FILT, FILT), (FILT // 4) ** -0.5, 1.5, (), jnp.float32)
    inner_bias = jnp.clip(jax.random.uniform(streams_of[11], (FILT,), jnp.float32, -3.140625, 3.140625), -3.140625, 3.140625)
    filter_weight = bell_draw(streams_of[12], (FILT, D), (FILT * LENGTH // 4) ** -0.5, 0.03125, (), jnp.float32)
    decay_rates = jnp.clip(jnp.exp(jax.random.uniform(streams_of[13], (D,), jnp.float32, math.log(3.07), math.log(15.35))), 3.07, 15.35)
    filter_bias = bell_draw(streams_of[14], (D,), 0.5, 3.0, (), jnp.float32)
    output_weight = bell_draw(streams_of[15], (D, D), D ** -0.5, 0.21875)
    output_bias = bell_draw(streams_of[16], (D,), 0.3, 1.75, (), jnp.float32)
    second_gain = jnp.clip(1.0 + 0.1 * jax.random.normal(streams_of[17], (D,), jnp.float32), 0.5, 1.5)
    second_shift = bell_draw(streams_of[18], (D,), 0.3, 1.75, (), jnp.float32)
    up_weight = bell_draw(streams_of[19], (D, FF), D ** -0.5, 0.21875)
    up_bias = bell_draw(streams_of[20], (FF,), 0.3, 1.75, (), jnp.float32)
    down_weight = bell_draw(streams_of[21], (FF, D), FF ** -0.5, 0.109375)
    down_bias = bell_draw(streams_of[22], (D,), 0.3, 1.75, (), jnp.float32)
    cotangent = bell_draw(streams_of[23], (ROWS, LENGTH, D), 1.0, 6.0, ((1, 32),))
    return {"tokens": tokens, "doc_lengths": doc_lengths, "first_gain": first_gain, "first_shift": first_shift, "input_weight": input_weight, "input_bias": input_bias, "short_kernel": short_kernel, "short_bias": short_bias, "embed_weight": embed_weight, "embed_bias": embed_bias, "inner_weight": inner_weight, "inner_bias": inner_bias, "filter_weight": filter_weight, "decay_rates": decay_rates, "filter_bias": filter_bias, "output_weight": output_weight, "output_bias": output_bias, "second_gain": second_gain, "second_shift": second_shift, "up_weight": up_weight, "up_bias": up_bias, "down_weight": down_weight, "down_bias": down_bias, "cotangent": cotangent}


HIGHEST_PRECISION = lax.Precision.HIGHEST
EPSILON = 1e-05

@jax.custom_vjp
def low(v):
    return lax.optimization_barrier(v.astype(jnp.bfloat16)).astype(jnp.float32)

@jax.custom_vjp
def low_back(v):
    return v

def low_keep(v):
    return (low(v), None)

def low_pass(kept, grad):
    return (grad,)

def back_keep(v):
    return (v, None)

def back_low(kept, grad):
    return (low(grad),)
low.defvjp(low_keep, low_pass)
low_back.defvjp(back_keep, back_low)

def layer_norm(values, norm_gain, norm_shift):
    center = values - lax.optimization_barrier(jnp.mean(values, axis=-1, keepdims=True))
    spread = lax.optimization_barrier(jnp.mean(center * center, axis=-1, keepdims=True))
    return center * lax.rsqrt(spread + EPSILON) * norm_gain + norm_shift

def embed_positions(positions, length, embed_width):
    band_count = (embed_width - 1) // 2
    harmonic = jnp.arange(1, band_count + 1, dtype=jnp.int32)
    phases = positions[:, None] * harmonic[None, :] % length
    angles = 2.0 * math.pi / length * phases.astype(jnp.float32)
    scaled = positions.astype(jnp.float32)[:, None] / length
    return jnp.concatenate([scaled, jnp.cos(angles), jnp.sin(angles)], axis=1)

def build_filter(embed_weight, embed_bias, inner_weight, inner_bias, filter_weight, decay_rates, embedded=None, scaled_positions=None):
    first_hidden = jnp.sin(jnp.dot(embedded, embed_weight, precision=HIGHEST_PRECISION) + embed_bias)
    second_hidden = jnp.sin(jnp.dot(first_hidden, inner_weight, precision=HIGHEST_PRECISION) + inner_bias)
    raw_filter = jnp.dot(second_hidden, filter_weight, precision=HIGHEST_PRECISION)
    return raw_filter * jnp.exp(-decay_rates[None, :] * scaled_positions[:, None])

def document_masks(length_row):
    doc_ends = jnp.cumsum(length_row)[:-1]
    positions = jnp.arange(LENGTH, dtype=jnp.int32)
    starting = jnp.any(positions[:, None] == doc_ends[None, :], axis=1) | (positions == 0)
    keep_one = jnp.where(starting, 0.0, 1.0).astype(jnp.float32)
    keep_two = keep_one * jnp.concatenate([jnp.zeros((1,), jnp.float32), keep_one[:-1]])
    return (keep_one, keep_two)

def row_forward(weights, token_row, filters, keep_one=None, keep_two=None):
    first_gain, first_shift, input_weight, input_bias, short_kernel, short_bias, filter_bias, output_weight, output_bias, second_gain, second_shift, up_weight, up_bias, down_weight, down_bias = weights
    normed = low(layer_norm(token_row, first_gain, first_shift))
    projected = low(low_back(jnp.dot(normed, input_weight, precision=HIGHEST_PRECISION) + input_bias))
    column_total = projected.shape[1]
    lag_one = jnp.concatenate([jnp.zeros((1, column_total), jnp.float32), projected[:-1]], axis=0)
    lag_two = jnp.concatenate([jnp.zeros((2, column_total), jnp.float32), projected[:-2]], axis=0)
    short_out = short_kernel[0] * projected + short_kernel[1] * keep_one[:, None] * lag_one + short_kernel[2] * keep_two[:, None] * lag_two + short_bias
    gate_zero = short_out[:, :D]
    gate_one = short_out[:, D:2 * D]
    value_part = short_out[:, 2 * D:]
    gated = value_part * gate_one
    fft_length = 2 * LENGTH
    spectrum = jnp.fft.rfft(gated, n=fft_length, axis=0) * jnp.fft.rfft(filters, n=fft_length, axis=0)
    conv = jnp.fft.irfft(spectrum, n=fft_length, axis=0)[:LENGTH] + filter_bias * gated
    mixed = low(conv * gate_zero)
    branch = low_back(jnp.dot(mixed, output_weight, precision=HIGHEST_PRECISION) + output_bias)
    residual = token_row + branch
    normed_two = low(layer_norm(residual, second_gain, second_shift))
    pre_active = low_back(jnp.dot(normed_two, up_weight, precision=HIGHEST_PRECISION) + up_bias)
    hidden = low(jax.nn.gelu(pre_active, approximate=True))
    return residual + jnp.dot(hidden, down_weight, precision=HIGHEST_PRECISION) + down_bias

def reference(tokens, doc_lengths, first_gain, first_shift, input_weight, input_bias, short_kernel, short_bias, embed_weight, embed_bias, inner_weight, inner_bias, filter_weight, decay_rates, filter_bias, output_weight, output_bias, second_gain, second_shift, up_weight, up_bias, down_weight, down_bias, cotangent):
    weights = (first_gain, first_shift, input_weight.astype(jnp.float32), input_bias, short_kernel, short_bias, filter_bias, output_weight.astype(jnp.float32), output_bias, second_gain, second_shift, up_weight.astype(jnp.float32), up_bias, down_weight.astype(jnp.float32), down_bias)
    positions = jnp.arange(LENGTH, dtype=jnp.int32)
    embedded = embed_positions(positions, LENGTH, EMB)
    scaled_positions = positions.astype(jnp.float32) / LENGTH
    filter_fn = functools.partial(build_filter, embedded=embedded, scaled_positions=scaled_positions)
    filters, filter_pullback = jax.vjp(filter_fn, embed_weight, embed_bias, inner_weight, inner_bias, filter_weight, decay_rates)

    def one_row(running, row_inputs):
        token_row, cot_row, length_row = row_inputs
        keep_one, keep_two = document_masks(length_row)
        row_fn = functools.partial(row_forward, keep_one=keep_one, keep_two=keep_two)
        row_out, pullback = jax.vjp(row_fn, weights, token_row.astype(jnp.float32), filters)
        weight_grads, token_grad, filter_grad = pullback(cot_row.astype(jnp.float32))
        summed = jax.tree.map(jnp.add, running[0], weight_grads)
        return ((summed, running[1] + filter_grad), (row_out.astype(jnp.bfloat16), token_grad.astype(jnp.bfloat16)))
    start_state = (jax.tree.map(jnp.zeros_like, weights), jnp.zeros_like(filters))
    final_state, stacked = lax.scan(one_row, start_state, (tokens, cotangent, doc_lengths))
    row_grads, filter_total = final_state
    output, grad_tokens = stacked
    g_first_gain, g_first_shift, g_input_weight, g_input_bias, g_short_kernel, g_short_bias, g_filter_bias, g_output_weight, g_output_bias, g_second_gain, g_second_shift, g_up_weight, g_up_bias, g_down_weight, g_down_bias = row_grads
    g_embed_weight, g_embed_bias, g_inner_weight, g_inner_bias, g_filter_weight, g_decay_rates = filter_pullback(filter_total)
    return (output, grad_tokens, g_first_gain, g_first_shift, g_input_weight, g_input_bias, g_short_kernel, g_short_bias, g_embed_weight, g_embed_bias, g_inner_weight, g_inner_bias, g_filter_weight, g_decay_rates, g_filter_bias, g_output_weight, g_output_bias, g_second_gain, g_second_shift, g_up_weight, g_up_bias, g_down_weight, g_down_bias)
```

```python
import functools
import math

import jax
import jax.numpy as jnp
from jax import lax
from jax.experimental import pallas as pl
from jax.experimental.pallas import tpu as pltpu
from jax.sharding import PartitionSpec as P

MESH = pl.DeviceIdType.MESH
EPSILON = 1e-05


def bit_of(me, bit):
    return lax.rem(lax.div(me, bit), 2)

def partner_of(me, bit):
    return me + bit - 2 * bit * bit_of(me, bit)

def halving_plan(rows, columns, order, row_unit, column_unit=128):
    steps = []
    for bit in order:
        if rows % (2 * row_unit) == 0:
            rows //= 2
            steps.append((bit, "row", rows, columns))
        elif columns % (2 * column_unit) == 0:
            columns //= 2
            steps.append((bit, "column", rows, columns))
        else:
            steps.append((bit, "full", rows, columns))
    return steps

class Reduction:
    def __init__(self, array, plan, inbox, sends, arrivals, free, me):
        self.array, self.plan, self.inbox = array, plan, inbox
        self.sends, self.arrivals, self.free, self.me = sends, arrivals, free, me
        self.row, self.column = 0, 0
        self.origin = []
        for bit, kind, rows, columns in plan:
            mine = bit_of(me, bit)
            keep, give = (self.row, self.column), (self.row, self.column)
            if kind == "row":
                keep = (self.row + mine * rows, self.column)
                give = (self.row + (1 - mine) * rows, self.column)
            elif kind == "column":
                keep = (self.row, self.column + mine * columns)
                give = (self.row, self.column + (1 - mine) * columns)
            self.origin.append((keep, give))
            self.row, self.column = keep
        self.unit_rows = plan[-1][2]
        self.unit_columns = plan[-1][3]
        self.unit_columns = min(p[3] for p in plan)
        self.unit_rows = min(p[2] for p in plan)

    def window(self, ref, origin, rows, columns):
        row, column = origin
        if not isinstance(row, int):
            row = pl.multiple_of(row, self.unit_rows)
        if not isinstance(column, int):
            column = pl.multiple_of(column, self.unit_columns)
        return ref.at[pl.ds(row, rows), pl.ds(column, columns)]

    def give_copy(self, s):
        bit, kind, rows, columns = self.plan[s]
        return pltpu.make_async_remote_copy(
            src_ref=self.window(self.array, self.origin[s][1], rows, columns),
            dst_ref=self.inbox[s],
            send_sem=self.sends.at[s], recv_sem=self.arrivals.at[s],
            device_id=(partner_of(self.me, bit),), device_id_type=MESH)

    def share_copy(self, s):
        bit, kind, rows, columns = self.plan[s]
        here = self.window(self.array, self.origin[s][0], rows, columns)
        n = len(self.plan)
        return pltpu.make_async_remote_copy(
            src_ref=here, dst_ref=here,
            send_sem=self.sends.at[n + s], recv_sem=self.arrivals.at[n + s],
            device_id=(partner_of(self.me, bit),), device_id_type=MESH)

    def give(self, s):
        self.give_copy(s).start()

    def take(self, s):
        self.give_copy(s).wait()
        bit, kind, rows, columns = self.plan[s]
        if kind != "full":
            pl.semaphore_signal(
                self.free.at[s], inc=1, device_id=(partner_of(self.me, bit),), device_id_type=MESH
            )
        row, column = self.origin[s][0]
        if not isinstance(column, int):
            column = pl.multiple_of(column, self.unit_columns)
        chunk = self.unit_rows
        inbox = self.inbox[s]
        array = self.array
        def body(i, carry):
            at = pl.multiple_of(i * chunk, chunk)
            here = (pl.ds(pl.multiple_of(row + at, chunk), chunk), pl.ds(column, columns))
            total = array[here].astype(jnp.float32) + inbox[pl.ds(at, chunk), :].astype(jnp.float32)
            array[here] = total.astype(array.dtype)
            return carry
        lax.fori_loop(0, rows // chunk, body, 0)

    def share(self, s):
        if self.plan[s][1] != "full":
            pl.semaphore_wait(self.free.at[s], 1)
            self.share_copy(s).start()

    def collect(self, s):
        if self.plan[s][1] != "full":
            self.share_copy(s).wait()

def inbox_shapes(plan, dtype):
    return [pltpu.VMEM((rows, columns), dtype) for _, _, rows, columns in plan]

def greet_partners(me, n):
    barrier = pltpu.get_barrier_semaphore()
    bit = 1
    count = 0
    while bit < n:
        pl.semaphore_signal(barrier, inc=1, device_id=(partner_of(me, bit),), device_id_type=MESH)
        bit *= 2
        count += 1
    pl.semaphore_wait(barrier, count)

def reduce_kernel(plans, *refs):
    k = len(plans)
    ins, outs, refs = refs[:k], refs[k:2 * k], refs[2 * k:]
    arrays, refs = refs[:k], refs[k:]
    inboxes = []
    for plan in plans:
        inboxes.append(refs[:len(plan)])
        refs = refs[len(plan):]
    sends, refs = refs[:k], refs[k:]
    arrivals, refs = refs[:k], refs[k:]
    free, refs = refs[:k], refs[k:]
    load_sem, store_sem = refs
    me = lax.axis_index("seq")
    n = lax.axis_size("seq")
    loads = [pltpu.make_async_copy(a, b, load_sem.at[i]) for i, (a, b) in enumerate(zip(ins, arrays))]
    for c in loads: c.start()
    greet_partners(me, n)
    work = [Reduction(arrays[i], plans[i], inboxes[i], sends[i], arrivals[i], free[i], me) for i in range(k)]
    steps = len(plans[0])
    for c, w in zip(loads, work):
        c.wait()
        w.give(0)
    for s in range(steps):
        for w in work:
            w.take(s)
            if s + 1 < steps: w.give(s + 1)
            else: w.share(s)
    for s in reversed(range(steps)):
        for w in work:
            w.collect(s)
            if s > 0: w.share(s - 1)
    stores = [pltpu.make_async_copy(b, a, store_sem.at[i]) for i, (a, b) in enumerate(zip(outs, arrays))]
    for c in stores: c.start()
    for c in stores: c.wait()

def default_orders(n):
    bits = []
    b = 1
    while b < n:
        bits.append(b); b *= 2
    core, rest = bits[:1], bits[1:]
    x, y, z = rest[0:1], rest[1:2], rest[2:]
    return [core + x + y + z, core + y + x + z, core + z + x + y]

def all_reduce(arrays, orders, collective_id):
    plans = []
    for a, order in zip(arrays, orders):
        unit = 8 if a.dtype == jnp.float32 else 16
        plans.append(halving_plan(a.shape[0], a.shape[1], order, unit))
    k = len(arrays)
    scratch = [pltpu.VMEM(a.shape, a.dtype) for a in arrays]
    for a, plan in zip(arrays, plans):
        scratch += inbox_shapes(plan, a.dtype)
    for plan in plans + plans:
        scratch.append(pltpu.SemaphoreType.DMA((2 * len(plan),)))
    for plan in plans:
        scratch.append(pltpu.SemaphoreType.REGULAR((len(plan),)))
    scratch += [pltpu.SemaphoreType.DMA((k,)), pltpu.SemaphoreType.DMA((k,))]
    return pl.pallas_call(
        functools.partial(reduce_kernel, plans),
        out_shape=[jax.ShapeDtypeStruct(a.shape, a.dtype) for a in arrays],
        in_specs=[pl.BlockSpec(memory_space=pl.ANY)] * k,
        out_specs=[pl.BlockSpec(memory_space=pl.ANY)] * k,
        scratch_shapes=scratch,
        compiler_params=pltpu.CompilerParams(collective_id=collective_id, has_side_effects=True, vmem_limit_bytes=62 << 20),
        name="reduce_gradients",
    )(*arrays)


HIGHEST = lax.Precision.HIGHEST
LANES = 128

def ceil8(v):
    return -(-v // 8) * 8

def sin_cos(x):
    turns = jnp.round(x * (2.0 / math.pi))
    r = ((x - turns * 1.5703125) - turns * 4.837512969970703125e-4) - turns * 7.54978995489188e-8
    quadrant = turns.astype(jnp.int32)
    z = r * r
    s = ((-1.9515295891e-4 * z + 8.3321608736e-3) * z - 1.6666654611e-1) * z * r + r
    c = ((2.443315711809948e-5 * z - 1.388731625493765e-3) * z + 4.166664568298827e-2) * z * z - 0.5 * z + 1.0
    swap = (quadrant & 1) == 1
    sin_part = jnp.where(swap, c, s)
    cos_part = jnp.where(swap, s, c)
    sin_out = jnp.where((quadrant & 2) == 2, -sin_part, sin_part)
    cos_out = jnp.where(((quadrant + 1) & 2) == 2, -cos_part, cos_part)
    return sin_out, cos_out

def dot(a, b, ca, cb, precision=None):
    return lax.dot_general(a, b, (((ca,), (cb,)), ((), ())), precision=precision, preferred_element_type=jnp.float32)

class Sizes:
    def __init__(self, n, rows, local, width, emb, filt):
        self.n, self.rows, self.local, self.width, self.emb, self.filt = n, rows, local, width, emb, filt
        self.length = n * local
        self.cpd = width // n
        self.cpad = ceil8(self.cpd)
        self.nb = self.length // LANES
        self.tokens = rows * local
        self.tiles = self.tokens // LANES
        self.erows = ceil8(emb)
        assert local * 2 == LANES and rows == 4

def own_selection(z, me):
    want = lax.broadcasted_iota(jnp.int32, (z.cpad, z.width), 0)
    have = lax.broadcasted_iota(jnp.int32, (z.cpad, z.width), 1)
    return jnp.where((have == want + me * z.cpd) & (want < z.cpd), 1.0, 0.0).astype(jnp.float32)

def embed_rows(z, at, count):
    row = lax.broadcasted_iota(jnp.int32, (z.erows, count), 0)
    t = at + lax.broadcasted_iota(jnp.int32, (z.erows, count), 1)
    bands = (z.emb - 1) // 2
    harmonic = jnp.where(row <= bands, row, row - bands)
    angle = lax.rem(t * harmonic, z.length).astype(jnp.float32) * (2.0 * math.pi / z.length)
    s, c = sin_cos(angle)
    scaled = t.astype(jnp.float32) / z.length
    return jnp.where(row == 0, scaled, jnp.where(row <= bands, c, jnp.where(row < z.emb, s, 0.0)))

def columns(ref, count):
    eye = (lax.broadcasted_iota(jnp.int32, (count, count), 0) == lax.broadcasted_iota(jnp.int32, (count, count), 1)).astype(jnp.float32)
    return dot(eye, jnp.broadcast_to(ref[...], (8, count)), 1, 1, HIGHEST)[:, 0:1]

CHUNK = 512

def filter_forward(z, me, w, keep):
    select = own_selection(z, me)
    own_filter = dot(select, w["filter_weight"][...], 1, 1, HIGHEST)
    own_decay = dot(select, jnp.broadcast_to(w["decay_rates"][...], (8, z.width)), 1, 1, HIGHEST)[:, 0:1]
    keep["own_filter"][...] = own_filter
    keep["own_decay"][...] = jnp.broadcast_to(own_decay, (z.cpad, LANES))
    keep["embed_pad"][...] = jnp.zeros((z.erows, z.filt), jnp.float32)
    keep["embed_pad"][0:z.emb, :] = w["embed_weight"][...]
    bias_one = columns(w["embed_bias"], z.filt)
    bias_two = columns(w["inner_bias"], z.filt)
    def body(i, carry):
        at = pl.multiple_of(i * CHUNK, CHUNK)
        here = (slice(None), pl.ds(at, CHUNK))
        embedded = embed_rows(z, at, CHUNK)
        s1, c1 = sin_cos(dot(keep["embed_pad"][...], embedded, 0, 0, HIGHEST) + bias_one)
        s2, c2 = sin_cos(dot(w["inner_weight"][...], s1, 0, 0, HIGHEST) + bias_two)
        raw = dot(own_filter, s2, 1, 0, HIGHEST)
        scaled = (at + lax.broadcasted_iota(jnp.int32, (z.cpad, CHUNK), 1)).astype(jnp.float32) / z.length
        keep["s1"][here] = s1
        keep["c1"][here] = c1
        keep["s2"][here] = s2
        keep["c2"][here] = c2
        keep["taps"][here] = raw * jnp.exp(-own_decay * scaled)
        return carry
    lax.fori_loop(0, z.length // CHUNK, body, 0)

def filter_backward(z, me, w, keep, grad_taps, sums):
    own_filter = keep["own_filter"][...]
    own_decay = keep["own_decay"][:, 0:1]
    for name in ("decay", "filter", "inner", "inner_bias", "embed", "embed_bias"):
        sums[name][...] = jnp.zeros(sums[name].shape, jnp.float32)
    def body(i, carry):
        at = pl.multiple_of(i * CHUNK, CHUNK)
        here = (slice(None), pl.ds(at, CHUNK))
        scaled = (at + lax.broadcasted_iota(jnp.int32, (z.cpad, CHUNK), 1)).astype(jnp.float32) / z.length
        grad = grad_taps[here]
        sums["decay"][...] += jnp.broadcast_to(-jnp.sum(grad * keep["taps"][here] * scaled, axis=1, keepdims=True), (z.cpad, LANES))
        grad_raw = grad * jnp.exp(-own_decay * scaled)
        s2 = keep["s2"][here]
        sums["filter"][...] += dot(grad_raw, s2, 1, 1, HIGHEST)
        two = dot(own_filter, grad_raw, 0, 0, HIGHEST) * keep["c2"][here]
        s1 = keep["s1"][here]
        sums["inner"][...] += dot(s1, two, 1, 1, HIGHEST)
        sums["inner_bias"][...] += jnp.broadcast_to(jnp.sum(two, axis=1, keepdims=True), (z.filt, LANES))
        one = dot(w["inner_weight"][...], two, 1, 0, HIGHEST) * keep["c1"][here]
        sums["embed"][...] += dot(embed_rows(z, at, CHUNK), one, 1, 1, HIGHEST)
        sums["embed_bias"][...] += jnp.broadcast_to(jnp.sum(one, axis=1, keepdims=True), (z.filt, LANES))
        return carry
    lax.fori_loop(0, z.length // CHUNK, body, 0)

def build_toeplitz(z, taps, toeplitz):
    sub = lax.broadcasted_iota(jnp.int32, (8, z.length), 0)
    lane = lax.broadcasted_iota(jnp.int32, (8, LANES), 1)
    sub1 = lax.broadcasted_iota(jnp.int32, (8, LANES), 0)
    def body(c, carry):
        base = jnp.broadcast_to(taps[pl.ds(c, 1), :], (8, z.length))
        for bit in (1, 2, 4):
            base = jnp.where((sub & bit) == bit, pltpu.roll(base, bit, 1), base)
        for q in range(0, LANES // 8, 2):
            parts = []
            for u in (q, q + 1):
                part = pltpu.roll(base, 8 * u, 1) if u else base
                first = jnp.where(lane >= sub1 + 8 * u, part[:, :LANES], 0.0)
                parts.append(jnp.concatenate([first, part[:, LANES:]], axis=1))
            toeplitz[c, 8 * q:8 * q + 16, :] = jnp.concatenate(parts, axis=0).astype(jnp.bfloat16)
        return carry
    lax.fori_loop(0, z.cpd, body, 0)

def fold_toeplitz(z, product):
    lane = lax.broadcasted_iota(jnp.int32, (8, LANES), 1)
    sub1 = lax.broadcasted_iota(jnp.int32, (8, LANES), 0)
    sub = lax.broadcasted_iota(jnp.int32, (8, z.length), 0)
    total = None
    for u in range(LANES // 8):
        part = product[8 * u:8 * u + 8, :]
        first = jnp.where(lane >= sub1 + 8 * u, part[:, :LANES], 0.0)
        part = jnp.concatenate([first, part[:, LANES:]], axis=1)
        part = pltpu.roll(part, z.length - 8 * u, 1) if u else part
        total = part if total is None else total + part
    for bit in (1, 2, 4):
        total = jnp.where((sub & bit) == bit, pltpu.roll(total, z.length - bit, 1), total)
    return jnp.sum(total, axis=0, keepdims=True)

class Exchange:
    def __init__(self, outgoing, incoming, sends, arrivals, me, n):
        self.outgoing, self.incoming, self.sends, self.arrivals, self.me, self.n = outgoing, incoming, sends, arrivals, me, n
    def copy(self, k):
        to = lax.rem(self.me + k, self.n)
        return pltpu.make_async_remote_copy(
            src_ref=self.outgoing.at[to], dst_ref=self.incoming.at[self.me],
            send_sem=self.sends.at[k], recv_sem=self.arrivals.at[k],
            device_id=(to,), device_id_type=MESH)
    def start(self):
        def body(k, carry):
            self.copy(k).start()
            return carry
        lax.fori_loop(1, self.n, body, 0)
        self.incoming[self.me] = self.outgoing[self.me]
    def wait(self):
        def body(k, carry):
            self.copy(k).wait()
            return carry
        lax.fori_loop(1, self.n, body, 0)

def greet_all(me, n):
    barrier = pltpu.get_barrier_semaphore()
    def body(k, carry):
        pl.semaphore_signal(barrier, inc=1, device_id=(lax.rem(me + k, n),), device_id_type=MESH)
        return carry
    lax.fori_loop(1, n, body, 0)
    pl.semaphore_wait(barrier, n - 1)

def each_slab(z, body):
    if z.cpd % 8 == 0:
        lax.fori_loop(0, z.n, body, 0)
    else:
        for k in range(z.n):
            body(k, 0)

def slabs_from_rows(z, flipped, outgoing):
    def body(k, carry):
        at = k * z.cpd
        if z.cpd % 8 == 0:
            at = pl.multiple_of(at, 8)
        slab = flipped[pl.ds(at, z.cpad), :]
        outgoing[k] = jnp.concatenate([slab[:, :LANES], slab[:, LANES:]], axis=0).astype(outgoing.dtype)
        return carry
    each_slab(z, body)

def rows_from_slabs(z, incoming, flipped):
    def body(k, carry):
        at = k * z.cpd
        if z.cpd % 8 == 0:
            at = pl.multiple_of(at, 8)
        slab = incoming[k].astype(jnp.float32)
        flipped[pl.ds(at, z.cpad), :] = jnp.concatenate([slab[:z.cpad], slab[z.cpad:]], axis=1)
        return carry
    each_slab(z, body)

def widen_slabs(z, incoming, wide):
    def body(j, carry):
        wide[pl.ds(pl.multiple_of(j * 2 * z.cpad, 8), 2 * z.cpad), :] = incoming[j].astype(jnp.float32)
        return carry
    lax.fori_loop(0, z.n, body, 0)

def narrow_slabs(z, wide, outgoing):
    def body(j, carry):
        outgoing[j] = wide[pl.ds(pl.multiple_of(j * 2 * z.cpad, 8), 2 * z.cpad), :].astype(outgoing.dtype)
        return carry
    lax.fori_loop(0, z.n, body, 0)

def channel_blocks(z, wide, c):
    lane = lax.broadcasted_iota(jnp.int32, (z.nb, LANES), 1)
    low = lane < LANES // 2
    out = []
    for t in range(2):
        even = wide[pl.ds(t * z.cpad + c, z.nb, 4 * z.cpad), :]
        odd = wide[pl.ds((2 + t) * z.cpad + c, z.nb, 4 * z.cpad), :]
        out.append(jnp.where(low, even, pltpu.roll(odd, LANES // 2, 1)))
        out.append(jnp.where(low, pltpu.roll(even, LANES // 2, 1), odd))
    return out

def put_channel_blocks(z, wide, c, blocks):
    lane = lax.broadcasted_iota(jnp.int32, (z.nb, LANES), 1)
    low = lane < LANES // 2
    for t in range(2):
        a, b = blocks[2 * t], blocks[2 * t + 1]
        wide[pl.ds(t * z.cpad + c, z.nb, 4 * z.cpad), :] = jnp.where(low, a, pltpu.roll(b, LANES // 2, 1))
        wide[pl.ds((2 + t) * z.cpad + c, z.nb, 4 * z.cpad), :] = jnp.where(low, pltpu.roll(a, LANES // 2, 1), b)

def convolve_forward(z, wide, toeplitz, kept, spread):
    def body(c, carry):
        blocks = channel_blocks(z, wide, c)
        x = jnp.concatenate(blocks, axis=0).astype(jnp.bfloat16)
        kept[c] = x
        spread[...] = jnp.zeros(spread.shape, jnp.float32)
        z_all = dot(x, toeplitz[c], 1, 0)
        for d in range(z.nb):
            for r in range(4):
                spread[r, d:d + z.nb, :] += z_all[r * z.nb:(r + 1) * z.nb, d * LANES:(d + 1) * LANES]
        put_channel_blocks(z, wide, c, [spread[r, 0:z.nb, :] for r in range(4)])
        return carry
    lax.fori_loop(0, z.cpd, body, 0)

def convolve_backward(z, wide, toeplitz, kept, spread, advanced, grad_taps):
    spread[...] = jnp.zeros(spread.shape, jnp.float32)
    def body(c, carry):
        blocks = channel_blocks(z, wide, c)
        for r in range(4):
            spread[r, 0:z.nb, :] = blocks[r]
        for d in range(z.nb):
            advanced[:, d * LANES:(d + 1) * LANES] = jnp.concatenate(
                [spread[r, d:d + z.nb, :] for r in range(4)], axis=0).astype(jnp.bfloat16)
        lagged = advanced[...]
        back = dot(lagged, toeplitz[c], 1, 1)
        put_channel_blocks(z, wide, c, [back[r * z.nb:(r + 1) * z.nb] for r in range(4)])
        product = dot(kept[c].astype(jnp.float32).T.astype(jnp.bfloat16), lagged, 1, 0)
        grad_taps[pl.ds(c, 1), :] = fold_toeplitz(z, product)
        return carry
    lax.fori_loop(0, z.cpd, body, 0)

W_NAMES = ("embed_weight", "embed_bias", "inner_weight", "inner_bias", "filter_weight", "decay_rates")
KEEP_NAMES = ("own_filter", "own_decay", "embed_pad", "s1", "c1", "s2", "c2", "taps")

def keep_shapes(z):
    return {"own_filter": (z.cpad, z.filt), "own_decay": (z.cpad, LANES), "embed_pad": (z.erows, z.filt),
            "s1": (z.filt, z.length), "c1": (z.filt, z.length), "s2": (z.filt, z.length), "c2": (z.filt, z.length),
            "taps": (z.cpad, z.length)}

def forward_kernel(z, gated, *refs):
    w = dict(zip(W_NAMES, refs[:6])); refs = refs[6:]
    conv, toeplitz_out, kept, refs = refs[0], refs[1], refs[2], refs[3:]
    keep = dict(zip(KEEP_NAMES, refs[:8])); refs = refs[8:]
    flipped, outgoing, incoming, outgoing2, incoming2, wide, spread, toeplitz, sends, arrivals, sends2, arrivals2, sem = refs
    me = lax.axis_index("seq")
    flipped[z.width:, :] = jnp.zeros((8, z.tokens), jnp.float32)
    flipped[:z.width, :] = gated[...].T
    slabs_from_rows(z, flipped, outgoing)
    greet_all(me, z.n)
    first = Exchange(outgoing, incoming, sends, arrivals, me, z.n)
    first.start()
    filter_forward(z, me, w, keep)
    build_toeplitz(z, keep["taps"], toeplitz)
    first.wait()
    widen_slabs(z, incoming, wide)
    convolve_forward(z, wide, toeplitz, kept, spread)
    narrow_slabs(z, wide, outgoing2)
    second = Exchange(outgoing2, incoming2, sends2, arrivals2, me, z.n)
    second.start()
    out = pltpu.make_async_copy(toeplitz, toeplitz_out, sem)
    out.start()
    second.wait()
    out.wait()
    rows_from_slabs(z, incoming2, flipped)
    conv[...] = flipped[:z.width, :].T

def forward(z, gated, weights, collective_id):
    V = pl.BlockSpec(memory_space=pltpu.VMEM)
    shapes = keep_shapes(z)
    slab = (z.n, 2 * z.cpad, LANES)
    f32, bf16 = jnp.float32, jnp.bfloat16
    outs = [jax.ShapeDtypeStruct((z.tokens, z.width), f32), jax.ShapeDtypeStruct((z.cpd, LANES, z.length), bf16),
            jax.ShapeDtypeStruct((z.cpd, 4 * z.nb, LANES), bf16)] + [jax.ShapeDtypeStruct(shapes[k], f32) for k in KEEP_NAMES]
    return pl.pallas_call(
        functools.partial(forward_kernel, z), out_shape=outs,
        in_specs=[V] * 7, out_specs=[V, pl.BlockSpec(memory_space=pl.ANY)] + [V] * 9,
        scratch_shapes=[pltpu.VMEM((z.width + 8, z.tokens), f32)] + [pltpu.VMEM(slab, bf16)] * 4
        + [pltpu.VMEM((z.n * 2 * z.cpad, LANES), f32), pltpu.VMEM((4, 2 * z.nb, LANES), f32), pltpu.VMEM((z.cpd, LANES, z.length), bf16)]
        + [pltpu.SemaphoreType.DMA((z.n,))] * 4 + [pltpu.SemaphoreType.DMA],
        compiler_params=pltpu.CompilerParams(collective_id=collective_id, has_side_effects=True, vmem_limit_bytes=60 << 20),
        name="convolution_forward")(gated, *weights)

SUM_NAMES = ("decay", "filter", "inner", "inner_bias", "embed", "embed_bias")
def sum_shapes(z):
    return {"decay": (z.cpad, LANES), "filter": (z.cpad, z.filt), "inner": (z.filt, z.filt), "inner_bias": (z.filt, LANES),
            "embed": (z.erows, z.filt), "embed_bias": (z.filt, LANES)}

def backward_kernel(z, grad_conv, *refs):
    w = dict(zip(W_NAMES, refs[:6])); refs = refs[6:]
    toeplitz_in, kept, refs = refs[0], refs[1], refs[2:]
    keep = dict(zip(KEEP_NAMES, refs[:8])); refs = refs[8:]
    grad_gated, refs = refs[0], refs[1:]
    sums = dict(zip(SUM_NAMES, refs[:6])); refs = refs[6:]
    grad_taps, refs = refs[0], refs[1:]
    flipped, outgoing, incoming, outgoing2, incoming2, wide, spread, toeplitz, advanced, sends, arrivals, sends2, arrivals2, sem = refs
    me = lax.axis_index("seq")
    load = pltpu.make_async_copy(toeplitz_in, toeplitz, sem)
    load.start()
    flipped[z.width:, :] = jnp.zeros((8, z.tokens), jnp.float32)
    flipped[:z.width, :] = grad_conv[...].T
    slabs_from_rows(z, flipped, outgoing)
    greet_all(me, z.n)
    first = Exchange(outgoing, incoming, sends, arrivals, me, z.n)
    first.start()
    load.wait()
    first.wait()
    widen_slabs(z, incoming, wide)
    convolve_backward(z, wide, toeplitz, kept, spread, advanced, grad_taps)
    narrow_slabs(z, wide, outgoing2)
    second = Exchange(outgoing2, incoming2, sends2, arrivals2, me, z.n)
    second.start()
    filter_backward(z, me, w, keep, grad_taps, sums)
    second.wait()
    rows_from_slabs(z, incoming2, flipped)
    grad_gated[...] = flipped[:z.width, :].T

def backward(z, grad_conv, weights, saved, collective_id):
    V = pl.BlockSpec(memory_space=pltpu.VMEM)
    slab = (z.n, 2 * z.cpad, LANES)
    f32, bf16 = jnp.float32, jnp.bfloat16
    shapes = sum_shapes(z)
    outs = [jax.ShapeDtypeStruct((z.tokens, z.width), f32)] + [jax.ShapeDtypeStruct(shapes[k], f32) for k in SUM_NAMES] + [jax.ShapeDtypeStruct((z.cpad, z.length), f32)]
    return pl.pallas_call(
        functools.partial(backward_kernel, z), out_shape=outs,
        in_specs=[V] * 7 + [pl.BlockSpec(memory_space=pl.ANY)] + [V] * 9, out_specs=[V] * 8,
        scratch_shapes=[pltpu.VMEM((z.width + 8, z.tokens), f32)] + [pltpu.VMEM(slab, bf16)] * 4
        + [pltpu.VMEM((z.n * 2 * z.cpad, LANES), f32), pltpu.VMEM((4, 2 * z.nb, LANES), f32), pltpu.VMEM((z.cpd, LANES, z.length), bf16), pltpu.VMEM((4 * z.nb, z.length), bf16)]
        + [pltpu.SemaphoreType.DMA((z.n,))] * 4 + [pltpu.SemaphoreType.DMA],
        compiler_params=pltpu.CompilerParams(collective_id=collective_id, has_side_effects=True, vmem_limit_bytes=60 << 20),
        name="convolution_backward")(grad_conv, *weights, *saved)


def from_behind(block, axis, distance):
    devices = range(lax.axis_size(axis))
    route = [(i - distance, i) for i in devices if i - distance in devices]
    return lax.ppermute(block, axis, route)


def shortened(x):
    return jax.tree.map(lambda a: a.astype(jnp.bfloat16) if a.dtype == jnp.float32 else a, x)


def layer_norm(values, norm_gain, norm_shift):
    center = values - jnp.mean(values, axis=-1, keepdims=True)
    spread = jnp.mean(center * center, axis=-1, keepdims=True)
    return center * lax.rsqrt(spread + EPSILON) * norm_gain + norm_shift


def shards(
    tokens,
    doc_lengths,
    first_gain,
    first_shift,
    input_weight,
    input_bias,
    short_kernel,
    short_bias,
    embed_weight,
    embed_bias,
    inner_weight,
    inner_bias,
    filter_weight,
    decay_rates,
    filter_bias,
    output_weight,
    output_bias,
    second_gain,
    second_shift,
    up_weight,
    up_bias,
    down_weight,
    down_bias,
    cotangent,
):
    row_count, local_count, model_width = tokens.shape
    stream_width = 3 * model_width
    device_count = lax.axis_size("seq")
    seq_length = local_count * device_count
    offset = lax.axis_index("seq") * local_count
    positions = offset + jnp.arange(local_count, dtype=jnp.int32)
    doc_ends = jnp.cumsum(doc_lengths, axis=1)[:, :-1]
    starting = jnp.any(positions[None, :, None] == doc_ends[:, None, :], axis=-1) | (
        positions[None, :] == 0
    )
    keep_one = jnp.where(starting, 0.0, 1.0).astype(jnp.float32)
    keep_two = keep_one * jnp.concatenate(
        [jnp.ones((row_count, 1), jnp.float32), keep_one[:, :-1]], axis=1
    )
    keep_one_col = keep_one[:, :, None]
    keep_two_col = keep_two[:, :, None]
    token_values = tokens.astype(jnp.float32)
    first_norm, first_pullback = jax.vjp(layer_norm, token_values, first_gain, first_shift)
    normed = first_norm.astype(jnp.bfloat16)
    projected = (
        jnp.einsum("rsd,de->rse", normed, input_weight, preferred_element_type=jnp.float32)
        + input_bias
    ).astype(jnp.bfloat16)
    rim_rows = jnp.concatenate(
        [projected[:, -2:-1] * keep_one_col[:, -1:].astype(jnp.bfloat16), projected[:, -1:]], axis=1
    )
    previous = from_behind(rim_rows, "seq", 1)
    extended = jnp.concatenate([previous, projected], axis=1).astype(jnp.float32)
    lag_one = extended[:, 1:-1]
    lag_two = extended[:, :-2]
    proj_values = extended[:, 2:]
    short_out = (
        short_kernel[0] * proj_values
        + short_kernel[1] * keep_one_col * lag_one
        + short_kernel[2] * keep_two_col * lag_two
        + short_bias
    )
    gate_zero = short_out[..., :model_width]
    gate_one = short_out[..., model_width : 2 * model_width]
    value_part = short_out[..., 2 * model_width :]
    gated = value_part * gate_one
    z = Sizes(device_count, row_count, local_count, model_width, embed_weight.shape[0], embed_weight.shape[1])
    filter_weights = (embed_weight, embed_bias[None], inner_weight, inner_bias[None], filter_weight, decay_rates[None])
    conv_rows, *saved = forward(z, gated.reshape(-1, model_width), filter_weights, 0)
    conv_rows = conv_rows.reshape(tokens.shape)
    conv_full = conv_rows + filter_bias * gated
    mixed_low = (conv_full * gate_zero).astype(jnp.bfloat16)
    branch = (
        jnp.einsum("rsd,de->rse", mixed_low, output_weight, preferred_element_type=jnp.float32)
        + output_bias
    )
    residual = token_values + branch
    second_norm, second_pullback = jax.vjp(layer_norm, residual, second_gain, second_shift)
    normed_two = second_norm.astype(jnp.bfloat16)
    pre_active = (
        jnp.einsum("rsd,df->rsf", normed_two, up_weight, preferred_element_type=jnp.float32)
        + up_bias
    )
    activated, gelu_pullback = jax.vjp(functools.partial(jax.nn.gelu, approximate=True), pre_active)
    hidden = activated.astype(jnp.bfloat16)
    output = (
        residual
        + jnp.einsum("rsf,fd->rsd", hidden, down_weight, preferred_element_type=jnp.float32)
        + down_bias
    ).astype(jnp.bfloat16)
    cot_values = cotangent.astype(jnp.float32)
    grad_down_weight = jnp.einsum(
        "rsf,rsd->fd", hidden, cotangent, preferred_element_type=jnp.float32
    )
    grad_down_bias = jnp.sum(cot_values, axis=(0, 1))
    grad_hidden = jnp.einsum(
        "rsd,fd->rsf", cotangent, down_weight, preferred_element_type=jnp.float32
    )
    grad_pre = gelu_pullback(grad_hidden)[0].astype(jnp.bfloat16)
    grad_up_weight = jnp.einsum(
        "rsd,rsf->df", normed_two, grad_pre, preferred_element_type=jnp.float32
    )
    grad_up_bias = jnp.sum(grad_pre.astype(jnp.float32), axis=(0, 1))
    grad_normed_two = jnp.einsum(
        "rsf,df->rsd", grad_pre, up_weight, preferred_element_type=jnp.float32
    )
    grad_residual_part, grad_second_gain, grad_second_shift = second_pullback(grad_normed_two)
    grad_residual = cot_values + grad_residual_part
    grad_branch = grad_residual.astype(jnp.bfloat16)
    grad_output_weight = jnp.einsum(
        "rsd,rse->de", mixed_low, grad_branch, preferred_element_type=jnp.float32
    )
    grad_output_bias = jnp.sum(grad_branch.astype(jnp.float32), axis=(0, 1))
    grad_mixed = jnp.einsum(
        "rse,de->rsd", grad_branch, output_weight, preferred_element_type=jnp.float32
    )
    grad_conv = grad_mixed * gate_zero
    grad_gate_zero = grad_mixed * conv_full
    grad_filter_bias = jnp.sum(grad_conv * gated, axis=(0, 1))
    grad_gated_rows, *sums = backward(z, grad_conv.reshape(-1, model_width), filter_weights, saved, 1)
    grad_gated_rows = grad_gated_rows.reshape(tokens.shape)
    sums = dict(zip(SUM_NAMES, sums))
    device = lax.axis_index("seq")
    owned = jnp.zeros((z.filt + 1, z.width), jnp.float32)
    own_sums = jnp.concatenate([sums["filter"][: z.cpd].T, sums["decay"][: z.cpd, :1].T], axis=0)
    owned = lax.dynamic_update_slice(owned, own_sums, (0, device * z.cpd))
    grad_gated = grad_gated_rows + filter_bias * grad_conv
    grad_short = jnp.concatenate(
        [grad_gate_zero, grad_gated * value_part, grad_gated * gate_one], axis=-1
    )
    grad_short_bias = jnp.sum(grad_short, axis=(0, 1))
    grad_short_kernel = jnp.stack(
        [
            jnp.sum(grad_short * proj_values, axis=(0, 1)),
            jnp.sum(grad_short * keep_one_col * lag_one, axis=(0, 1)),
            jnp.sum(grad_short * keep_two_col * lag_two, axis=(0, 1)),
        ]
    )
    tap_one = short_kernel[1] * keep_one_col * grad_short
    tap_two = short_kernel[2] * keep_two_col * grad_short
    outgoing = jnp.concatenate([tap_two[:, 0:1], tap_one[:, 0:1] + tap_two[:, 1:2]], axis=1)
    incoming = from_behind(shortened(outgoing), "seq", -1).astype(outgoing.dtype)
    grad_proj = (
        short_kernel[0] * grad_short
        + jnp.concatenate(
            [tap_one[:, 1:], jnp.zeros((row_count, 1, stream_width), jnp.float32)], axis=1
        )
        + jnp.concatenate(
            [tap_two[:, 2:], jnp.zeros((row_count, 2, stream_width), jnp.float32)], axis=1
        )
    )
    rim_terms = jnp.concatenate(
        [
            jnp.zeros((row_count, local_count - 2, stream_width), jnp.float32),
            incoming[:, 0:1] * keep_one_col[:, -1:],
            incoming[:, 1:2],
        ],
        axis=1,
    )
    grad_proj_low = (grad_proj + rim_terms).astype(jnp.bfloat16)
    grad_input_weight = jnp.einsum(
        "rsd,rse->de", normed, grad_proj_low, preferred_element_type=jnp.float32
    )
    grad_input_bias = jnp.sum(grad_proj_low.astype(jnp.float32), axis=(0, 1))
    grad_normed = jnp.einsum(
        "rse,de->rsd", grad_proj_low, input_weight, preferred_element_type=jnp.float32
    )
    grad_token_part, grad_first_gain, grad_first_shift = first_pullback(grad_normed)
    grad_tokens = (grad_residual + grad_token_part).astype(jnp.bfloat16)
    small = [
        grad_first_gain,
        grad_first_shift,
        grad_input_bias,
        grad_short_kernel,
        grad_short_bias,
        sums["embed"][: z.emb],
        sums["embed_bias"][:, 0],
        sums["inner"],
        sums["inner_bias"][:, 0],
        owned,
        grad_filter_bias,
        grad_output_bias,
        grad_second_gain,
        grad_second_shift,
        grad_up_bias,
        grad_down_bias,
    ]
    count = sum(v.size for v in small)
    rows = -(-count // (z.width * 128)) * 128
    packed = jnp.concatenate(
        [v.reshape(-1) for v in small] + [jnp.zeros((rows * z.width - count,), jnp.float32)]
    ).reshape(rows, z.width)
    orders = default_orders(device_count)
    large = [grad_down_weight, grad_up_weight, grad_input_weight, grad_output_weight]
    reduced = all_reduce(
        [v.astype(jnp.bfloat16) for v in large] + [packed],
        [orders[0], orders[1], orders[2], orders[0], orders[1]],
        2,
    )
    grad_down_weight, grad_up_weight, grad_input_weight, grad_output_weight = [
        v.astype(jnp.float32) for v in reduced[:4]
    ]
    flat = reduced[4].reshape(-1)
    parts = []
    at = 0
    for v in small:
        parts.append(flat[at : at + v.size].reshape(v.shape))
        at += v.size
    return (
        output,
        grad_tokens,
        parts[0],
        parts[1],
        grad_input_weight,
        parts[2],
        parts[3],
        parts[4],
        parts[5],
        parts[6],
        parts[7],
        parts[8],
        parts[9][: z.filt],
        parts[9][z.filt],
        parts[10],
        grad_output_weight,
        parts[11],
        parts[12],
        parts[13],
        grad_up_weight,
        parts[14],
        grad_down_weight,
        parts[15],
    )


def solution(mesh):
    return jax.shard_map(
        shards,
        mesh=mesh,
        in_specs=(
            P(None, "seq", None),
            P(),
            P(),
            P(),
            P(),
            P(),
            P(),
            P(),
            P(),
            P(),
            P(),
            P(),
            P(),
            P(),
            P(),
            P(),
            P(),
            P(),
            P(),
            P(),
            P(),
            P(),
            P(),
            P(None, "seq", None),
        ),
        out_specs=(
            P(None, "seq", None),
            P(None, "seq", None),
            P(),
            P(),
            P(),
            P(),
            P(),
            P(),
            P(),
            P(),
            P(),
            P(),
            P(),
            P(),
            P(),
            P(),
            P(),
            P(),
            P(),
            P(),
            P(),
            P(),
            P(),
        ),
        check_vma=False,
    )
```

```python
import functools
import math

import jax
import jax.numpy as jnp
from jax import lax
from jax.experimental import pallas as pl
from jax.experimental.pallas import tpu as pltpu
from jax.sharding import PartitionSpec as P

MESH = pl.DeviceIdType.MESH
EPSILON = 1e-05


def bit_of(me, bit):
    return lax.rem(lax.div(me, bit), 2)

def partner_of(me, bit):
    return me + bit - 2 * bit * bit_of(me, bit)

def halving_plan(rows, columns, order, row_unit, column_unit=128):
    steps = []
    for bit in order:
        if rows % (2 * row_unit) == 0:
            rows //= 2
            steps.append((bit, "row", rows, columns))
        elif columns % (2 * column_unit) == 0:
            columns //= 2
            steps.append((bit, "column", rows, columns))
        else:
            steps.append((bit, "full", rows, columns))
    return steps

class Reduction:
    def __init__(self, array, plan, inbox, sends, arrivals, free, me):
        self.array, self.plan, self.inbox = array, plan, inbox
        self.sends, self.arrivals, self.free, self.me = sends, arrivals, free, me
        self.row, self.column = 0, 0
        self.origin = []
        for bit, kind, rows, columns in plan:
            mine = bit_of(me, bit)
            keep, give = (self.row, self.column), (self.row, self.column)
            if kind == "row":
                keep = (self.row + mine * rows, self.column)
                give = (self.row + (1 - mine) * rows, self.column)
            elif kind == "column":
                keep = (self.row, self.column + mine * columns)
                give = (self.row, self.column + (1 - mine) * columns)
            self.origin.append((keep, give))
            self.row, self.column = keep
        self.unit_rows = plan[-1][2]
        self.unit_columns = plan[-1][3]
        self.unit_columns = min(p[3] for p in plan)
        self.unit_rows = min(p[2] for p in plan)

    def window(self, ref, origin, rows, columns):
        row, column = origin
        if not isinstance(row, int):
            row = pl.multiple_of(row, self.unit_rows)
        if not isinstance(column, int):
            column = pl.multiple_of(column, self.unit_columns)
        return ref.at[pl.ds(row, rows), pl.ds(column, columns)]

    def give_copy(self, s):
        bit, kind, rows, columns = self.plan[s]
        return pltpu.make_async_remote_copy(
            src_ref=self.window(self.array, self.origin[s][1], rows, columns),
            dst_ref=self.inbox[s],
            send_sem=self.sends.at[s], recv_sem=self.arrivals.at[s],
            device_id=(partner_of(self.me, bit),), device_id_type=MESH)

    def share_copy(self, s):
        bit, kind, rows, columns = self.plan[s]
        here = self.window(self.array, self.origin[s][0], rows, columns)
        n = len(self.plan)
        return pltpu.make_async_remote_copy(
            src_ref=here, dst_ref=here,
            send_sem=self.sends.at[n + s], recv_sem=self.arrivals.at[n + s],
            device_id=(partner_of(self.me, bit),), device_id_type=MESH)

    def give(self, s):
        self.give_copy(s).start()

    def take(self, s):
        self.give_copy(s).wait()
        bit, kind, rows, columns = self.plan[s]
        if kind != "full":
            pl.semaphore_signal(
                self.free.at[s], inc=1, device_id=(partner_of(self.me, bit),), device_id_type=MESH
            )
        row, column = self.origin[s][0]
        if not isinstance(column, int):
            column = pl.multiple_of(column, self.unit_columns)
        chunk = self.unit_rows
        inbox = self.inbox[s]
        array = self.array
        def body(i, carry):
            at = pl.multiple_of(i * chunk, chunk)
            here = (pl.ds(pl.multiple_of(row + at, chunk), chunk), pl.ds(column, columns))
            total = array[here].astype(jnp.float32) + inbox[pl.ds(at, chunk), :].astype(jnp.float32)
            array[here] = total.astype(array.dtype)
            return carry
        lax.fori_loop(0, rows // chunk, body, 0)

    def share(self, s):
        if self.plan[s][1] != "full":
            pl.semaphore_wait(self.free.at[s], 1)
            self.share_copy(s).start()

    def collect(self, s):
        if self.plan[s][1] != "full":
            self.share_copy(s).wait()


HIGHEST = lax.Precision.HIGHEST
LANES = 128
PANEL = 2048

def ceil8(v):
    return -(-v // 8) * 8

def sin_cos(x):
    turns = jnp.round(x * (2.0 / math.pi))
    r = ((x - turns * 1.5703125) - turns * 4.837512969970703125e-4) - turns * 7.54978995489188e-8
    quadrant = turns.astype(jnp.int32)
    z = r * r
    s = ((-1.9515295891e-4 * z + 8.3321608736e-3) * z - 1.6666654611e-1) * z * r + r
    c = ((2.443315711809948e-5 * z - 1.388731625493765e-3) * z + 4.166664568298827e-2) * z * z - 0.5 * z + 1.0
    swap = (quadrant & 1) == 1
    sin_part = jnp.where(swap, c, s)
    cos_part = jnp.where(swap, s, c)
    sin_out = jnp.where((quadrant & 2) == 2, -sin_part, sin_part)
    cos_out = jnp.where(((quadrant + 1) & 2) == 2, -cos_part, cos_part)
    return sin_out, cos_out

def dot(a, b, ca, cb, precision=None):
    return lax.dot_general(a, b, (((ca,), (cb,)), ((), ())), precision=precision, preferred_element_type=jnp.float32)

class Sizes:
    def __init__(self, n, rows, local, width, emb, filt, hidden=3072):
        self.hidden, self.block = hidden, hidden // 8
        self.n, self.rows, self.local, self.width, self.emb, self.filt = n, rows, local, width, emb, filt
        self.length = n * local
        self.cpd = width // n
        self.cpad = ceil8(self.cpd)
        self.nb = self.length // LANES
        self.tokens = rows * local
        self.tiles = self.tokens // LANES
        self.erows = ceil8(emb)
        self.panel = min(PANEL, self.length)
        self.panels = self.length // self.panel
        assert local * 2 == LANES and rows == 4

def own_selection(z, me):
    want = lax.broadcasted_iota(jnp.int32, (z.cpad, z.width), 0)
    have = lax.broadcasted_iota(jnp.int32, (z.cpad, z.width), 1)
    return jnp.where((have == want + me * z.cpd) & (want < z.cpd), 1.0, 0.0).astype(jnp.float32)

def embed_rows(z, at, count):
    row = lax.broadcasted_iota(jnp.int32, (z.erows, count), 0)
    t = at + lax.broadcasted_iota(jnp.int32, (z.erows, count), 1)
    bands = (z.emb - 1) // 2
    harmonic = jnp.where(row <= bands, row, row - bands)
    angle = lax.rem(t * harmonic, z.length).astype(jnp.float32) * (2.0 * math.pi / z.length)
    s, c = sin_cos(angle)
    scaled = t.astype(jnp.float32) / z.length
    return jnp.where(row == 0, scaled, jnp.where(row <= bands, c, jnp.where(row < z.emb, s, 0.0)))

def columns(ref, count):
    eye = (lax.broadcasted_iota(jnp.int32, (count, count), 0) == lax.broadcasted_iota(jnp.int32, (count, count), 1)).astype(jnp.float32)
    return dot(eye, jnp.broadcast_to(ref[...], (8, count)), 1, 1, HIGHEST)[:, 0:1]

CHUNK = 512

def filter_setup(z, me, w, keep):
    select = own_selection(z, me)
    keep.own_filter[...] = dot(select, w.filter_weight[...], 1, 1, HIGHEST)
    own_decay = dot(select, jnp.broadcast_to(w.decay_rates[...], (8, z.width)), 1, 1, HIGHEST)[:, 0:1]
    keep.own_decay[...] = jnp.broadcast_to(own_decay, (z.cpad, LANES))
    keep.embed_pad[...] = jnp.zeros((z.erows, z.filt), jnp.float32)
    keep.embed_pad[0:z.emb, :] = w.embed_weight[...]
    keep.bias_one[...] = jnp.broadcast_to(columns(w.embed_bias, z.filt), (z.filt, LANES))
    keep.bias_two[...] = jnp.broadcast_to(columns(w.inner_bias, z.filt), (z.filt, LANES))


def filter_hidden(z, w, keep, at):
    embedded = embed_rows(z, at, CHUNK)
    s1, c1 = sin_cos(dot(keep.embed_pad[...], embedded, 0, 0, HIGHEST) + keep.bias_one[:, 0:1])
    s2, c2 = sin_cos(dot(w.inner_weight[...], s1, 0, 0, HIGHEST) + keep.bias_two[:, 0:1])
    scaled = (at + lax.broadcasted_iota(jnp.int32, (z.cpad, CHUNK), 1)).astype(jnp.float32) / z.length
    window = jnp.exp(-keep.own_decay[:, 0:1] * scaled)
    return embedded, s1, c1, s2, c2, scaled, window


def filter_forward(z, w, keep, begin, end):
    def body(i, carry):
        at = pl.multiple_of(i * CHUNK, CHUNK)
        embedded, s1, c1, s2, c2, scaled, window = filter_hidden(z, w, keep, at)
        keep.taps[:, pl.ds(at, CHUNK)] = dot(keep.own_filter[...], s2, 1, 0, HIGHEST) * window
        return carry
    lax.fori_loop(begin, end, body, 0)

def filter_backward(z, w, keep, grad_taps, sums):
    for ref in vars(sums).values():
        ref[...] = jnp.zeros(ref.shape, jnp.float32)
    def body(i, carry):
        at = pl.multiple_of(i * CHUNK, CHUNK)
        here = (slice(None), pl.ds(at, CHUNK))
        embedded, s1, c1, s2, c2, scaled, window = filter_hidden(z, w, keep, at)
        grad = grad_taps[here]
        decay = -jnp.sum(grad * keep.taps[here] * scaled, axis=1, keepdims=True)
        sums.decay[...] += jnp.broadcast_to(decay, (z.cpad, LANES))
        grad_raw = grad * window
        sums.filter[...] += dot(grad_raw, s2, 1, 1, HIGHEST)
        two = dot(keep.own_filter[...], grad_raw, 0, 0, HIGHEST) * c2
        sums.inner[...] += dot(s1, two, 1, 1, HIGHEST)
        sums.inner_bias[...] += jnp.broadcast_to(jnp.sum(two, axis=1, keepdims=True), (z.filt, LANES))
        one = dot(w.inner_weight[...], two, 1, 0, HIGHEST) * c1
        sums.embed[...] += dot(embedded, one, 1, 1, HIGHEST)
        sums.embed_bias[...] += jnp.broadcast_to(jnp.sum(one, axis=1, keepdims=True), (z.filt, LANES))
        return carry
    lax.fori_loop(0, z.length // CHUNK, body, 0)

def build_toeplitz(z, taps, pool):
    sub = lax.broadcasted_iota(jnp.int32, (8, z.length), 0)
    lane = lax.broadcasted_iota(jnp.int32, (8, LANES), 1)
    sub1 = lax.broadcasted_iota(jnp.int32, (8, LANES), 0)
    def body(c, carry):
        base = jnp.broadcast_to(taps[pl.ds(c, 1), :], (8, z.length))
        for bit in (1, 2, 4):
            base = jnp.where((sub & bit) == bit, pltpu.roll(base, bit, 1), base)
        for q in range(0, LANES // 8, 2):
            parts = []
            for u in (q, q + 1):
                part = pltpu.roll(base, 8 * u, 1) if u else base
                first = jnp.where(lane >= sub1 + 8 * u, part[:, :LANES], 0.0)
                parts.append(jnp.concatenate([first, part[:, LANES:]], axis=1))
            pair = jnp.concatenate(parts, axis=0).astype(jnp.bfloat16)
            for k in range(z.panels):
                at = pl.multiple_of((c * z.panels + k) * LANES, LANES) + 8 * q
                pool[pl.ds(pl.multiple_of(at, 16), 16), :] = pair[:, k * z.panel:(k + 1) * z.panel]
        return carry
    lax.fori_loop(0, z.cpd, body, 0)

def fold_panel(z, k, product, fold):
    lane = lax.broadcasted_iota(jnp.int32, (8, LANES), 1)
    row = lax.broadcasted_iota(jnp.int32, (8, LANES), 0)
    sums, before = None, None
    for u in range(LANES // 8):
        part = product[8 * u:8 * u + 8, :]
        first = part[:, :LANES]
        inside = lane >= row + 8 * u
        part = jnp.concatenate([jnp.where(inside, first, 0.0), part[:, LANES:]], axis=1)
        part = pltpu.roll(part, z.panel - 8 * u, 1) if u else part
        sums = part if sums is None else sums + part
        if k:
            outside = jnp.where(inside, 0.0, first)
            outside = pltpu.roll(outside, LANES - 8 * u, 1) if u else outside
            before = outside if before is None else before + outside
    fold[:, k * z.panel:(k + 1) * z.panel] = sums
    if k:
        fold[:, k * z.panel - LANES:k * z.panel] += before


def fold_rows(z, fold):
    sums = fold[...]
    row = lax.broadcasted_iota(jnp.int32, sums.shape, 0)
    for bit in (1, 2, 4):
        sums = jnp.where((row & bit) == bit, pltpu.roll(sums, z.length - bit, 1), sums)
    return jnp.sum(sums, axis=0, keepdims=True)

class Exchange:
    def __init__(self, outgoing, incoming, sends, arrivals, me, n):
        self.outgoing, self.incoming, self.sends, self.arrivals, self.me, self.n = outgoing, incoming, sends, arrivals, me, n
    def copy(self, k):
        to = lax.rem(self.me + k, self.n)
        return pltpu.make_async_remote_copy(
            src_ref=self.outgoing.at[to], dst_ref=self.incoming.at[self.me],
            send_sem=self.sends.at[k], recv_sem=self.arrivals.at[k],
            device_id=(to,), device_id_type=MESH)
    def start(self):
        def body(k, carry):
            self.copy(k).start()
            return carry
        lax.fori_loop(1, self.n, body, 0)
        self.incoming[self.me] = self.outgoing[self.me]
    def wait(self):
        def body(k, carry):
            self.copy(k).wait()
            return carry
        lax.fori_loop(1, self.n, body, 0)

def each_slab(z, body):
    if z.cpd % 8 == 0:
        lax.fori_loop(0, z.n, body, 0)
    else:
        for k in range(z.n):
            body(k, 0)

def slabs_from_rows(z, flipped, outgoing):
    def body(k, carry):
        at = k * z.cpd
        if z.cpd % 8 == 0:
            at = pl.multiple_of(at, 8)
        slab = flipped[pl.ds(at, z.cpad), :]
        outgoing[k] = jnp.concatenate([slab[:, :LANES], slab[:, LANES:]], axis=0).astype(outgoing.dtype)
        return carry
    each_slab(z, body)

def rows_from_slabs(z, incoming, flipped):
    def body(k, carry):
        at = k * z.cpd
        if z.cpd % 8 == 0:
            at = pl.multiple_of(at, 8)
        slab = incoming[k].astype(jnp.float32)
        flipped[pl.ds(at, z.cpad), :] = jnp.concatenate([slab[:z.cpad], slab[z.cpad:]], axis=1)
        return carry
    each_slab(z, body)

def widen_slabs(z, incoming, wide):
    def body(j, carry):
        wide[pl.ds(pl.multiple_of(j * 2 * z.cpad, 8), 2 * z.cpad), :] = incoming[j].astype(jnp.float32)
        return carry
    lax.fori_loop(0, z.n, body, 0)

def narrow_slabs(z, wide, outgoing):
    def body(j, carry):
        outgoing[j] = wide[pl.ds(pl.multiple_of(j * 2 * z.cpad, 8), 2 * z.cpad), :].astype(outgoing.dtype)
        return carry
    lax.fori_loop(0, z.n, body, 0)

def channel_blocks(z, wide, c):
    lane = lax.broadcasted_iota(jnp.int32, (z.nb, LANES), 1)
    low = lane < LANES // 2
    out = []
    for t in range(2):
        even = wide[pl.ds(t * z.cpad + c, z.nb, 4 * z.cpad), :]
        odd = wide[pl.ds((2 + t) * z.cpad + c, z.nb, 4 * z.cpad), :]
        out.append(jnp.where(low, even, pltpu.roll(odd, LANES // 2, 1)))
        out.append(jnp.where(low, pltpu.roll(even, LANES // 2, 1), odd))
    return out

def put_channel_blocks(z, wide, c, blocks):
    lane = lax.broadcasted_iota(jnp.int32, (z.nb, LANES), 1)
    low = lane < LANES // 2
    for t in range(2):
        a, b = blocks[2 * t], blocks[2 * t + 1]
        wide[pl.ds(t * z.cpad + c, z.nb, 4 * z.cpad), :] = jnp.where(low, a, pltpu.roll(b, LANES // 2, 1))
        wide[pl.ds((2 + t) * z.cpad + c, z.nb, 4 * z.cpad), :] = jnp.where(low, pltpu.roll(a, LANES // 2, 1), b)

def panel_rows(z, c, k):
    return pl.ds(pl.multiple_of((c * z.panels + k) * LANES, LANES), LANES)


def convolve_forward(z, wide, pool, kept, spread):
    each = z.panel // LANES
    def body(c, carry):
        blocks = channel_blocks(z, wide, c)
        x = jnp.concatenate(blocks, axis=0).astype(jnp.bfloat16)
        kept[c] = x
        spread[...] = jnp.zeros(spread.shape, jnp.float32)
        for k in range(z.panels):
            product = dot(x, pool[panel_rows(z, c, k), :], 1, 0)
            for i in range(each):
                d = k * each + i
                for r in range(4):
                    spread[r, d:d + z.nb, :] += product[r * z.nb:(r + 1) * z.nb, i * LANES:(i + 1) * LANES]
        put_channel_blocks(z, wide, c, [spread[r, 0:z.nb, :] for r in range(4)])
        return carry
    lax.fori_loop(0, z.cpd, body, 0)


def convolve_back_channel(z, c, wide, panel_of, kept, spread, advanced, back, fold, grad_taps):
    blocks = channel_blocks(z, wide, c)
    for r in range(4):
        spread[r, 0:z.nb, :] = blocks[r]
    each = z.panel // LANES
    source = kept[c].astype(jnp.float32).T.astype(jnp.bfloat16)
    for k in range(z.panels):
        for i in range(each):
            d = k * each + i
            advanced[:, i * LANES:(i + 1) * LANES] = jnp.concatenate(
                [spread[r, d:d + z.nb, :] for r in range(4)], axis=0).astype(jnp.bfloat16)
        panel = panel_of(c, k)
        product = dot(advanced[...], panel[...], 1, 1)
        back[...] = product if k == 0 else back[...] + product
        fold_panel(z, k, dot(source, advanced[...], 1, 0), fold)
    put_channel_blocks(z, wide, c, [back[r * z.nb:(r + 1) * z.nb, :] for r in range(4)])
    grad_taps[pl.ds(c, 1), :] = fold_rows(z, fold)


class Names:
    def __init__(self, names, values):
        vars(self).update(zip(names, values))


def keep_shapes(z):
    return dict(
        own_filter=(z.cpad, z.filt), own_decay=(z.cpad, LANES), embed_pad=(z.erows, z.filt),
        bias_one=(z.filt, LANES), bias_two=(z.filt, LANES), taps=(z.cpad, z.length),
    )


def sum_shapes(z):
    return dict(
        decay=(z.cpad, LANES), filter=(z.cpad, z.filt), inner=(z.filt, z.filt), inner_bias=(z.filt, LANES),
        embed=(z.erows, z.filt), embed_bias=(z.filt, LANES),
    )


F32, BF16 = jnp.float32, jnp.bfloat16
BLOCKS = 8
WIDE = 256


class Row:
    FIRST_GAIN, FIRST_SHIFT, INPUT_BIAS, SHORT_KERNEL, SHORT_BIAS = 0, 1, 2, 5, 14
    DECAY, FILTER_BIAS, OUTPUT_BIAS, SECOND_GAIN, SECOND_SHIFT, UP_BIAS, DOWN_BIAS = 17, 18, 19, 20, 21, 22, 26
    EMBED_BIAS, INNER_BIAS = 27, 28
    FILTER, NETWORK, TOTAL = 32, 96, 128


def normalize(x):
    center = x - jnp.mean(x, axis=-1, keepdims=True)
    inverse = lax.rsqrt(jnp.mean(center * center, axis=-1, keepdims=True) + EPSILON)
    return center * inverse, inverse


def normalize_back(gradient, gain, unit, inverse):
    q = gradient * gain
    return (q - jnp.mean(q, axis=-1, keepdims=True) - unit * jnp.mean(q * unit, axis=-1, keepdims=True)) * inverse


def as_row(column):
    size = column.shape[0]
    row, lane = (lax.broadcasted_iota(jnp.int32, (size, size), i) for i in range(2))
    return dot(column, jnp.where(row == lane, 1.0, 0.0).astype(F32), 0, 0, HIGHEST)[0:1, :]


def total(x):
    return jnp.sum(x, axis=0, keepdims=True)


def row_masks(z, me, lengths, keep_one, keep_two):
    for r in range(z.rows):
        position = me * z.local + lax.broadcasted_iota(jnp.int32, (z.local, LANES), 0)
        first = position == 0
        second = position == 1
        end = 0
        for j in range(lengths.shape[1] - 1):
            end = end + lengths[r, j]
            first = first | (position == end)
            second = second | (position == end + 1)
        keep_one[r * z.local:(r + 1) * z.local, :] = jnp.where(first, 0.0, 1.0)
        keep_two[r * z.local:(r + 1) * z.local, :] = jnp.where(first | second, 0.0, 1.0)


def lagged(z, values, halo, t, columns):
    row = lax.broadcasted_iota(jnp.int32, (LANES, 1), 0)
    one, two = pltpu.roll(values, 1, 0), pltpu.roll(values, 2, 0)
    for u in range(2):
        r = 2 * t + u
        older, newer = halo[2 * r:2 * r + 1, columns], halo[2 * r + 1:2 * r + 2, columns]
        one = jnp.where(row == u * z.local, newer, one)
        two = jnp.where(row == u * z.local, older, jnp.where(row == u * z.local + 1, newer, two))
    return one, two


def halves(t):
    return slice(t * LANES, (t + 1) * LANES)


class Flow:
    def __init__(self, reduction):
        self.reduction = reduction
        self.steps = len(reduction.plan)
        self.at = -1
    def advance(self):
        s, n, r = self.at, self.steps, self.reduction
        if s < 0:
            r.give(0)
        elif s < n - 1:
            r.take(s)
            r.give(s + 1)
        elif s == n - 1:
            r.take(s)
            r.share(s)
        elif s < 2 * n - 1:
            r.collect(2 * n - 1 - s)
            r.share(2 * n - 2 - s)
        elif s == 2 * n - 1:
            r.collect(0)
        self.at += 1
    @property
    def done(self):
        return self.at >= 2 * self.steps


def advance(*flows):
    for flow in flows:
        if not flow.done:
            flow.advance()


def block_kernel(z, order, schedule, *refs):
    inputs, outs, scratch, fetched, keep_names, sum_names = order
    v = Names(inputs + outs + scratch, refs)
    me = lax.axis_index("seq")
    n = z.n
    d = z.width
    p = Names(fetched, [getattr(v, "v_" + name) for name in fetched])
    def fetch(name):
        source, target = getattr(v, name), getattr(p, name)
        if len(source.shape) == 1:
            target = target.at[0]
        return pltpu.make_async_copy(source, target, v.loads.at[fetched.index(name)])
    late = ("input_weight", "output_weight", "cotangent")
    soon = [name for name in fetched if name not in late]
    for name in soon + list(late):
        fetch(name).start()
    def weight_block(j, slot):
        at = pl.multiple_of(j * z.block, LANES)
        return (
            pltpu.make_async_copy(v.up_weight.at[:, pl.ds(at, z.block)], v.up_slots.at[slot], v.stream.at[0, slot]),
            pltpu.make_async_copy(v.down_weight.at[pl.ds(at, z.block), :], v.down_slots.at[slot], v.stream.at[1, slot]),
        )
    for copy in weight_block(0, 0):
        copy.start()
    barrier = pltpu.get_barrier_semaphore()
    def greet(k, carry):
        pl.semaphore_signal(barrier, inc=1, device_id=(lax.rem(me + k, n),), device_id_type=MESH)
        return carry
    lax.fori_loop(1, n, greet, 0)
    small = v.g_small
    small[0:Row.FILTER, :] = jnp.zeros((Row.FILTER, d), F32)
    small[Row.NETWORK:Row.TOTAL, :] = jnp.zeros((Row.TOTAL - Row.NETWORK, d), F32)
    row_masks(z, me, v.doc_lengths, v.keep_one, v.keep_two)

    for name in soon:
        fetch(name).wait()
    tokens = p.tokens
    for t in range(z.tiles):
        unit, inverse = normalize(tokens[halves(t), :].astype(F32))
        v.unit_one[halves(t), :] = unit
        v.inverse_one[halves(t), :] = jnp.broadcast_to(inverse, (LANES, LANES))
        v.normed[halves(t), :] = (unit * p.first_gain[...] + p.first_shift[...]).astype(BF16)
    fetch("input_weight").wait()
    part = 3 * d // 6
    def project(j, carry):
        here = pl.ds(pl.multiple_of(j * part, LANES), part)
        values = (dot(v.normed[...], p.input_weight[:, here], 1, 0) + p.input_bias[:, here]).astype(BF16)
        v.projected[:, here] = values
        rounded = values.astype(F32)
        for r in range(z.rows):
            last = (r + 1) * z.local
            v.rim_out[2 * r:2 * r + 2, here] = rounded[last - 2:last, :]
        return carry
    lax.fori_loop(0, 6, project, 0)
    pl.semaphore_wait(barrier, n - 1)
    ahead, behind = lax.rem(me + 1, n), lax.rem(me + n - 1, n)
    rim = pltpu.make_async_remote_copy(
        src_ref=v.rim_out, dst_ref=v.rim_in, send_sem=v.rims.at[0], recv_sem=v.rims.at[1],
        device_id=(ahead,), device_id_type=MESH)
    rim.start()
    keep = Names(keep_names, [getattr(v, "k_" + name) for name in keep_names])
    chunks = z.length // CHUNK
    early = chunks // 2
    filter_setup(z, me, p, keep)
    filter_forward(z, p, keep, 0, early)
    rim.wait()

    def short(j, carry):
        inner = pl.ds(pl.multiple_of(j * WIDE, LANES), WIDE)
        for t in range(z.tiles):
            k1, k2 = v.keep_one[halves(t), 0:1], v.keep_two[halves(t), 0:1]
            streams = []
            for s in range(3):
                here = pl.ds(pl.multiple_of(s * d + j * WIDE, LANES), WIDE)
                values = v.projected[halves(t), here].astype(F32)
                one, two = lagged(z, values, v.rim_in, t, here)
                taps = p.short_kernel
                out = (taps[0:1, here] * values + taps[1:2, here] * (k1 * one) + taps[2:3, here] * (k2 * two)
                       + p.short_bias[:, here])
                (v.gate_zero, v.gate_one, v.value_part)[s][halves(t), inner] = out
                streams.append(out)
            v.flipped[inner, halves(t)] = (streams[1] * streams[2]).T
        return carry
    lax.fori_loop(0, d // WIDE, short, 0)
    v.flipped[d:, :] = jnp.zeros((8, z.tokens), F32)

    def exchange(i):
        return Exchange(v.slabs_out.at[i % 2], v.slabs_in.at[i % 2], v.sends.at[i], v.arrivals.at[i], me, n)
    slabs_from_rows(z, v.flipped, v.slabs_out.at[0])
    first = exchange(0)
    first.start()
    filter_forward(z, p, keep, early, chunks)
    build_toeplitz(z, keep.taps, v.pool)
    first.wait()
    widen_slabs(z, v.slabs_in.at[0], v.wide)
    save = pltpu.make_async_copy(v.pool, v.toeplitz_saved, v.saves.at[0])
    save.start()
    convolve_forward(z, v.wide, v.pool, v.kept, v.spread)
    save.wait()
    narrow_slabs(z, v.wide, v.slabs_out.at[1])
    second = exchange(1)
    second.start()
    fetch("output_weight").wait()
    fetch("cotangent").wait()
    cotangent = p.cotangent
    small[Row.DOWN_BIAS:Row.DOWN_BIAS + 1, :] = total(cotangent[...].astype(F32))
    second.wait()
    rows_from_slabs(z, v.slabs_in.at[1], v.flipped)

    def gate(j, carry):
        inner = pl.ds(pl.multiple_of(j * WIDE, LANES), WIDE)
        for t in range(z.tiles):
            gated = v.value_part[halves(t), inner] * v.gate_one[halves(t), inner]
            conv = v.flipped[inner, halves(t)].T + p.filter_bias[:, inner] * gated
            v.conv[halves(t), inner] = conv
            v.mixed[halves(t), inner] = (conv * v.gate_zero[halves(t), inner]).astype(BF16)
        return carry
    lax.fori_loop(0, d // WIDE, gate, 0)
    for t in range(z.tiles):
        branch = dot(v.mixed[halves(t), :], p.output_weight[...], 1, 0) + p.output_bias[...]
        residual = tokens[halves(t), :].astype(F32) + branch
        unit, inverse = normalize(residual)
        v.unit_two[halves(t), :] = unit
        v.inverse_two[halves(t), :] = jnp.broadcast_to(inverse, (LANES, LANES))
        v.normed_two[halves(t), :] = (unit * p.second_gain[...] + p.second_shift[...]).astype(BF16)
        v.residual[halves(t), :] = residual + p.down_bias[...]
    v.grad_normed[...] = jnp.zeros((z.tokens, d), F32)

    flows = {}
    for name in PARTS:
        inboxes = part_inboxes(z, v, name)
        flows[name] = Flow(Reduction(getattr(v, "g_" + name), z.plans[name], inboxes, getattr(v, "sends_" + name), getattr(v, "arrivals_" + name), getattr(v, "free_" + name), me))

    def mlp(j, down_grad, up_grad, first_block):
        slot = lax.rem(j, 2)
        for copy in weight_block(j, slot):
            copy.wait()
        @pl.when(j + 1 < BLOCKS)
        def _():
            for copy in weight_block(j + 1, 1 - slot):
                copy.start()
        up, down = v.up_slots[slot], v.down_slots[slot]
        here = pl.ds(pl.multiple_of(j * z.block, LANES), z.block)
        local = j - first_block
        x = dot(v.normed_two[...], up, 1, 0) + p.up_bias[:, here]
        grad_hidden = dot(cotangent[...], down, 1, 1)
        root = math.sqrt(2.0 / math.pi)
        square = x * x
        curve = jnp.tanh(root * (x + 0.044715 * (square * x)))
        half = 0.5 * (1.0 + curve)
        hidden = (x * half).astype(BF16)
        slope = half + 0.5 * x * (1.0 - curve * curve) * (root * (1.0 + 3.0 * 0.044715 * square))
        grad_pre = (grad_hidden * slope).astype(BF16)
        v.residual[...] += dot(hidden, down, 1, 0)
        v.grad_normed[...] += dot(grad_pre, up, 1, 1)
        down_grad[pl.ds(pl.multiple_of(local * z.block, LANES), z.block), :] = dot(hidden, cotangent[...], 0, 0).astype(BF16)
        up_grad[:, pl.ds(pl.multiple_of(local * z.block, LANES), z.block)] = dot(v.normed_two[...], grad_pre, 0, 0).astype(BF16)
        v.up_sums[:, here] = total(grad_pre.astype(F32))
    def mlp_half(k):
        def body(j, carry):
            mlp(j, getattr(v, "g_down" + str(k)), getattr(v, "g_up" + str(k)), k * BLOCKS // 2)
            return carry
        lax.fori_loop(k * BLOCKS // 2, (k + 1) * BLOCKS // 2, body, 0)
    mlp_half(0)
    advance(flows["down0"], flows["up0"])
    mlp_half(1)
    advance(flows["down1"], flows["up1"])
    wide_rows = v.up_sums.shape[1] // d
    for i in range(wide_rows):
        small[Row.UP_BIAS + i:Row.UP_BIAS + i + 1, :] = v.up_sums[:, i * d:(i + 1) * d]
    v.normed_two[...] = v.residual[...].astype(BF16)
    store_out = pltpu.make_async_copy(v.normed_two, v.output, v.saves.at[1])
    store_out.start()

    gain_sum, shift_sum, bias_sum = 0.0, 0.0, 0.0
    for t in range(z.tiles):
        gradient = v.grad_normed[halves(t), :]
        unit = v.unit_two[halves(t), :]
        gain_sum = gain_sum + total(gradient * unit)
        shift_sum = shift_sum + total(gradient)
        value = cotangent[halves(t), :].astype(F32) + normalize_back(gradient, p.second_gain[...], unit, v.inverse_two[halves(t), 0:1])
        v.residual[halves(t), :] = value
        branch = value.astype(BF16)
        v.grad_branch[halves(t), :] = branch
        bias_sum = bias_sum + total(branch.astype(F32))
    small[Row.SECOND_GAIN:Row.SECOND_GAIN + 1, :] = gain_sum
    small[Row.SECOND_SHIFT:Row.SECOND_SHIFT + 1, :] = shift_sum
    small[Row.OUTPUT_BIAS:Row.OUTPUT_BIAS + 1, :] = bias_sum
    grad_conv, grad_gate_zero = v.unit_two, v.grad_normed
    def mix_back(j, carry):
        inner = pl.ds(pl.multiple_of(j * WIDE, LANES), WIDE)
        sums = jnp.zeros((1, WIDE), F32)
        for t in range(z.tiles):
            grad_mixed = dot(v.grad_branch[halves(t), :], p.output_weight[inner, :], 1, 1)
            back = grad_mixed * v.gate_zero[halves(t), inner]
            grad_conv[halves(t), inner] = back
            grad_gate_zero[halves(t), inner] = grad_mixed * v.conv[halves(t), inner]
            gated = v.value_part[halves(t), inner] * v.gate_one[halves(t), inner]
            sums = sums + total(back * gated)
            v.flipped[inner, halves(t)] = back.T
        small[Row.FILTER_BIAS:Row.FILTER_BIAS + 1, inner] = sums
        return carry
    lax.fori_loop(0, d // WIDE, mix_back, 0)
    slabs_from_rows(z, v.flipped, v.slabs_out.at[0])
    third = exchange(2)
    third.start()
    def load_panel(i):
        saved = v.toeplitz_saved.at[pl.ds(pl.multiple_of(i * LANES, LANES), LANES), :]
        slot = lax.rem(i, 2)
        return pltpu.make_async_copy(saved, v.toeplitz_slots.at[slot], v.stream.at[2, slot])
    load_panel(0).start()
    def panel_of(c, k):
        i = c * z.panels + k
        load_panel(i).wait()
        @pl.when(i + 1 < z.cpd * z.panels)
        def _():
            load_panel(i + 1).start()
        return v.toeplitz_slots.at[lax.rem(i, 2)]
    def out_grad(j, carry):
        inner = pl.ds(pl.multiple_of(j * WIDE, LANES), WIDE)
        v.g_out[:, inner] = dot(v.mixed[...], v.grad_branch[:, inner], 0, 0).astype(BF16)
        return carry
    lax.fori_loop(0, d // WIDE, out_grad, 0)
    def run(step):
        for name in schedule.get(step, ()):
            advance(flows[name])
    run("start")
    third.wait()
    widen_slabs(z, v.slabs_in.at[0], v.wide)
    v.spread[...] = jnp.zeros(v.spread.shape, F32)
    v.grad_taps[...] = jnp.zeros(v.grad_taps.shape, F32)
    pieces = 4
    bounds = [z.cpd * i // pieces for i in range(pieces + 1)]
    def back_channel(c, carry):
        convolve_back_channel(z, c, v.wide, panel_of, v.kept, v.spread, v.advanced, v.back, v.fold, v.grad_taps)
        return carry
    for i in range(pieces):
        lax.fori_loop(bounds[i], bounds[i + 1], back_channel, 0)
        run("piece%d" % i)
    narrow_slabs(z, v.wide, v.slabs_out.at[1])
    fourth = exchange(3)
    fourth.start()
    run("sent")
    sums = Names(sum_names, [getattr(v, "s_" + name) for name in sum_names])
    filter_backward(z, p, keep, v.grad_taps, sums)
    select = own_selection(z, me)
    small[Row.FILTER:Row.NETWORK, :] = dot(sums.filter[...], select, 0, 0, HIGHEST)
    small[Row.DECAY:Row.DECAY + 1, :] = dot(sums.decay[...], select, 0, 0, HIGHEST)[0:1, :]
    half = z.filt // 2
    small[Row.NETWORK:Row.NETWORK + half, 0:z.filt] = sums.inner[0:half, :]
    small[Row.NETWORK:Row.NETWORK + half, LANES:LANES + z.filt] = sums.inner[half:, :]
    small[Row.NETWORK:Row.NETWORK + half, 2 * LANES:2 * LANES + z.filt] = sums.embed[0:half, :]
    small[Row.NETWORK:Row.NETWORK + z.erows - half, 3 * LANES:3 * LANES + z.filt] = sums.embed[half:, :]
    small[Row.EMBED_BIAS:Row.EMBED_BIAS + 1, 0:z.filt] = as_row(sums.embed_bias[...])
    small[Row.INNER_BIAS:Row.INNER_BIAS + 1, 0:z.filt] = as_row(sums.inner_bias[...])
    run("filter")
    fourth.wait()
    rows_from_slabs(z, v.slabs_in.at[1], v.flipped)
    run("back")

    def gate_back(j, carry):
        inner = pl.ds(pl.multiple_of(j * WIDE, LANES), WIDE)
        for t in range(z.tiles):
            grad_gated = v.flipped[inner, halves(t)].T + p.filter_bias[:, inner] * grad_conv[halves(t), inner]
            first_part = grad_gated * v.value_part[halves(t), inner]
            second_part = grad_gated * v.gate_one[halves(t), inner]
            v.gate_one[halves(t), inner] = first_part
            v.value_part[halves(t), inner] = second_part
            for s, value in enumerate((grad_gate_zero[halves(t), inner], first_part, second_part)):
                here = pl.ds(pl.multiple_of(s * d + j * WIDE, LANES), WIDE)
                taps = p.short_kernel
                for u in range(2):
                    r = 2 * t + u
                    lo = u * z.local
                    head = value[lo:lo + 8, :]
                    one = (taps[1:2, here] * v.keep_one[r * z.local:r * z.local + 8, 0:1]) * head
                    two = (taps[2:3, here] * v.keep_two[r * z.local:r * z.local + 8, 0:1]) * head
                    v.rim_back_out[2 * r:2 * r + 1, here] = two[0:1]
                    v.rim_back_out[2 * r + 1:2 * r + 2, here] = one[0:1] + two[1:2]
        return carry
    lax.fori_loop(0, d // WIDE, gate_back, 0)
    rim_back = pltpu.make_async_remote_copy(
        src_ref=v.rim_back_out, dst_ref=v.rim_back_in, send_sem=v.rims.at[2], recv_sem=v.rims.at[3],
        device_id=(behind,), device_id_type=MESH)
    rim_back.start()
    grad_streams = (grad_gate_zero, v.gate_one, v.value_part)
    def short_sums(j, carry):
        inner = pl.ds(pl.multiple_of(j * WIDE, LANES), WIDE)
        for s in range(3):
            here = pl.ds(pl.multiple_of(s * d + j * WIDE, LANES), WIDE)
            acc = [jnp.zeros((1, WIDE), F32)] * 4
            for t in range(z.tiles):
                k1, k2 = v.keep_one[halves(t), 0:1], v.keep_two[halves(t), 0:1]
                values = v.projected[halves(t), here].astype(F32)
                one, two = lagged(z, values, v.rim_in, t, here)
                value = grad_streams[s][halves(t), inner]
                acc[0] = acc[0] + total(value * values)
                acc[1] = acc[1] + total(value * (k1 * one))
                acc[2] = acc[2] + total(value * (k2 * two))
                acc[3] = acc[3] + total(value)
            for i in range(3):
                small[Row.SHORT_KERNEL + 3 * i + s:Row.SHORT_KERNEL + 3 * i + s + 1, inner] = acc[i]
            small[Row.SHORT_BIAS + s:Row.SHORT_BIAS + s + 1, inner] = acc[3]
        return carry
    lax.fori_loop(0, d // WIDE, short_sums, 0)
    run("short")
    rim_back.wait()
    def spread_back(j, carry):
        inner = pl.ds(pl.multiple_of(j * WIDE, LANES), WIDE)
        row = lax.broadcasted_iota(jnp.int32, (LANES, 1), 0)
        for s in range(3):
            here = pl.ds(pl.multiple_of(s * d + j * WIDE, LANES), WIDE)
            taps = p.short_kernel
            sums = jnp.zeros((1, WIDE), F32)
            for t in range(z.tiles):
                k1, k2 = v.keep_one[halves(t), 0:1], v.keep_two[halves(t), 0:1]
                value = grad_streams[s][halves(t), inner]
                one = pltpu.roll((taps[1:2, here] * k1) * value, LANES - 1, 0)
                two = pltpu.roll((taps[2:3, here] * k2) * value, LANES - 2, 0)
                later = one + two
                for u in range(2):
                    r = 2 * t + u
                    last = (u + 1) * z.local - 1
                    far, near = v.rim_back_in[2 * r:2 * r + 1, here], v.rim_back_in[2 * r + 1:2 * r + 2, here]
                    later = jnp.where(row == last, near, jnp.where(row == last - 1, one + far, later))
                low = (taps[0:1, here] * value + later).astype(BF16)
                v.projected[halves(t), here] = low
                sums = sums + total(low.astype(F32))
            small[Row.INPUT_BIAS + s:Row.INPUT_BIAS + s + 1, inner] = sums
        return carry
    lax.fori_loop(0, d // WIDE, spread_back, 0)
    run("spread")
    for k in range(2):
        width = 3 * d // 2
        step = width // 3
        def in_grad(j, carry, k=k):
            here = pl.ds(pl.multiple_of(k * width + j * step, LANES), step)
            there = pl.ds(pl.multiple_of(j * step, LANES), step)
            getattr(v, "g_in" + str(k))[:, there] = dot(v.normed[...], v.projected[:, here], 0, 0).astype(BF16)
            return carry
        lax.fori_loop(0, 3, in_grad, 0)
        advance(flows["in" + str(k)])
    v.conv[...] = jnp.zeros((z.tokens, d), F32)
    def norm_grad(j, carry):
        here = pl.ds(pl.multiple_of(j * part, LANES), part)
        v.conv[...] += dot(v.projected[:, here], p.input_weight[:, here], 1, 1)
        return carry
    lax.fori_loop(0, 6, norm_grad, 0)
    gain_sum, shift_sum = 0.0, 0.0
    store_out.wait()
    for t in range(z.tiles):
        gradient = v.conv[halves(t), :]
        unit = v.unit_one[halves(t), :]
        gain_sum = gain_sum + total(gradient * unit)
        shift_sum = shift_sum + total(gradient)
        value = v.residual[halves(t), :] + normalize_back(gradient, p.first_gain[...], unit, v.inverse_one[halves(t), 0:1])
        v.normed_two[halves(t), :] = value.astype(BF16)
    store_grad = pltpu.make_async_copy(v.normed_two, v.grad_tokens, v.saves.at[2])
    store_grad.start()
    small[Row.FIRST_GAIN:Row.FIRST_GAIN + 1, :] = gain_sum
    small[Row.FIRST_SHIFT:Row.FIRST_SHIFT + 1, :] = shift_sum
    advance(flows["small"])

    stored = {}
    def finish(name):
        flow = flows[name]
        if not flow.done:
            flow.advance()
        if flow.done and name not in stored:
            stored[name] = pltpu.make_async_copy(getattr(v, "g_" + name), getattr(v, "r_" + name), v.saves.at[3 + PARTS.index(name)])
            stored[name].start()
    for names in schedule["tail"]:
        for name in names:
            finish(name)
    while len(stored) < len(PARTS):
        for name in PARTS:
            finish(name)
    for copy in stored.values():
        copy.wait()
    store_grad.wait()


PARTS = ("down0", "up0", "down1", "up1", "out", "in0", "in1", "small")


def part_shapes(z):
    d, f = z.width, z.hidden
    return {
        "down0": ((f // 2, d), BF16), "down1": ((f // 2, d), BF16), "up0": ((d, f // 2), BF16), "up1": ((d, f // 2), BF16),
        "out": ((d, d), BF16), "in0": ((d, 3 * d // 2), BF16), "in1": ((d, 3 * d // 2), BF16), "small": ((Row.TOTAL, d), F32),
    }


def part_plans(z):
    bits = []
    bit = 1
    while bit < z.n:
        bits.append(bit)
        bit *= 2
    core, x, y, rest = bits[:1], bits[1:2], bits[2:3], bits[3:]
    first = core + x + rest[:1] + y + rest[1:]
    second = core + y + rest[:1] + x + rest[1:]
    orders = {"down0": first, "down1": first, "up0": second, "up1": second, "out": first, "in0": first, "in1": second, "small": second}
    shapes = part_shapes(z)
    plans = {}
    for name in PARTS:
        (rows, columns), kind = shapes[name]
        plans[name] = halving_plan(rows, columns, orders[name], 8 if kind == F32 else 16)
    return plans


POOLED = ("up0", "up1", "down0", "down1")


def part_inboxes(z, v, name):
    if name not in POOLED:
        return [getattr(v, "inbox_%s_%d" % (name, s)) for s in range(len(z.plans[name]))]
    d = z.width
    index = POOLED.index(name)
    views = []
    row, column = (index * d, 0) if index < 2 else (2 * d, (index - 2) * d)
    whole = part_shapes(z)[name][0][1]
    for _, _, rows, columns in z.plans[name]:
        views.append(v.pool.at[pl.ds(row, rows), pl.ds(column, columns)])
        if columns == whole:
            row += rows
        else:
            column += columns
    return views


def block(z, inputs, collective_id=0):
    d, f = z.width, z.hidden
    shapes = part_shapes(z)
    keep = keep_shapes(z)
    sums = sum_shapes(z)
    names, specs = [], []
    any_space = pl.BlockSpec(memory_space=pl.ANY)
    for name in inputs:
        names.append(name)
        specs.append(pl.BlockSpec(memory_space=pltpu.SMEM) if name == "doc_lengths" else any_space)
    outs = dict(output=((z.tokens, d), BF16), grad_tokens=((z.tokens, d), BF16))
    for name in PARTS:
        outs["r_" + name] = shapes[name]
    pool = (z.cpd * z.panels * LANES, z.panel)
    outs["toeplitz_saved"] = (pool, BF16)
    scratch = {}
    fetched = tuple(name for name in inputs if name not in ("doc_lengths", "up_weight", "down_weight"))
    for name in fetched:
        shape = inputs[name].shape
        scratch["v_" + name] = pltpu.VMEM(shape if len(shape) > 1 else (1,) + shape, inputs[name].dtype)
    t = z.tokens
    buffers = dict(
        unit_one=((t, d), F32), inverse_one=((t, LANES), F32), normed=((t, d), BF16), projected=((t, 3 * d), BF16),
        rim_out=((8, 3 * d), F32), rim_in=((8, 3 * d), F32), rim_back_out=((8, 3 * d), F32), rim_back_in=((8, 3 * d), F32),
        keep_one=((t, LANES), F32), keep_two=((t, LANES), F32),
        gate_zero=((t, d), F32), gate_one=((t, d), F32), value_part=((t, d), F32),
        flipped=((d + 8, t), F32), slabs_out=((2, z.n, 2 * z.cpad, LANES), BF16), slabs_in=((2, z.n, 2 * z.cpad, LANES), BF16),
        wide=((z.n * 2 * z.cpad, LANES), F32), spread=((4, 2 * z.nb, LANES), F32), kept=((z.cpd, 4 * z.nb, LANES), BF16),
        pool=(pool, BF16),
        conv=((t, d), F32), mixed=((t, d), BF16), unit_two=((t, d), F32), inverse_two=((t, LANES), F32),
        normed_two=((t, d), BF16), residual=((t, d), F32), grad_normed=((t, d), F32),
        up_slots=((2, d, z.block), BF16), down_slots=((2, z.block, d), BF16), up_sums=((1, f), F32),
        grad_branch=((t, d), BF16), toeplitz_slots=((2, LANES, z.panel), BF16), back=((4 * z.nb, LANES), F32), fold=((8, z.length), F32),
        advanced=((4 * z.nb, z.panel), BF16), grad_taps=((z.cpad, z.length), F32),
    )
    for name, (shape, kind) in buffers.items():
        scratch[name] = pltpu.VMEM(shape, kind)
    for name in keep:
        scratch["k_" + name] = pltpu.VMEM(keep[name], F32)
    for name in sums:
        scratch["s_" + name] = pltpu.VMEM(sums[name], F32)
    for name in PARTS:
        scratch["g_" + name] = pltpu.VMEM(*shapes[name])
        if name not in POOLED:
            for s, (_, _, rows, columns) in enumerate(z.plans[name]):
                scratch["inbox_%s_%d" % (name, s)] = pltpu.VMEM((rows, columns), shapes[name][1])
        steps = len(z.plans[name])
        scratch["sends_" + name] = pltpu.SemaphoreType.DMA((2 * steps,))
        scratch["arrivals_" + name] = pltpu.SemaphoreType.DMA((2 * steps,))
        scratch["free_" + name] = pltpu.SemaphoreType.REGULAR((steps,))
    scratch["loads"] = pltpu.SemaphoreType.DMA((len(fetched),))
    scratch["stream"] = pltpu.SemaphoreType.DMA((3, 2))
    scratch["saves"] = pltpu.SemaphoreType.DMA((3 + len(PARTS),))
    scratch["rims"] = pltpu.SemaphoreType.DMA((4,))
    scratch["sends"] = pltpu.SemaphoreType.DMA((4, z.n))
    scratch["arrivals"] = pltpu.SemaphoreType.DMA((4, z.n))
    order = (tuple(names), tuple(outs), tuple(scratch), fetched, tuple(keep), tuple(sums))
    results = pl.pallas_call(
        functools.partial(block_kernel, z, order, SCHEDULE),
        out_shape=[jax.ShapeDtypeStruct(*outs[name]) for name in outs],
        in_specs=specs, out_specs=[any_space] * len(outs),
        scratch_shapes=list(scratch.values()),
        compiler_params=pltpu.CompilerParams(collective_id=collective_id, has_side_effects=True, vmem_limit_bytes=61 << 20),
        name="hyena_block",
    )(*inputs.values())
    return dict(zip(outs, results))


SCHEDULE = {
    "start": ("down0", "up0", "out", "down1", "up1"),
    "piece0": ("out",),
    "piece1": ("down0", "up0", "out"),
    "piece2": ("down1", "up1"),
    "piece3": ("down0", "up0", "out"),
    "sent": ("down1", "up1"),
    "filter": ("down0", "up0", "out"),
    "back": ("down1", "up1"),
    "short": ("down0", "up0", "out"),
    "spread": ("down1", "up1"),
    "tail": (),
}


def finish_layout(z):
    d, f = z.width, z.hidden
    return dict(
        grad_down_weight=((f, d), [("down0", 0, 0), ("down1", f // 2, 0)]),
        grad_up_weight=((d, f), [("up0", 0, 0), ("up1", 0, f // 2)]),
        grad_output_weight=((d, d), [("out", 0, 0)]),
        grad_input_weight=((d, 3 * d), [("in0", 0, 0), ("in1", 0, 3 * d // 2)]),
    )


def small_layout(z):
    d, half = z.width, z.filt // 2
    def line(row, count=1):
        return (count * d,), [(row + i, 0, 1, d, 0, i * d) for i in range(count)]
    def short(row):
        return (z.filt,), [(row, 0, 1, z.filt, 0, 0)]
    return dict(
        grad_first_gain=line(Row.FIRST_GAIN), grad_first_shift=line(Row.FIRST_SHIFT), grad_input_bias=line(Row.INPUT_BIAS, 3),
        grad_short_kernel=((3, 3 * d), [(Row.SHORT_KERNEL + 3 * i + s, 0, 1, d, i, s * d) for i in range(3) for s in range(3)]),
        grad_short_bias=line(Row.SHORT_BIAS, 3),
        grad_embed_weight=((z.emb, z.filt), [
            (Row.NETWORK, 2 * LANES, half, z.filt, 0, 0), (Row.NETWORK, 3 * LANES, z.emb - half, z.filt, half, 0)]),
        grad_embed_bias=short(Row.EMBED_BIAS),
        grad_inner_weight=((z.filt, z.filt), [
            (Row.NETWORK, 0, half, z.filt, 0, 0), (Row.NETWORK, LANES, half, z.filt, half, 0)]),
        grad_inner_bias=short(Row.INNER_BIAS),
        grad_filter_weight=((z.filt, d), [(Row.FILTER, 0, z.filt, d, 0, 0)]),
        grad_decay_rates=line(Row.DECAY), grad_filter_bias=line(Row.FILTER_BIAS), grad_output_bias=line(Row.OUTPUT_BIAS),
        grad_second_gain=line(Row.SECOND_GAIN), grad_second_shift=line(Row.SECOND_SHIFT),
        grad_up_bias=line(Row.UP_BIAS, z.hidden // d), grad_down_bias=line(Row.DOWN_BIAS),
    )


RUN = 192


def finish_kernel(z, order, pieces, *refs):
    weights, little, names = order
    v = Names(names, refs)
    loads, stores = [], []
    for i, (part, name, row, column, at, rows, columns) in enumerate(pieces):
        source, target = getattr(v, "r_" + part), getattr(v, "l_" + part)
        wide, out = getattr(v, "w_" + name), getattr(v, name)
        there = (pl.ds(row, rows), pl.ds(column, columns))
        loads.append(pltpu.make_async_copy(source.at[pl.ds(at, rows), :], target.at[pl.ds(at, rows), :], v.loads.at[i]))
        stores.append(pltpu.make_async_copy(wide.at[there], out.at[there], v.stores.at[i]))
    for copy in loads:
        copy.start()
    others = [
        pltpu.make_async_copy(v.block_output, v.output, v.others.at[0]),
        pltpu.make_async_copy(v.block_grad_tokens, v.grad_tokens, v.others.at[1]),
    ]
    for copy in others:
        copy.start()
    for i, (part, name, row, column, at, rows, columns) in enumerate(pieces):
        loads[i].wait()
        getattr(v, "w_" + name)[row:row + rows, column:column + columns] = getattr(v, "l_" + part)[at:at + rows, :].astype(F32)
        stores[i].start()
    for name, (shape, moves) in small_layout(z).items():
        out = getattr(v, name)
        for row, column, rows, columns, to_row, to_column in moves:
            value = v.r_small[row:row + rows, column:column + columns]
            if len(shape) == 1:
                out[to_column:to_column + columns] = value.reshape(columns)
            else:
                out[to_row:to_row + rows, to_column:to_column + columns] = value
    for copy in stores + others:
        copy.wait()


def finish(z, results):
    layout, little = finish_layout(z), small_layout(z)
    shapes = part_shapes(z)
    pieces = []
    for name in layout:
        for part, row, column in layout[name][1]:
            rows, columns = shapes[part][0]
            for at in range(0, rows, RUN):
                pieces.append((part, name, row + at, column, at, min(RUN, rows - at), columns))
    any_space, vmem = pl.BlockSpec(memory_space=pl.ANY), pl.BlockSpec(memory_space=pltpu.VMEM)
    parts = [part for part in PARTS if part != PARTS[-1]]
    arguments = dict(("r_" + part, results["r_" + part]) for part in PARTS)
    arguments.update(block_output=results["output"], block_grad_tokens=results["grad_tokens"])
    outs = dict((name, jax.ShapeDtypeStruct(layout[name][0], F32)) for name in layout)
    token_shape = jax.ShapeDtypeStruct((z.tokens, z.width), BF16)
    outs.update(output=token_shape, grad_tokens=token_shape)
    outs.update((name, jax.ShapeDtypeStruct(little[name][0], F32)) for name in little)
    scratch = dict(("l_" + part, pltpu.VMEM(*shapes[part])) for part in parts)
    scratch.update(("w_" + name, pltpu.VMEM(layout[name][0], F32)) for name in layout)
    scratch.update(
        loads=pltpu.SemaphoreType.DMA((len(pieces),)), stores=pltpu.SemaphoreType.DMA((len(pieces),)), others=pltpu.SemaphoreType.DMA((2,))
    )
    names = tuple(arguments) + tuple(outs) + tuple(scratch)
    outputs = pl.pallas_call(
        functools.partial(finish_kernel, z, (tuple(layout), tuple(little), names), pieces),
        out_shape=list(outs.values()),
        in_specs=[any_space] * len(parts) + [vmem, any_space, any_space],
        out_specs=[any_space] * (len(layout) + 2) + [vmem] * len(little),
        scratch_shapes=list(scratch.values()),
        compiler_params=pltpu.CompilerParams(vmem_limit_bytes=58 << 20),
        name="widen_gradients",
    )(*arguments.values())
    return Names(outs, outputs)


def shards(
    n, tokens, doc_lengths, first_gain, first_shift, input_weight, input_bias, short_kernel, short_bias, embed_weight, embed_bias,
    inner_weight, inner_bias, filter_weight, decay_rates, filter_bias, output_weight, output_bias, second_gain, second_shift,
    up_weight, up_bias, down_weight, down_bias, cotangent,
):
    rows, local, width = tokens.shape
    z = Sizes(n, rows, local, width, *embed_weight.shape, up_weight.shape[1])
    z.plans = part_plans(z)
    inputs = dict(
        tokens=tokens.reshape(rows * local, width), doc_lengths=doc_lengths, first_gain=first_gain, first_shift=first_shift,
        input_weight=input_weight, input_bias=input_bias, short_kernel=short_kernel, short_bias=short_bias, embed_weight=embed_weight,
        embed_bias=embed_bias, inner_weight=inner_weight, inner_bias=inner_bias, filter_weight=filter_weight, decay_rates=decay_rates,
        filter_bias=filter_bias, output_weight=output_weight, output_bias=output_bias, second_gain=second_gain,
        second_shift=second_shift, up_weight=up_weight, up_bias=up_bias, down_weight=down_weight, down_bias=down_bias,
        cotangent=cotangent.reshape(rows * local, width),
    )
    o = finish(z, block(z, inputs))
    return (
        o.output.reshape(tokens.shape), o.grad_tokens.reshape(tokens.shape), o.grad_first_gain, o.grad_first_shift, o.grad_input_weight,
        o.grad_input_bias, o.grad_short_kernel, o.grad_short_bias, o.grad_embed_weight, o.grad_embed_bias, o.grad_inner_weight,
        o.grad_inner_bias, o.grad_filter_weight, o.grad_decay_rates, o.grad_filter_bias, o.grad_output_weight, o.grad_output_bias,
        o.grad_second_gain, o.grad_second_shift, o.grad_up_weight, o.grad_up_bias, o.grad_down_weight, o.grad_down_bias,
    )


def solution(mesh):
    split, whole = P(None, "seq", None), P()
    return jax.shard_map(
        functools.partial(shards, mesh.shape["seq"]),
        mesh=mesh,
        in_specs=(split,) + (whole,) * 22 + (split,),
        out_specs=(split, split) + (whole,) * 21,
        check_vma=False,
    )
```

```python
import functools
import math

import jax
import jax.numpy as jnp
from jax import lax
from jax.experimental import pallas as pl
from jax.experimental.pallas import tpu as pltpu
from jax.sharding import PartitionSpec as P

MESH = pl.DeviceIdType.MESH
EPSILON = 1e-05


def bit_of(me, bit):
    return lax.rem(lax.div(me, bit), 2)

def partner_of(me, bit):
    return me + bit - 2 * bit * bit_of(me, bit)

def halving_plan(rows, columns, order, row_unit, column_unit=128):
    steps = []
    for bit in order:
        if rows % (2 * row_unit) == 0:
            rows //= 2
            steps.append((bit, "row", rows, columns))
        elif columns % (2 * column_unit) == 0:
            columns //= 2
            steps.append((bit, "column", rows, columns))
        else:
            steps.append((bit, "full", rows, columns))
    return steps

class Reduction:
    def __init__(self, array, plan, inbox, sends, arrivals, free, me):
        self.array, self.plan, self.inbox = array, plan, inbox
        self.sends, self.arrivals, self.free, self.me = sends, arrivals, free, me
        self.row, self.column = 0, 0
        self.origin = []
        for bit, kind, rows, columns in plan:
            mine = bit_of(me, bit)
            keep, give = (self.row, self.column), (self.row, self.column)
            if kind == "row":
                keep = (self.row + mine * rows, self.column)
                give = (self.row + (1 - mine) * rows, self.column)
            elif kind == "column":
                keep = (self.row, self.column + mine * columns)
                give = (self.row, self.column + (1 - mine) * columns)
            self.origin.append((keep, give))
            self.row, self.column = keep
        self.unit_rows = plan[-1][2]
        self.unit_columns = plan[-1][3]
        self.unit_columns = min(p[3] for p in plan)
        self.unit_rows = min(p[2] for p in plan)

    def window(self, ref, origin, rows, columns):
        row, column = origin
        if not isinstance(row, int):
            row = pl.multiple_of(row, self.unit_rows)
        if not isinstance(column, int):
            column = pl.multiple_of(column, self.unit_columns)
        return ref.at[pl.ds(row, rows), pl.ds(column, columns)]

    def give_copy(self, s):
        bit, kind, rows, columns = self.plan[s]
        return pltpu.make_async_remote_copy(
            src_ref=self.window(self.array, self.origin[s][1], rows, columns),
            dst_ref=self.inbox[s],
            send_sem=self.sends.at[s], recv_sem=self.arrivals.at[s],
            device_id=(partner_of(self.me, bit),), device_id_type=MESH)

    def share_copy(self, s):
        bit, kind, rows, columns = self.plan[s]
        here = self.window(self.array, self.origin[s][0], rows, columns)
        n = len(self.plan)
        return pltpu.make_async_remote_copy(
            src_ref=here, dst_ref=here,
            send_sem=self.sends.at[n + s], recv_sem=self.arrivals.at[n + s],
            device_id=(partner_of(self.me, bit),), device_id_type=MESH)

    def give(self, s):
        self.give_copy(s).start()

    def take(self, s):
        self.give_copy(s).wait()
        bit, kind, rows, columns = self.plan[s]
        if kind != "full":
            pl.semaphore_signal(
                self.free.at[s], inc=1, device_id=(partner_of(self.me, bit),), device_id_type=MESH
            )
        row, column = self.origin[s][0]
        if not isinstance(column, int):
            column = pl.multiple_of(column, self.unit_columns)
        chunk = self.unit_rows
        while chunk * 2 <= 96 and rows % (chunk * 2) == 0:
            chunk *= 2
        inbox = self.inbox[s]
        array = self.array
        def body(i, carry):
            at = pl.multiple_of(i * chunk, chunk)
            here = (pl.ds(pl.multiple_of(row + at, self.unit_rows), chunk), pl.ds(column, columns))
            array[here] = array[here] + inbox[pl.ds(at, chunk), :]
            return carry
        lax.fori_loop(0, rows // chunk, body, 0)

    def share(self, s):
        if self.plan[s][1] != "full":
            pl.semaphore_wait(self.free.at[s], 1)
            self.share_copy(s).start()

    def collect(self, s):
        if self.plan[s][1] != "full":
            self.share_copy(s).wait()


HIGHEST = lax.Precision.HIGHEST
LANES = 128
PANEL = 2048

def ceil8(v):
    return -(-v // 8) * 8

def sin_cos(x):
    turns = jnp.round(x * (2.0 / math.pi))
    r = ((x - turns * 1.5703125) - turns * 4.837512969970703125e-4) - turns * 7.54978995489188e-8
    quadrant = turns.astype(jnp.int32)
    z = r * r
    s = ((-1.9515295891e-4 * z + 8.3321608736e-3) * z - 1.6666654611e-1) * z * r + r
    c = ((2.443315711809948e-5 * z - 1.388731625493765e-3) * z + 4.166664568298827e-2) * z * z - 0.5 * z + 1.0
    swap = (quadrant & 1) == 1
    sin_part = jnp.where(swap, c, s)
    cos_part = jnp.where(swap, s, c)
    sin_out = jnp.where((quadrant & 2) == 2, -sin_part, sin_part)
    cos_out = jnp.where(((quadrant + 1) & 2) == 2, -cos_part, cos_part)
    return sin_out, cos_out

def dot(a, b, ca, cb, precision=None):
    return lax.dot_general(a, b, (((ca,), (cb,)), ((), ())), precision=precision, preferred_element_type=jnp.float32)

class Sizes:
    def __init__(self, n, rows, local, width, emb, filt, hidden=3072):
        self.hidden, self.block = hidden, hidden // 8
        self.n, self.rows, self.local, self.width, self.emb, self.filt = n, rows, local, width, emb, filt
        self.length = n * local
        self.cpd = width // n
        self.cpad = ceil8(self.cpd)
        self.nb = self.length // LANES
        self.tokens = rows * local
        self.tiles = self.tokens // LANES
        self.erows = ceil8(emb)
        self.panel = min(PANEL, self.length)
        self.panels = self.length // self.panel
        assert local * 2 == LANES and rows == 4

def own_selection(z, me):
    want = lax.broadcasted_iota(jnp.int32, (z.cpad, z.width), 0)
    have = lax.broadcasted_iota(jnp.int32, (z.cpad, z.width), 1)
    return jnp.where((have == want + me * z.cpd) & (want < z.cpd), 1.0, 0.0).astype(jnp.float32)

def embed_rows(z, at, count):
    row = lax.broadcasted_iota(jnp.int32, (z.erows, count), 0)
    t = at + lax.broadcasted_iota(jnp.int32, (z.erows, count), 1)
    bands = (z.emb - 1) // 2
    harmonic = jnp.where(row <= bands, row, row - bands)
    angle = lax.rem(t * harmonic, z.length).astype(jnp.float32) * (2.0 * math.pi / z.length)
    s, c = sin_cos(angle)
    scaled = t.astype(jnp.float32) / z.length
    return jnp.where(row == 0, scaled, jnp.where(row <= bands, c, jnp.where(row < z.emb, s, 0.0)))

def columns(ref, count):
    eye = (lax.broadcasted_iota(jnp.int32, (count, count), 0) == lax.broadcasted_iota(jnp.int32, (count, count), 1)).astype(jnp.float32)
    return dot(eye, jnp.broadcast_to(ref[...], (8, count)), 1, 1, HIGHEST)[:, 0:1]

CHUNK = 512

def filter_setup(z, me, w, keep):
    select = own_selection(z, me)
    keep.own_filter[...] = dot(select, w.filter_weight[...], 1, 1, HIGHEST)
    own_decay = dot(select, jnp.broadcast_to(w.decay_rates[...], (8, z.width)), 1, 1, HIGHEST)[:, 0:1]
    keep.own_decay[...] = jnp.broadcast_to(own_decay, (z.cpad, LANES))
    keep.embed_pad[...] = jnp.zeros((z.erows, z.filt), jnp.float32)
    keep.embed_pad[0:z.emb, :] = w.embed_weight[...]
    keep.bias_one[...] = jnp.broadcast_to(columns(w.embed_bias, z.filt), (z.filt, LANES))
    keep.bias_two[...] = jnp.broadcast_to(columns(w.inner_bias, z.filt), (z.filt, LANES))


def filter_hidden(z, w, keep, at):
    embedded = embed_rows(z, at, CHUNK)
    s1, c1 = sin_cos(dot(keep.embed_pad[...], embedded, 0, 0, HIGHEST) + keep.bias_one[:, 0:1])
    s2, c2 = sin_cos(dot(w.inner_weight[...], s1, 0, 0, HIGHEST) + keep.bias_two[:, 0:1])
    scaled = (at + lax.broadcasted_iota(jnp.int32, (z.cpad, CHUNK), 1)).astype(jnp.float32) / z.length
    window = jnp.exp(-keep.own_decay[:, 0:1] * scaled)
    return embedded, s1, c1, s2, c2, scaled, window


def filter_forward(z, w, keep, begin, end):
    def body(i, carry):
        at = pl.multiple_of(i * CHUNK, CHUNK)
        embedded, s1, c1, s2, c2, scaled, window = filter_hidden(z, w, keep, at)
        keep.taps[:, pl.ds(at, CHUNK)] = dot(keep.own_filter[...], s2, 1, 0, HIGHEST) * window
        return carry
    lax.fori_loop(begin, end, body, 0)

def filter_backward(z, w, keep, grad_taps, sums):
    for ref in vars(sums).values():
        ref[...] = jnp.zeros(ref.shape, jnp.float32)
    def body(i, carry):
        at = pl.multiple_of(i * CHUNK, CHUNK)
        here = (slice(None), pl.ds(at, CHUNK))
        embedded, s1, c1, s2, c2, scaled, window = filter_hidden(z, w, keep, at)
        grad = grad_taps[here]
        decay = -jnp.sum(grad * keep.taps[here] * scaled, axis=1, keepdims=True)
        sums.decay[...] += jnp.broadcast_to(decay, (z.cpad, LANES))
        grad_raw = grad * window
        sums.filter[...] += dot(grad_raw, s2, 1, 1, HIGHEST)
        two = dot(keep.own_filter[...], grad_raw, 0, 0, HIGHEST) * c2
        sums.inner[...] += dot(s1, two, 1, 1, HIGHEST)
        sums.inner_bias[...] += jnp.broadcast_to(jnp.sum(two, axis=1, keepdims=True), (z.filt, LANES))
        one = dot(w.inner_weight[...], two, 1, 0, HIGHEST) * c1
        sums.embed[...] += dot(embedded, one, 1, 1, HIGHEST)
        sums.embed_bias[...] += jnp.broadcast_to(jnp.sum(one, axis=1, keepdims=True), (z.filt, LANES))
        return carry
    lax.fori_loop(0, z.length // CHUNK, body, 0)

def build_toeplitz(z, taps, pool):
    sub = lax.broadcasted_iota(jnp.int32, (8, z.length), 0)
    lane = lax.broadcasted_iota(jnp.int32, (8, LANES), 1)
    sub1 = lax.broadcasted_iota(jnp.int32, (8, LANES), 0)
    def body(c, carry):
        base = jnp.broadcast_to(taps[pl.ds(c, 1), :], (8, z.length))
        for bit in (1, 2, 4):
            base = jnp.where((sub & bit) == bit, pltpu.roll(base, bit, 1), base)
        for q in range(0, LANES // 8, 2):
            parts = []
            for u in (q, q + 1):
                part = pltpu.roll(base, 8 * u, 1) if u else base
                first = jnp.where(lane >= sub1 + 8 * u, part[:, :LANES], 0.0)
                parts.append(jnp.concatenate([first, part[:, LANES:]], axis=1))
            pair = jnp.concatenate(parts, axis=0).astype(jnp.bfloat16)
            for k in range(z.panels):
                at = pl.multiple_of((c * z.panels + k) * LANES, LANES) + 8 * q
                pool[pl.ds(pl.multiple_of(at, 16), 16), :] = pair[:, k * z.panel:(k + 1) * z.panel]
        return carry
    lax.fori_loop(0, z.cpd, body, 0)

def fold_panel(z, k, product, fold):
    lane = lax.broadcasted_iota(jnp.int32, (8, LANES), 1)
    row = lax.broadcasted_iota(jnp.int32, (8, LANES), 0)
    sums, before = None, None
    for u in range(LANES // 8):
        part = product[8 * u:8 * u + 8, :]
        first = part[:, :LANES]
        inside = lane >= row + 8 * u
        part = jnp.concatenate([jnp.where(inside, first, 0.0), part[:, LANES:]], axis=1)
        part = pltpu.roll(part, z.panel - 8 * u, 1) if u else part
        sums = part if sums is None else sums + part
        if k:
            outside = jnp.where(inside, 0.0, first)
            outside = pltpu.roll(outside, LANES - 8 * u, 1) if u else outside
            before = outside if before is None else before + outside
    fold[:, k * z.panel:(k + 1) * z.panel] = sums
    if k:
        fold[:, k * z.panel - LANES:k * z.panel] += before


def fold_rows(z, fold):
    sums = fold[...]
    row = lax.broadcasted_iota(jnp.int32, sums.shape, 0)
    for bit in (1, 2, 4):
        sums = jnp.where((row & bit) == bit, pltpu.roll(sums, z.length - bit, 1), sums)
    return jnp.sum(sums, axis=0, keepdims=True)

class Exchange:
    def __init__(self, outgoing, incoming, sends, arrivals, me, n):
        self.outgoing, self.incoming, self.sends, self.arrivals, self.me, self.n = outgoing, incoming, sends, arrivals, me, n
    def copy(self, k):
        to = lax.rem(self.me + k, self.n)
        return pltpu.make_async_remote_copy(
            src_ref=self.outgoing.at[to], dst_ref=self.incoming.at[self.me],
            send_sem=self.sends.at[k], recv_sem=self.arrivals.at[k],
            device_id=(to,), device_id_type=MESH)
    def start(self):
        def body(k, carry):
            self.copy(k).start()
            return carry
        lax.fori_loop(1, self.n, body, 0)
        self.incoming[self.me] = self.outgoing[self.me]
    def wait(self):
        def body(k, carry):
            self.copy(k).wait()
            return carry
        lax.fori_loop(1, self.n, body, 0)

def each_slab(z, body):
    if z.cpd % 8 == 0:
        lax.fori_loop(0, z.n, body, 0)
    else:
        for k in range(z.n):
            body(k, 0)

def slabs_from_rows(z, flipped, outgoing):
    def body(k, carry):
        at = k * z.cpd
        if z.cpd % 8 == 0:
            at = pl.multiple_of(at, 8)
        slab = flipped[pl.ds(at, z.cpad), :]
        outgoing[k] = jnp.concatenate([slab[:, :LANES], slab[:, LANES:]], axis=0).astype(outgoing.dtype)
        return carry
    each_slab(z, body)

def rows_from_slabs(z, incoming, flipped):
    def body(k, carry):
        at = k * z.cpd
        if z.cpd % 8 == 0:
            at = pl.multiple_of(at, 8)
        slab = incoming[k].astype(jnp.float32)
        flipped[pl.ds(at, z.cpad), :] = jnp.concatenate([slab[:z.cpad], slab[z.cpad:]], axis=1)
        return carry
    each_slab(z, body)

def widen_slabs(z, incoming, wide):
    def body(j, carry):
        wide[pl.ds(pl.multiple_of(j * 2 * z.cpad, 8), 2 * z.cpad), :] = incoming[j].astype(jnp.float32)
        return carry
    lax.fori_loop(0, z.n, body, 0)

def narrow_slabs(z, wide, outgoing):
    def body(j, carry):
        outgoing[j] = wide[pl.ds(pl.multiple_of(j * 2 * z.cpad, 8), 2 * z.cpad), :].astype(outgoing.dtype)
        return carry
    lax.fori_loop(0, z.n, body, 0)

def channel_blocks(z, wide, c):
    lane = lax.broadcasted_iota(jnp.int32, (z.nb, LANES), 1)
    low = lane < LANES // 2
    out = []
    for t in range(2):
        even = wide[pl.ds(t * z.cpad + c, z.nb, 4 * z.cpad), :]
        odd = wide[pl.ds((2 + t) * z.cpad + c, z.nb, 4 * z.cpad), :]
        out.append(jnp.where(low, even, pltpu.roll(odd, LANES // 2, 1)))
        out.append(jnp.where(low, pltpu.roll(even, LANES // 2, 1), odd))
    return out

def put_channel_blocks(z, wide, c, blocks):
    lane = lax.broadcasted_iota(jnp.int32, (z.nb, LANES), 1)
    low = lane < LANES // 2
    for t in range(2):
        a, b = blocks[2 * t], blocks[2 * t + 1]
        wide[pl.ds(t * z.cpad + c, z.nb, 4 * z.cpad), :] = jnp.where(low, a, pltpu.roll(b, LANES // 2, 1))
        wide[pl.ds((2 + t) * z.cpad + c, z.nb, 4 * z.cpad), :] = jnp.where(low, pltpu.roll(a, LANES // 2, 1), b)

def panel_rows(z, c, k):
    return pl.ds(pl.multiple_of((c * z.panels + k) * LANES, LANES), LANES)


def convolve_forward(z, wide, pool, kept, spread):
    each = z.panel // LANES
    def body(c, carry):
        blocks = channel_blocks(z, wide, c)
        x = jnp.concatenate(blocks, axis=0).astype(jnp.bfloat16)
        kept[c] = x
        spread[...] = jnp.zeros(spread.shape, jnp.float32)
        for k in range(z.panels):
            product = dot(x, pool[panel_rows(z, c, k), :], 1, 0)
            for i in range(each):
                d = k * each + i
                for r in range(4):
                    spread[r, d:d + z.nb, :] += product[r * z.nb:(r + 1) * z.nb, i * LANES:(i + 1) * LANES]
        put_channel_blocks(z, wide, c, [spread[r, 0:z.nb, :] for r in range(4)])
        return carry
    lax.fori_loop(0, z.cpd, body, 0)


def convolve_back_channel(z, c, wide, panel_of, kept, spread, advanced, back, fold, grad_taps):
    blocks = channel_blocks(z, wide, c)
    for r in range(4):
        spread[r, 0:z.nb, :] = blocks[r]
    each = z.panel // LANES
    source = kept[c].astype(jnp.float32).T.astype(jnp.bfloat16)
    for k in range(z.panels):
        for i in range(each):
            d = k * each + i
            advanced[:, i * LANES:(i + 1) * LANES] = jnp.concatenate(
                [spread[r, d:d + z.nb, :] for r in range(4)], axis=0).astype(jnp.bfloat16)
        panel = panel_of(c, k)
        product = dot(advanced[...], panel[...], 1, 1)
        back[...] = product if k == 0 else back[...] + product
        fold_panel(z, k, dot(source, advanced[...], 1, 0), fold)
    put_channel_blocks(z, wide, c, [back[r * z.nb:(r + 1) * z.nb, :] for r in range(4)])
    grad_taps[pl.ds(c, 1), :] = fold_rows(z, fold)


class Names:
    def __init__(self, names, values):
        vars(self).update(zip(names, values))


def keep_shapes(z):
    return dict(
        own_filter=(z.cpad, z.filt), own_decay=(z.cpad, LANES), embed_pad=(z.erows, z.filt),
        bias_one=(z.filt, LANES), bias_two=(z.filt, LANES), taps=(z.cpad, z.length),
    )


def sum_shapes(z):
    return dict(
        decay=(z.cpad, LANES), filter=(z.cpad, z.filt), inner=(z.filt, z.filt), inner_bias=(z.filt, LANES),
        embed=(z.erows, z.filt), embed_bias=(z.filt, LANES),
    )


F32, BF16 = jnp.float32, jnp.bfloat16
BLOCKS = 8
WIDE = 256


class Row:
    FIRST_GAIN, FIRST_SHIFT, INPUT_BIAS, SHORT_KERNEL, SHORT_BIAS = 0, 1, 2, 5, 14
    DECAY, FILTER_BIAS, OUTPUT_BIAS, SECOND_GAIN, SECOND_SHIFT, UP_BIAS, DOWN_BIAS = 17, 18, 19, 20, 21, 22, 26
    EMBED_BIAS, INNER_BIAS = 27, 28
    FILTER, NETWORK, TOTAL = 32, 96, 128


def normalize(x):
    center = x - jnp.mean(x, axis=-1, keepdims=True)
    inverse = lax.rsqrt(jnp.mean(center * center, axis=-1, keepdims=True) + EPSILON)
    return center * inverse, inverse


def normalize_back(gradient, gain, unit, inverse):
    q = gradient * gain
    return (q - jnp.mean(q, axis=-1, keepdims=True) - unit * jnp.mean(q * unit, axis=-1, keepdims=True)) * inverse


def as_row(column):
    size = column.shape[0]
    row, lane = (lax.broadcasted_iota(jnp.int32, (size, size), i) for i in range(2))
    return dot(column, jnp.where(row == lane, 1.0, 0.0).astype(F32), 0, 0, HIGHEST)[0:1, :]


def total(x):
    return jnp.sum(x, axis=0, keepdims=True)


def row_masks(z, me, lengths, keep_one, keep_two):
    for r in range(z.rows):
        position = me * z.local + lax.broadcasted_iota(jnp.int32, (z.local, LANES), 0)
        first = position == 0
        second = position == 1
        end = 0
        for j in range(lengths.shape[1] - 1):
            end = end + lengths[r, j]
            first = first | (position == end)
            second = second | (position == end + 1)
        keep_one[r * z.local:(r + 1) * z.local, :] = jnp.where(first, 0.0, 1.0)
        keep_two[r * z.local:(r + 1) * z.local, :] = jnp.where(first | second, 0.0, 1.0)


def lagged(z, values, halo, t, columns):
    row = lax.broadcasted_iota(jnp.int32, (LANES, 1), 0)
    one, two = pltpu.roll(values, 1, 0), pltpu.roll(values, 2, 0)
    for u in range(2):
        r = 2 * t + u
        older, newer = halo[2 * r:2 * r + 1, columns], halo[2 * r + 1:2 * r + 2, columns]
        one = jnp.where(row == u * z.local, newer, one)
        two = jnp.where(row == u * z.local, older, jnp.where(row == u * z.local + 1, newer, two))
    return one, two


def halves(t):
    return slice(t * LANES, (t + 1) * LANES)


class Flow:
    def __init__(self, reduction):
        self.reduction = reduction
        self.steps = len(reduction.plan)
        self.at = -1
    def advance(self):
        s, n, r = self.at, self.steps, self.reduction
        if s < 0:
            r.give(0)
        elif s < n - 1:
            r.take(s)
            r.give(s + 1)
        elif s == n - 1:
            r.take(s)
            r.share(s)
        elif s < 2 * n - 1:
            r.collect(2 * n - 1 - s)
            r.share(2 * n - 2 - s)
        elif s == 2 * n - 1:
            r.collect(0)
        self.at += 1
    @property
    def done(self):
        return self.at >= 2 * self.steps


def block_kernel(z, order, *refs):
    inputs, outs, scratch, fetched, keep_names, sum_names = order
    v = Names(inputs + outs + scratch, refs)
    me = lax.axis_index("seq")
    n = z.n
    d = z.width
    p = Names(fetched, [getattr(v, "v_" + name) for name in fetched])
    def fetch(name):
        source, target = getattr(v, name), getattr(p, name)
        if len(source.shape) == 1:
            target = target.at[0]
        return pltpu.make_async_copy(source, target, v.loads.at[fetched.index(name)])
    late = ("input_weight", "output_weight", "cotangent")
    soon = [name for name in fetched if name not in late]
    for name in soon + list(late):
        fetch(name).start()
    def weight_block(j, slot):
        at = pl.multiple_of(j * z.block, LANES)
        return (
            pltpu.make_async_copy(v.up_weight.at[:, pl.ds(at, z.block)], v.up_slots.at[slot], v.stream.at[0, slot]),
            pltpu.make_async_copy(v.down_weight.at[pl.ds(at, z.block), :], v.down_slots.at[slot], v.stream.at[1, slot]),
        )
    for copy in weight_block(0, 0):
        copy.start()
    barrier = pltpu.get_barrier_semaphore()
    def greet(k, carry):
        pl.semaphore_signal(barrier, inc=1, device_id=(lax.rem(me + k, n),), device_id_type=MESH)
        return carry
    lax.fori_loop(1, n, greet, 0)
    small = v.r_small
    small[0:Row.FILTER, :] = jnp.zeros((Row.FILTER, d), F32)
    small[Row.NETWORK:Row.TOTAL, :] = jnp.zeros((Row.TOTAL - Row.NETWORK, d), F32)
    row_masks(z, me, v.doc_lengths, v.keep_one, v.keep_two)

    for name in soon:
        fetch(name).wait()
    tokens = p.tokens
    for t in range(z.tiles):
        unit, inverse = normalize(tokens[halves(t), :].astype(F32))
        v.unit_one[halves(t), :] = unit
        v.inverse_one[halves(t), :] = jnp.broadcast_to(inverse, (LANES, LANES))
        v.normed[halves(t), :] = (unit * p.first_gain[...] + p.first_shift[...]).astype(BF16)
    fetch("input_weight").wait()
    part = 3 * d // 6
    def project(j, carry):
        here = pl.ds(pl.multiple_of(j * part, LANES), part)
        values = (dot(v.normed[...], p.input_weight[:, here], 1, 0) + p.input_bias[:, here]).astype(BF16)
        v.projected[:, here] = values
        rounded = values.astype(F32)
        for r in range(z.rows):
            last = (r + 1) * z.local
            v.rim_out[2 * r:2 * r + 2, here] = rounded[last - 2:last, :]
        return carry
    lax.fori_loop(0, 6, project, 0)
    pl.semaphore_wait(barrier, n - 1)
    ahead, behind = lax.rem(me + 1, n), lax.rem(me + n - 1, n)
    rim = pltpu.make_async_remote_copy(
        src_ref=v.rim_out, dst_ref=v.rim_in, send_sem=v.rims.at[0], recv_sem=v.rims.at[1],
        device_id=(ahead,), device_id_type=MESH)
    rim.start()
    keep = Names(keep_names, [getattr(v, "k_" + name) for name in keep_names])
    chunks = z.length // CHUNK
    early = chunks // 2
    filter_setup(z, me, p, keep)
    filter_forward(z, p, keep, 0, early)
    rim.wait()

    def short(j, carry):
        inner = pl.ds(pl.multiple_of(j * WIDE, LANES), WIDE)
        for t in range(z.tiles):
            k1, k2 = v.keep_one[halves(t), 0:1], v.keep_two[halves(t), 0:1]
            streams = []
            for s in range(3):
                here = pl.ds(pl.multiple_of(s * d + j * WIDE, LANES), WIDE)
                values = v.projected[halves(t), here].astype(F32)
                one, two = lagged(z, values, v.rim_in, t, here)
                taps = p.short_kernel
                out = (taps[0:1, here] * values + taps[1:2, here] * (k1 * one) + taps[2:3, here] * (k2 * two)
                       + p.short_bias[:, here])
                (v.gate_zero, v.gate_one, v.value_part)[s][halves(t), inner] = out
                streams.append(out)
            v.flipped[inner, halves(t)] = (streams[1] * streams[2]).T
        return carry
    lax.fori_loop(0, d // WIDE, short, 0)
    v.flipped[d:, :] = jnp.zeros((8, z.tokens), F32)

    def exchange(i):
        return Exchange(v.slabs_out.at[i % 2], v.slabs_in.at[i % 2], v.sends.at[i], v.arrivals.at[i], me, n)
    slabs_from_rows(z, v.flipped, v.slabs_out.at[0])
    first = exchange(0)
    first.start()
    filter_forward(z, p, keep, early, chunks)
    build_toeplitz(z, keep.taps, v.pool)
    first.wait()
    widen_slabs(z, v.slabs_in.at[0], v.wide)
    save = pltpu.make_async_copy(v.pool, v.toeplitz_saved, v.saves.at[0])
    save.start()
    convolve_forward(z, v.wide, v.pool, v.kept, v.spread)
    save.wait()
    narrow_slabs(z, v.wide, v.slabs_out.at[1])
    second = exchange(1)
    second.start()
    fetch("output_weight").wait()
    fetch("cotangent").wait()
    cotangent = p.cotangent
    small[Row.DOWN_BIAS:Row.DOWN_BIAS + 1, :] = total(cotangent[...].astype(F32))
    second.wait()
    rows_from_slabs(z, v.slabs_in.at[1], v.flipped)

    def gate(j, carry):
        inner = pl.ds(pl.multiple_of(j * WIDE, LANES), WIDE)
        for t in range(z.tiles):
            gated = v.value_part[halves(t), inner] * v.gate_one[halves(t), inner]
            conv = v.flipped[inner, halves(t)].T + p.filter_bias[:, inner] * gated
            v.conv[halves(t), inner] = conv
            v.mixed[halves(t), inner] = (conv * v.gate_zero[halves(t), inner]).astype(BF16)
        return carry
    lax.fori_loop(0, d // WIDE, gate, 0)
    for t in range(z.tiles):
        branch = dot(v.mixed[halves(t), :], p.output_weight[...], 1, 0) + p.output_bias[...]
        residual = tokens[halves(t), :].astype(F32) + branch
        unit, inverse = normalize(residual)
        v.unit_two[halves(t), :] = unit
        v.inverse_two[halves(t), :] = jnp.broadcast_to(inverse, (LANES, LANES))
        v.normed_two[halves(t), :] = (unit * p.second_gain[...] + p.second_shift[...]).astype(BF16)
        v.residual[halves(t), :] = residual + p.down_bias[...]
    v.grad_normed[...] = jnp.zeros((z.tokens, d), F32)

    arrays = [v.r_down.at[i] for i in range(4)] + [v.r_up.at[i] for i in range(4)] + [v.r_out] + [v.r_inner.at[i] for i in range(3)] + [v.r_small]
    flows = []
    for i, (array, plan) in enumerate(zip(arrays, z.plans)):
        reduction = Reduction(array, plan, part_inboxes(z, v, i), v.part_sends.at[i], v.part_arrivals.at[i], v.part_free.at[i], me)
        flows.append(Flow(reduction))
    def run(parts):
        for i in parts:
            if not flows[i].done:
                flows[i].advance()

    def mlp(j, carry):
        slot = lax.rem(j, 2)
        for copy in weight_block(j, slot):
            copy.wait()
        @pl.when(j + 1 < BLOCKS)
        def _():
            for copy in weight_block(j + 1, 1 - slot):
                copy.start()
        up, down = v.up_slots[slot], v.down_slots[slot]
        here = pl.ds(pl.multiple_of(j * z.block, LANES), z.block)
        x = dot(v.normed_two[...], up, 1, 0) + p.up_bias[:, here]
        grad_hidden = dot(cotangent[...], down, 1, 1)
        root = math.sqrt(2.0 / math.pi)
        square = x * x
        curve = jnp.tanh(root * (x + 0.044715 * (square * x)))
        half = 0.5 * (1.0 + curve)
        hidden = (x * half).astype(BF16)
        slope = half + 0.5 * x * (1.0 - curve * curve) * (root * (1.0 + 3.0 * 0.044715 * square))
        grad_pre = (grad_hidden * slope).astype(BF16)
        v.residual[...] += dot(hidden, down, 1, 0)
        v.grad_normed[...] += dot(grad_pre, up, 1, 1)
        part, half_part = lax.div(j, 2), lax.rem(j, 2)
        there = pl.ds(pl.multiple_of(half_part * z.block, LANES), z.block)
        v.r_down[part, there, :] = dot(hidden, cotangent[...], 0, 0).astype(BF16)
        v.r_up[part, :, there] = dot(v.normed_two[...], grad_pre, 0, 0).astype(BF16)
        v.up_sums[:, here] = total(grad_pre.astype(F32))
        return carry
    for i in range(4):
        lax.fori_loop(2 * i, 2 * i + 2, mlp, 0)
        if i:
            run(Schedule.MLP[i - 1])
        run((i, 4 + i))
    wide_rows = v.up_sums.shape[1] // d
    for i in range(wide_rows):
        small[Row.UP_BIAS + i:Row.UP_BIAS + i + 1, :] = v.up_sums[:, i * d:(i + 1) * d]
    v.output[...] = v.residual[...].astype(BF16)

    gain_sum, shift_sum, bias_sum = 0.0, 0.0, 0.0
    for t in range(z.tiles):
        gradient = v.grad_normed[halves(t), :]
        unit = v.unit_two[halves(t), :]
        gain_sum = gain_sum + total(gradient * unit)
        shift_sum = shift_sum + total(gradient)
        value = cotangent[halves(t), :].astype(F32) + normalize_back(gradient, p.second_gain[...], unit, v.inverse_two[halves(t), 0:1])
        v.residual[halves(t), :] = value
        branch = value.astype(BF16)
        v.grad_branch[halves(t), :] = branch
        bias_sum = bias_sum + total(branch.astype(F32))
    small[Row.SECOND_GAIN:Row.SECOND_GAIN + 1, :] = gain_sum
    small[Row.SECOND_SHIFT:Row.SECOND_SHIFT + 1, :] = shift_sum
    small[Row.OUTPUT_BIAS:Row.OUTPUT_BIAS + 1, :] = bias_sum
    grad_conv, grad_gate_zero = v.unit_two, v.grad_normed
    def mix_back(j, carry):
        inner = pl.ds(pl.multiple_of(j * WIDE, LANES), WIDE)
        sums = jnp.zeros((1, WIDE), F32)
        for t in range(z.tiles):
            grad_mixed = dot(v.grad_branch[halves(t), :], p.output_weight[inner, :], 1, 1)
            back = grad_mixed * v.gate_zero[halves(t), inner]
            grad_conv[halves(t), inner] = back
            grad_gate_zero[halves(t), inner] = grad_mixed * v.conv[halves(t), inner]
            gated = v.value_part[halves(t), inner] * v.gate_one[halves(t), inner]
            sums = sums + total(back * gated)
            v.flipped[inner, halves(t)] = back.T
        small[Row.FILTER_BIAS:Row.FILTER_BIAS + 1, inner] = sums
        return carry
    lax.fori_loop(0, d // WIDE, mix_back, 0)
    slabs_from_rows(z, v.flipped, v.slabs_out.at[0])
    third = exchange(2)
    third.start()
    run(Schedule.THREE)
    def load_panel(i):
        saved = v.toeplitz_saved.at[pl.ds(pl.multiple_of(i * LANES, LANES), LANES), :]
        slot = lax.rem(i, 2)
        return pltpu.make_async_copy(saved, v.toeplitz_slots.at[slot], v.stream.at[2, slot])
    load_panel(0).start()
    def panel_of(c, k):
        i = c * z.panels + k
        load_panel(i).wait()
        @pl.when(i + 1 < z.cpd * z.panels)
        def _():
            load_panel(i + 1).start()
        return v.toeplitz_slots.at[lax.rem(i, 2)]
    def out_grad(j, carry):
        inner = pl.ds(pl.multiple_of(j * WIDE, LANES), WIDE)
        v.r_out[:, inner] = dot(v.mixed[...], v.grad_branch[:, inner], 0, 0).astype(BF16)
        return carry
    lax.fori_loop(0, d // WIDE, out_grad, 0)
    run((8,))
    run(Schedule.WAIT_THREE)
    third.wait()
    widen_slabs(z, v.slabs_in.at[0], v.wide)
    v.spread[...] = jnp.zeros(v.spread.shape, F32)
    v.grad_taps[...] = jnp.zeros(v.grad_taps.shape, F32)
    pieces = len(Schedule.PIECES)
    bounds = [z.cpd * i // pieces for i in range(pieces + 1)]
    def back_channel(c, carry):
        convolve_back_channel(z, c, v.wide, panel_of, v.kept, v.spread, v.advanced, v.back, v.fold, v.grad_taps)
        return carry
    for i in range(pieces):
        lax.fori_loop(bounds[i], bounds[i + 1], back_channel, 0)
        run(Schedule.PIECES[i])
    narrow_slabs(z, v.wide, v.slabs_out.at[1])
    fourth = exchange(3)
    fourth.start()
    run(Schedule.SENT)
    sums = Names(sum_names, [getattr(v, "s_" + name) for name in sum_names])
    filter_backward(z, p, keep, v.grad_taps, sums)
    select = own_selection(z, me)
    small[Row.FILTER:Row.NETWORK, :] = dot(sums.filter[...], select, 0, 0, HIGHEST)
    small[Row.DECAY:Row.DECAY + 1, :] = dot(sums.decay[...], select, 0, 0, HIGHEST)[0:1, :]
    half = z.filt // 2
    small[Row.NETWORK:Row.NETWORK + half, 0:z.filt] = sums.inner[0:half, :]
    small[Row.NETWORK:Row.NETWORK + half, LANES:LANES + z.filt] = sums.inner[half:, :]
    small[Row.NETWORK:Row.NETWORK + half, 2 * LANES:2 * LANES + z.filt] = sums.embed[0:half, :]
    small[Row.NETWORK:Row.NETWORK + z.erows - half, 3 * LANES:3 * LANES + z.filt] = sums.embed[half:, :]
    small[Row.EMBED_BIAS:Row.EMBED_BIAS + 1, 0:z.filt] = as_row(sums.embed_bias[...])
    small[Row.INNER_BIAS:Row.INNER_BIAS + 1, 0:z.filt] = as_row(sums.inner_bias[...])
    run(Schedule.FILTER)
    run(Schedule.WAIT_FOUR)
    fourth.wait()
    rows_from_slabs(z, v.slabs_in.at[1], v.flipped)

    def gate_back(j, carry):
        inner = pl.ds(pl.multiple_of(j * WIDE, LANES), WIDE)
        for t in range(z.tiles):
            grad_gated = v.flipped[inner, halves(t)].T + p.filter_bias[:, inner] * grad_conv[halves(t), inner]
            first_part = grad_gated * v.value_part[halves(t), inner]
            second_part = grad_gated * v.gate_one[halves(t), inner]
            v.gate_one[halves(t), inner] = first_part
            v.value_part[halves(t), inner] = second_part
            for s, value in enumerate((grad_gate_zero[halves(t), inner], first_part, second_part)):
                here = pl.ds(pl.multiple_of(s * d + j * WIDE, LANES), WIDE)
                taps = p.short_kernel
                for u in range(2):
                    r = 2 * t + u
                    lo = u * z.local
                    head = value[lo:lo + 8, :]
                    one = (taps[1:2, here] * v.keep_one[r * z.local:r * z.local + 8, 0:1]) * head
                    two = (taps[2:3, here] * v.keep_two[r * z.local:r * z.local + 8, 0:1]) * head
                    v.rim_back_out[2 * r:2 * r + 1, here] = two[0:1]
                    v.rim_back_out[2 * r + 1:2 * r + 2, here] = one[0:1] + two[1:2]
        return carry
    lax.fori_loop(0, d // WIDE, gate_back, 0)
    rim_back = pltpu.make_async_remote_copy(
        src_ref=v.rim_back_out, dst_ref=v.rim_back_in, send_sem=v.rims.at[2], recv_sem=v.rims.at[3],
        device_id=(behind,), device_id_type=MESH)
    rim_back.start()
    run(Schedule.RIM)
    grad_streams = (grad_gate_zero, v.gate_one, v.value_part)
    def short_sums(j, carry):
        inner = pl.ds(pl.multiple_of(j * WIDE, LANES), WIDE)
        for s in range(3):
            here = pl.ds(pl.multiple_of(s * d + j * WIDE, LANES), WIDE)
            acc = [jnp.zeros((1, WIDE), F32)] * 4
            for t in range(z.tiles):
                k1, k2 = v.keep_one[halves(t), 0:1], v.keep_two[halves(t), 0:1]
                values = v.projected[halves(t), here].astype(F32)
                one, two = lagged(z, values, v.rim_in, t, here)
                value = grad_streams[s][halves(t), inner]
                acc[0] = acc[0] + total(value * values)
                acc[1] = acc[1] + total(value * (k1 * one))
                acc[2] = acc[2] + total(value * (k2 * two))
                acc[3] = acc[3] + total(value)
            for i in range(3):
                small[Row.SHORT_KERNEL + 3 * i + s:Row.SHORT_KERNEL + 3 * i + s + 1, inner] = acc[i]
            small[Row.SHORT_BIAS + s:Row.SHORT_BIAS + s + 1, inner] = acc[3]
        return carry
    lax.fori_loop(0, d // WIDE, short_sums, 0)
    run(Schedule.SHORT)
    rim_back.wait()
    def spread_back(j, carry):
        inner = pl.ds(pl.multiple_of(j * WIDE, LANES), WIDE)
        row = lax.broadcasted_iota(jnp.int32, (LANES, 1), 0)
        for s in range(3):
            here = pl.ds(pl.multiple_of(s * d + j * WIDE, LANES), WIDE)
            taps = p.short_kernel
            sums = jnp.zeros((1, WIDE), F32)
            for t in range(z.tiles):
                k1, k2 = v.keep_one[halves(t), 0:1], v.keep_two[halves(t), 0:1]
                value = grad_streams[s][halves(t), inner]
                one = pltpu.roll((taps[1:2, here] * k1) * value, LANES - 1, 0)
                two = pltpu.roll((taps[2:3, here] * k2) * value, LANES - 2, 0)
                later = one + two
                for u in range(2):
                    r = 2 * t + u
                    last = (u + 1) * z.local - 1
                    far, near = v.rim_back_in[2 * r:2 * r + 1, here], v.rim_back_in[2 * r + 1:2 * r + 2, here]
                    later = jnp.where(row == last, near, jnp.where(row == last - 1, one + far, later))
                low = (taps[0:1, here] * value + later).astype(BF16)
                v.projected[halves(t), here] = low
                sums = sums + total(low.astype(F32))
            small[Row.INPUT_BIAS + s:Row.INPUT_BIAS + s + 1, inner] = sums
        return carry
    lax.fori_loop(0, d // WIDE, spread_back, 0)
    run(Schedule.SPREAD)
    for k in range(3):
        v.r_inner[k] = dot(v.normed[...], v.projected[:, k * d:(k + 1) * d], 0, 0).astype(BF16)
        run((9 + k,))
    run(Schedule.NORMAL)
    v.conv[...] = jnp.zeros((z.tokens, d), F32)
    def norm_grad(j, carry):
        here = pl.ds(pl.multiple_of(j * part, LANES), part)
        v.conv[...] += dot(v.projected[:, here], p.input_weight[:, here], 1, 1)
        return carry
    lax.fori_loop(0, 6, norm_grad, 0)
    gain_sum, shift_sum = 0.0, 0.0
    for t in range(z.tiles):
        gradient = v.conv[halves(t), :]
        unit = v.unit_one[halves(t), :]
        gain_sum = gain_sum + total(gradient * unit)
        shift_sum = shift_sum + total(gradient)
        value = v.residual[halves(t), :] + normalize_back(gradient, p.first_gain[...], unit, v.inverse_one[halves(t), 0:1])
        v.grad_tokens[halves(t), :] = value.astype(BF16)
    small[Row.FIRST_GAIN:Row.FIRST_GAIN + 1, :] = gain_sum
    small[Row.FIRST_SHIFT:Row.FIRST_SHIFT + 1, :] = shift_sum
    run((12,))

    run(Schedule.TAIL)
    while not all(flow.done for flow in flows):
        run(range(len(flows)))


class Schedule:
    ORDERS = (
        (0, 1, 2, 3, 4),
        (0, 2, 1, 3, 4),
        (0, 2, 3, 1, 4),
        (0, 2, 1, 3, 4),
        (0, 2, 1, 3, 4),
        (0, 3, 2, 1, 4),
        (0, 1, 2, 3, 4),
        (0, 1, 2, 3, 4),
        (0, 3, 1, 2, 4),
        (0, 2, 1, 3, 4),
        (0, 1, 3, 2, 4),
        (0, 3, 2, 1, 4),
        (0, 2, 1, 3, 4),
    )
    MLP = (
        (0, 4,),
        (),
        (),
    )
    THREE = (1, 5, 2, 6, 0, 4, 3, 7,)
    WAIT_THREE = (8,)
    SENT = (3, 2, 6, 1, 7, 5, 0, 8, 4,)
    FILTER = ()
    WAIT_FOUR = ()
    RIM = (3, 4, 7, 2, 0, 6,)
    SHORT = (1, 5, 2, 8,)
    SPREAD = ()
    NORMAL = (9, 1, 4,)
    TAIL = (
        10, 11, 2, 4, 3, 0, 12, 9, 10, 11, 7, 2, 12, 10, 6, 2, 0, 3, 11, 8, 7, 0, 9, 10,
        1, 12, 5, 6, 11, 3, 9, 8, 12, 10, 11, 7, 1, 9, 12, 10, 1, 6, 11, 9, 12, 5, 10, 3,
        9, 12, 8, 6, 11, 10, 5, 6, 9, 12, 7, 3, 8, 3, 11, 8, 10, 5, 10, 9, 5, 12, 9, 7,
        12, 11, 7, 11,
    )
    PIECES = (
        (1, 6,),
        (5, 4,),
        (2,),
        (8, 0, 4, 7,),
        (2, 1, 0,),
        (3, 4, 8, 2, 1, 6,),
        (0, 4, 5,),
        (),
    )


def part_shapes(z):
    d = z.width
    return dict(down=((4, d, d), BF16), up=((4, d, d), BF16), out=((d, d), BF16), inner=((3, d, d), BF16), small=((Row.TOTAL, d), F32))


def part_plans(z):
    bits = [1 << i for i in range(z.n.bit_length() - 1)]
    plans = []
    for i, order in enumerate(Schedule.ORDERS):
        ordered = [bits[k] for k in order] + bits[len(order):] if len(bits) >= len(order) else bits
        rows = Row.TOTAL if i == len(Schedule.ORDERS) - 1 else z.width
        plans.append(halving_plan(rows, z.width, ordered, 8))
    return plans


def part_inboxes(z, v, i):
    d = z.width
    if i < 8:
        box = v.pool.at[pl.ds((i // 2) * d, d), pl.ds((i % 2) * d, d)]
    elif i < 12:
        box = v.boxes.at[i - 8]
    else:
        box = v.small_box
    views, row, column = [], 0, 0
    for _, _, rows, columns in z.plans[i]:
        views.append(box.at[pl.ds(row, rows), pl.ds(column, columns)])
        if columns == d:
            row += rows
        else:
            column += columns
            if column == d:
                row, column = row + rows, 0
    return views


def block(z, inputs, collective_id=0):
    d, f = z.width, z.hidden
    shapes = part_shapes(z)
    keep = keep_shapes(z)
    sums = sum_shapes(z)
    names, specs = [], []
    any_space = pl.BlockSpec(memory_space=pl.ANY)
    for name in inputs:
        names.append(name)
        specs.append(pl.BlockSpec(memory_space=pltpu.SMEM) if name == "doc_lengths" else any_space)
    outs = dict(output=((z.tokens, d), BF16), grad_tokens=((z.tokens, d), BF16))
    for name in shapes:
        outs["r_" + name] = shapes[name]
    pool = (z.cpd * z.panels * LANES, z.panel)
    saved = "toeplitz_saved"
    outs[saved] = (pool, BF16)
    scratch = {}
    fetched = tuple(name for name in inputs if name not in ("doc_lengths", "up_weight", "down_weight"))
    for name in fetched:
        shape = inputs[name].shape
        scratch["v_" + name] = pltpu.VMEM(shape if len(shape) > 1 else (1,) + shape, inputs[name].dtype)
    t = z.tokens
    buffers = dict(
        unit_one=((t, d), F32), inverse_one=((t, LANES), F32), normed=((t, d), BF16), projected=((t, 3 * d), BF16),
        rim_out=((8, 3 * d), F32), rim_in=((8, 3 * d), F32), rim_back_out=((8, 3 * d), F32), rim_back_in=((8, 3 * d), F32),
        keep_one=((t, LANES), F32), keep_two=((t, LANES), F32),
        gate_zero=((t, d), F32), gate_one=((t, d), F32), value_part=((t, d), F32),
        flipped=((d + 8, t), F32), slabs_out=((2, z.n, 2 * z.cpad, LANES), BF16), slabs_in=((2, z.n, 2 * z.cpad, LANES), BF16),
        wide=((z.n * 2 * z.cpad, LANES), F32), spread=((4, 2 * z.nb, LANES), F32), kept=((z.cpd, 4 * z.nb, LANES), BF16),
        pool=(pool, BF16),
        conv=((t, d), F32), mixed=((t, d), BF16), unit_two=((t, d), F32), inverse_two=((t, LANES), F32),
        normed_two=((t, d), BF16), residual=((t, d), F32), grad_normed=((t, d), F32),
        up_slots=((2, d, z.block), BF16), down_slots=((2, z.block, d), BF16), up_sums=((1, f), F32),
        grad_branch=((t, d), BF16), toeplitz_slots=((2, LANES, z.panel), BF16), back=((4 * z.nb, LANES), F32), fold=((8, z.length), F32),
        advanced=((4 * z.nb, z.panel), BF16), grad_taps=((z.cpad, z.length), F32),
    )
    for name, (shape, kind) in buffers.items():
        scratch[name] = pltpu.VMEM(shape, kind)
    for name in keep:
        scratch["k_" + name] = pltpu.VMEM(keep[name], F32)
    for name in sums:
        scratch["s_" + name] = pltpu.VMEM(sums[name], F32)
    steps, count = len(z.plans[0]), len(z.plans)
    scratch.update(
        boxes=pltpu.VMEM((4, d, d), BF16), small_box=pltpu.VMEM((Row.TOTAL + 8, d), F32),
        part_sends=pltpu.SemaphoreType.DMA((count, 2 * steps)), part_arrivals=pltpu.SemaphoreType.DMA((count, 2 * steps)),
        part_free=pltpu.SemaphoreType.REGULAR((count, steps)),
        loads=pltpu.SemaphoreType.DMA((len(fetched),)), stream=pltpu.SemaphoreType.DMA((3, 2)),
        saves=pltpu.SemaphoreType.DMA((1,)), rims=pltpu.SemaphoreType.DMA((4,)),
        sends=pltpu.SemaphoreType.DMA((4, z.n)), arrivals=pltpu.SemaphoreType.DMA((4, z.n)),
    )
    order = (tuple(names), tuple(outs), tuple(scratch), fetched, tuple(keep), tuple(sums))
    results = pl.pallas_call(
        functools.partial(block_kernel, z, order),
        out_shape=[jax.ShapeDtypeStruct(*outs[name]) if name == saved else pltpu.VMEM(*outs[name]) for name in outs],
        in_specs=specs,
        out_specs=[any_space if name == saved else pl.BlockSpec(memory_space=pltpu.VMEM) for name in outs],
        scratch_shapes=list(scratch.values()),
        compiler_params=pltpu.CompilerParams(collective_id=collective_id, has_side_effects=True, vmem_limit_bytes=47 << 20),
        name="hyena_block",
    )(*inputs.values())
    return dict(zip(outs, results))


def finish_layout(z):
    d, f = z.width, z.hidden
    return dict(
        grad_down_weight=((f, d), [("down", i, i * d, 0) for i in range(4)]),
        grad_up_weight=((d, f), [("up", i, 0, i * d) for i in range(4)]),
        grad_output_weight=((d, d), [("out", None, 0, 0)]),
        grad_input_weight=((d, 3 * d), [("inner", i, 0, i * d) for i in range(3)]),
    )


def small_layout(z):
    d, half = z.width, z.filt // 2
    def line(row, count=1):
        return (count * d,), [(row + i, 0, 1, d, 0, i * d) for i in range(count)]
    def short(row):
        return (z.filt,), [(row, 0, 1, z.filt, 0, 0)]
    return dict(
        grad_first_gain=line(Row.FIRST_GAIN), grad_first_shift=line(Row.FIRST_SHIFT), grad_input_bias=line(Row.INPUT_BIAS, 3),
        grad_short_kernel=((3, 3 * d), [(Row.SHORT_KERNEL + 3 * i + s, 0, 1, d, i, s * d) for i in range(3) for s in range(3)]),
        grad_short_bias=line(Row.SHORT_BIAS, 3),
        grad_embed_weight=((z.emb, z.filt), [
            (Row.NETWORK, 2 * LANES, half, z.filt, 0, 0), (Row.NETWORK, 3 * LANES, z.emb - half, z.filt, half, 0)]),
        grad_embed_bias=short(Row.EMBED_BIAS),
        grad_inner_weight=((z.filt, z.filt), [
            (Row.NETWORK, 0, half, z.filt, 0, 0), (Row.NETWORK, LANES, half, z.filt, half, 0)]),
        grad_inner_bias=short(Row.INNER_BIAS),
        grad_filter_weight=((z.filt, d), [(Row.FILTER, 0, z.filt, d, 0, 0)]),
        grad_decay_rates=line(Row.DECAY), grad_filter_bias=line(Row.FILTER_BIAS), grad_output_bias=line(Row.OUTPUT_BIAS),
        grad_second_gain=line(Row.SECOND_GAIN), grad_second_shift=line(Row.SECOND_SHIFT),
        grad_up_bias=line(Row.UP_BIAS, z.hidden // d), grad_down_bias=line(Row.DOWN_BIAS),
    )


RUN = 384


def finish_kernel(z, order, pieces, *refs):
    weights, little, names = order
    v = Names(names, refs)
    stores = []
    landed = []
    for i, (part, index, name, row, column, at, rows, columns) in enumerate(pieces):
        source = getattr(v, "r_" + part)
        landed.append(source if index is None else source.at[index])
        wide, out = getattr(v, "w_" + name), getattr(v, name)
        there = (pl.ds(row, rows), pl.ds(column, columns))
        stores.append(pltpu.make_async_copy(wide.at[there], out.at[there], v.stores.at[i]))
    others = [
        pltpu.make_async_copy(v.block_output, v.output, v.others.at[0]),
        pltpu.make_async_copy(v.block_grad_tokens, v.grad_tokens, v.others.at[1]),
    ]
    for copy in others:
        copy.start()
    for i, (part, index, name, row, column, at, rows, columns) in enumerate(pieces):
        getattr(v, "w_" + name)[row:row + rows, column:column + columns] = landed[i][at:at + rows, :].astype(F32)
        stores[i].start()
    for name, (shape, moves) in small_layout(z).items():
        out = getattr(v, name)
        for row, column, rows, columns, to_row, to_column in moves:
            value = v.r_small[row:row + rows, column:column + columns]
            if len(shape) == 1:
                out[to_column:to_column + columns] = value.reshape(columns)
            else:
                out[to_row:to_row + rows, to_column:to_column + columns] = value
    for copy in stores + others:
        copy.wait()


def finish(z, results):
    layout, little = finish_layout(z), small_layout(z)
    shapes = part_shapes(z)
    pieces = []
    for name in layout:
        for part, index, row, column in layout[name][1]:
            rows, columns = shapes[part][0][-2:]
            for at in range(0, rows, RUN):
                pieces.append((part, index, name, row + at, column, at, min(RUN, rows - at), columns))
    any_space, vmem = pl.BlockSpec(memory_space=pl.ANY), pl.BlockSpec(memory_space=pltpu.VMEM)
    arguments = dict(("r_" + part, results["r_" + part]) for part in shapes)
    arguments.update(block_output=results["output"], block_grad_tokens=results["grad_tokens"])
    arguments = dict((name, pltpu.with_memory_space_constraint(value, pltpu.VMEM)) for name, value in arguments.items())
    outs = dict((name, jax.ShapeDtypeStruct(layout[name][0], F32)) for name in layout)
    token_shape = jax.ShapeDtypeStruct((z.tokens, z.width), BF16)
    outs.update(output=token_shape, grad_tokens=token_shape)
    outs.update((name, jax.ShapeDtypeStruct(little[name][0], F32)) for name in little)
    scratch = dict(("w_" + name, pltpu.VMEM(layout[name][0], F32)) for name in layout)
    scratch.update(
        stores=pltpu.SemaphoreType.DMA((len(pieces),)), others=pltpu.SemaphoreType.DMA((2,))
    )
    names = tuple(arguments) + tuple(outs) + tuple(scratch)
    outputs = pl.pallas_call(
        functools.partial(finish_kernel, z, (tuple(layout), tuple(little), names), pieces),
        out_shape=list(outs.values()),
        in_specs=[vmem] * len(arguments),
        out_specs=[any_space] * (len(layout) + 2) + [vmem] * len(little),
        scratch_shapes=list(scratch.values()),
        compiler_params=pltpu.CompilerParams(vmem_limit_bytes=30 << 20),
        name="widen_gradients",
    )(*arguments.values())
    return Names(outs, outputs)


def shards(
    n, tokens, doc_lengths, first_gain, first_shift, input_weight, input_bias, short_kernel, short_bias, embed_weight, embed_bias,
    inner_weight, inner_bias, filter_weight, decay_rates, filter_bias, output_weight, output_bias, second_gain, second_shift,
    up_weight, up_bias, down_weight, down_bias, cotangent,
):
    rows, local, width = tokens.shape
    z = Sizes(n, rows, local, width, *embed_weight.shape, up_weight.shape[1])
    z.plans = part_plans(z)
    inputs = dict(
        tokens=tokens.reshape(rows * local, width), doc_lengths=doc_lengths, first_gain=first_gain, first_shift=first_shift,
        input_weight=input_weight, input_bias=input_bias, short_kernel=short_kernel, short_bias=short_bias, embed_weight=embed_weight,
        embed_bias=embed_bias, inner_weight=inner_weight, inner_bias=inner_bias, filter_weight=filter_weight, decay_rates=decay_rates,
        filter_bias=filter_bias, output_weight=output_weight, output_bias=output_bias, second_gain=second_gain,
        second_shift=second_shift, up_weight=up_weight, up_bias=up_bias, down_weight=down_weight, down_bias=down_bias,
        cotangent=cotangent.reshape(rows * local, width),
    )
    o = finish(z, block(z, inputs))
    return (
        o.output.reshape(tokens.shape), o.grad_tokens.reshape(tokens.shape), o.grad_first_gain, o.grad_first_shift, o.grad_input_weight,
        o.grad_input_bias, o.grad_short_kernel, o.grad_short_bias, o.grad_embed_weight, o.grad_embed_bias, o.grad_inner_weight,
        o.grad_inner_bias, o.grad_filter_weight, o.grad_decay_rates, o.grad_filter_bias, o.grad_output_weight, o.grad_output_bias,
        o.grad_second_gain, o.grad_second_shift, o.grad_up_weight, o.grad_up_bias, o.grad_down_weight, o.grad_down_bias,
    )


def solution(mesh):
    split, whole = P(None, "seq", None), P()
    return jax.shard_map(
        functools.partial(shards, mesh.shape["seq"]),
        mesh=mesh,
        in_specs=(split,) + (whole,) * 22 + (split,),
        out_specs=(split, split) + (whole,) * 21,
        check_vma=False,
    )
```

```python
import functools
import math

import jax
import jax.numpy as jnp
from jax import lax
from jax.experimental import pallas as pl
from jax.experimental.pallas import tpu as pltpu
from jax.sharding import PartitionSpec as P

MESH = pl.DeviceIdType.MESH
EPSILON = 1e-05


def bit_of(me, bit):
    return lax.rem(lax.div(me, bit), 2)

def partner_of(me, bit):
    return me + bit - 2 * bit * bit_of(me, bit)

def halving_plan(rows, columns, order, row_unit, column_unit=128):
    steps = []
    for bit in order:
        if rows % (2 * row_unit) == 0:
            rows //= 2
            steps.append((bit, "row", rows, columns))
        elif columns % (2 * column_unit) == 0:
            columns //= 2
            steps.append((bit, "column", rows, columns))
        else:
            steps.append((bit, "full", rows, columns))
    return steps

class Reduction:
    def __init__(self, array, plan, inbox, sends, arrivals, free, me):
        self.array, self.plan, self.inbox = array, plan, inbox
        self.sends, self.arrivals, self.free, self.me = sends, arrivals, free, me
        self.row, self.column = 0, 0
        self.origin = []
        for bit, kind, rows, columns in plan:
            mine = bit_of(me, bit)
            keep, give = (self.row, self.column), (self.row, self.column)
            if kind == "row":
                keep = (self.row + mine * rows, self.column)
                give = (self.row + (1 - mine) * rows, self.column)
            elif kind == "column":
                keep = (self.row, self.column + mine * columns)
                give = (self.row, self.column + (1 - mine) * columns)
            self.origin.append((keep, give))
            self.row, self.column = keep
        self.unit_rows = plan[-1][2]
        self.unit_columns = plan[-1][3]
        self.unit_columns = min(p[3] for p in plan)
        self.unit_rows = min(p[2] for p in plan)

    def window(self, ref, origin, rows, columns):
        row, column = origin
        if not isinstance(row, int):
            row = pl.multiple_of(row, self.unit_rows)
        if not isinstance(column, int):
            column = pl.multiple_of(column, self.unit_columns)
        return ref.at[pl.ds(row, rows), pl.ds(column, columns)]

    def give_copy(self, s):
        bit, kind, rows, columns = self.plan[s]
        return pltpu.make_async_remote_copy(
            src_ref=self.window(self.array, self.origin[s][1], rows, columns),
            dst_ref=self.inbox[s],
            send_sem=self.sends.at[s], recv_sem=self.arrivals.at[s],
            device_id=(partner_of(self.me, bit),), device_id_type=MESH)

    def share_copy(self, s):
        bit, kind, rows, columns = self.plan[s]
        here = self.window(self.array, self.origin[s][0], rows, columns)
        n = len(self.plan)
        return pltpu.make_async_remote_copy(
            src_ref=here, dst_ref=here,
            send_sem=self.sends.at[n + s], recv_sem=self.arrivals.at[n + s],
            device_id=(partner_of(self.me, bit),), device_id_type=MESH)

    def give(self, s):
        self.give_copy(s).start()

    def take(self, s):
        self.give_copy(s).wait()
        bit, kind, rows, columns = self.plan[s]
        if kind != "full":
            pl.semaphore_signal(
                self.free.at[s], inc=1, device_id=(partner_of(self.me, bit),), device_id_type=MESH
            )
        row, column = self.origin[s][0]
        if not isinstance(column, int):
            column = pl.multiple_of(column, self.unit_columns)
        chunk = self.unit_rows
        while chunk * 2 <= 96 and rows % (chunk * 2) == 0:
            chunk *= 2
        inbox = self.inbox[s]
        array = self.array
        def body(i, carry):
            at = pl.multiple_of(i * chunk, chunk)
            here = (pl.ds(pl.multiple_of(row + at, self.unit_rows), chunk), pl.ds(column, columns))
            array[here] = array[here] + inbox[pl.ds(at, chunk), :]
            return carry
        lax.fori_loop(0, rows // chunk, body, 0)

    def share(self, s):
        if self.plan[s][1] != "full":
            pl.semaphore_wait(self.free.at[s], 1)
            self.share_copy(s).start()

    def collect(self, s):
        if self.plan[s][1] != "full":
            self.share_copy(s).wait()


HIGHEST = lax.Precision.HIGHEST
LANES = 128
PANEL = 2048

def ceil8(v):
    return -(-v // 8) * 8

def sin_cos(x):
    turns = jnp.round(x * (2.0 / math.pi))
    r = ((x - turns * 1.5703125) - turns * 4.837512969970703125e-4) - turns * 7.54978995489188e-8
    quadrant = turns.astype(jnp.int32)
    z = r * r
    s = ((-1.9515295891e-4 * z + 8.3321608736e-3) * z - 1.6666654611e-1) * z * r + r
    c = ((2.443315711809948e-5 * z - 1.388731625493765e-3) * z + 4.166664568298827e-2) * z * z - 0.5 * z + 1.0
    swap = (quadrant & 1) == 1
    sin_part = jnp.where(swap, c, s)
    cos_part = jnp.where(swap, s, c)
    sin_out = jnp.where((quadrant & 2) == 2, -sin_part, sin_part)
    cos_out = jnp.where(((quadrant + 1) & 2) == 2, -cos_part, cos_part)
    return sin_out, cos_out

def dot(a, b, ca, cb, precision=None):
    return lax.dot_general(a, b, (((ca,), (cb,)), ((), ())), precision=precision, preferred_element_type=jnp.float32)

class Sizes:
    def __init__(self, n, rows, local, width, emb, filt, hidden=3072):
        self.hidden, self.block = hidden, hidden // 8
        self.n, self.rows, self.local, self.width, self.emb, self.filt = n, rows, local, width, emb, filt
        self.length = n * local
        self.cpd = width // n
        self.cpad = ceil8(self.cpd)
        self.nb = self.length // LANES
        self.tokens = rows * local
        self.tiles = self.tokens // LANES
        self.erows = ceil8(emb)
        self.panel = min(PANEL, self.length)
        self.panels = self.length // self.panel
        assert local * 2 == LANES and rows == 4

def own_selection(z, me):
    want = lax.broadcasted_iota(jnp.int32, (z.cpad, z.width), 0)
    have = lax.broadcasted_iota(jnp.int32, (z.cpad, z.width), 1)
    return jnp.where((have == want + me * z.cpd) & (want < z.cpd), 1.0, 0.0).astype(jnp.float32)

def embed_rows(z, at, count):
    row = lax.broadcasted_iota(jnp.int32, (z.erows, count), 0)
    t = at + lax.broadcasted_iota(jnp.int32, (z.erows, count), 1)
    bands = (z.emb - 1) // 2
    harmonic = jnp.where(row <= bands, row, row - bands)
    angle = lax.rem(t * harmonic, z.length).astype(jnp.float32) * (2.0 * math.pi / z.length)
    s, c = sin_cos(angle)
    scaled = t.astype(jnp.float32) / z.length
    return jnp.where(row == 0, scaled, jnp.where(row <= bands, c, jnp.where(row < z.emb, s, 0.0)))

def columns(ref, count):
    eye = (lax.broadcasted_iota(jnp.int32, (count, count), 0) == lax.broadcasted_iota(jnp.int32, (count, count), 1)).astype(jnp.float32)
    return dot(eye, jnp.broadcast_to(ref[...], (8, count)), 1, 1, HIGHEST)[:, 0:1]

CHUNK = 512

def filter_setup(z, me, w, keep):
    select = own_selection(z, me)
    keep.own_filter[...] = dot(select, w.filter_weight[...], 1, 1, HIGHEST)
    own_decay = dot(select, jnp.broadcast_to(w.decay_rates[...], (8, z.width)), 1, 1, HIGHEST)[:, 0:1]
    keep.own_decay[...] = jnp.broadcast_to(own_decay, (z.cpad, LANES))
    keep.embed_pad[...] = jnp.zeros((z.erows, z.filt), jnp.float32)
    keep.embed_pad[0:z.emb, :] = w.embed_weight[...]
    keep.bias_one[...] = jnp.broadcast_to(columns(w.embed_bias, z.filt), (z.filt, LANES))
    keep.bias_two[...] = jnp.broadcast_to(columns(w.inner_bias, z.filt), (z.filt, LANES))


def filter_hidden(z, w, keep, at):
    embedded = embed_rows(z, at, CHUNK)
    s1, c1 = sin_cos(dot(keep.embed_pad[...], embedded, 0, 0, HIGHEST) + keep.bias_one[:, 0:1])
    s2, c2 = sin_cos(dot(w.inner_weight[...], s1, 0, 0, HIGHEST) + keep.bias_two[:, 0:1])
    scaled = (at + lax.broadcasted_iota(jnp.int32, (z.cpad, CHUNK), 1)).astype(jnp.float32) / z.length
    window = jnp.exp(-keep.own_decay[:, 0:1] * scaled)
    return embedded, s1, c1, s2, c2, scaled, window


def filter_forward(z, w, keep, begin, end):
    def body(i, carry):
        at = pl.multiple_of(i * CHUNK, CHUNK)
        embedded, s1, c1, s2, c2, scaled, window = filter_hidden(z, w, keep, at)
        keep.taps[:, pl.ds(at, CHUNK)] = dot(keep.own_filter[...], s2, 1, 0, HIGHEST) * window
        return carry
    lax.fori_loop(begin, end, body, 0)

def filter_backward(z, w, keep, grad_taps, sums):
    for ref in vars(sums).values():
        ref[...] = jnp.zeros(ref.shape, jnp.float32)
    def body(i, carry):
        at = pl.multiple_of(i * CHUNK, CHUNK)
        here = (slice(None), pl.ds(at, CHUNK))
        embedded, s1, c1, s2, c2, scaled, window = filter_hidden(z, w, keep, at)
        grad = grad_taps[here]
        decay = -jnp.sum(grad * keep.taps[here] * scaled, axis=1, keepdims=True)
        sums.decay[...] += jnp.broadcast_to(decay, (z.cpad, LANES))
        grad_raw = grad * window
        sums.filter[...] += dot(grad_raw, s2, 1, 1, HIGHEST)
        two = dot(keep.own_filter[...], grad_raw, 0, 0, HIGHEST) * c2
        sums.inner[...] += dot(s1, two, 1, 1, HIGHEST)
        sums.inner_bias[...] += jnp.broadcast_to(jnp.sum(two, axis=1, keepdims=True), (z.filt, LANES))
        one = dot(w.inner_weight[...], two, 1, 0, HIGHEST) * c1
        sums.embed[...] += dot(embedded, one, 1, 1, HIGHEST)
        sums.embed_bias[...] += jnp.broadcast_to(jnp.sum(one, axis=1, keepdims=True), (z.filt, LANES))
        return carry
    lax.fori_loop(0, z.length // CHUNK, body, 0)

def build_toeplitz(z, taps, pool):
    sub = lax.broadcasted_iota(jnp.int32, (8, z.length), 0)
    lane = lax.broadcasted_iota(jnp.int32, (8, LANES), 1)
    sub1 = lax.broadcasted_iota(jnp.int32, (8, LANES), 0)
    def body(c, carry):
        base = jnp.broadcast_to(taps[pl.ds(c, 1), :], (8, z.length))
        for bit in (1, 2, 4):
            base = jnp.where((sub & bit) == bit, pltpu.roll(base, bit, 1), base)
        for q in range(0, LANES // 8, 2):
            parts = []
            for u in (q, q + 1):
                part = pltpu.roll(base, 8 * u, 1) if u else base
                first = jnp.where(lane >= sub1 + 8 * u, part[:, :LANES], 0.0)
                parts.append(jnp.concatenate([first, part[:, LANES:]], axis=1))
            pair = jnp.concatenate(parts, axis=0).astype(jnp.bfloat16)
            for k in range(z.panels):
                at = pl.multiple_of((c * z.panels + k) * LANES, LANES) + 8 * q
                pool[pl.ds(pl.multiple_of(at, 16), 16), :] = pair[:, k * z.panel:(k + 1) * z.panel]
        return carry
    lax.fori_loop(0, z.cpd, body, 0)

def fold_panel(z, k, product, fold):
    lane = lax.broadcasted_iota(jnp.int32, (8, LANES), 1)
    row = lax.broadcasted_iota(jnp.int32, (8, LANES), 0)
    sums, before = None, None
    for u in range(LANES // 8):
        part = product[8 * u:8 * u + 8, :]
        first = part[:, :LANES]
        inside = lane >= row + 8 * u
        part = jnp.concatenate([jnp.where(inside, first, 0.0), part[:, LANES:]], axis=1)
        part = pltpu.roll(part, z.panel - 8 * u, 1) if u else part
        sums = part if sums is None else sums + part
        if k:
            outside = jnp.where(inside, 0.0, first)
            outside = pltpu.roll(outside, LANES - 8 * u, 1) if u else outside
            before = outside if before is None else before + outside
    fold[:, k * z.panel:(k + 1) * z.panel] = sums
    if k:
        fold[:, k * z.panel - LANES:k * z.panel] += before


def fold_rows(z, fold):
    sums = fold[...]
    row = lax.broadcasted_iota(jnp.int32, sums.shape, 0)
    for bit in (1, 2, 4):
        sums = jnp.where((row & bit) == bit, pltpu.roll(sums, z.length - bit, 1), sums)
    return jnp.sum(sums, axis=0, keepdims=True)

class Exchange:
    def __init__(self, outgoing, incoming, sends, arrivals, me, n):
        self.outgoing, self.incoming, self.sends, self.arrivals, self.me, self.n = outgoing, incoming, sends, arrivals, me, n
    def copy(self, k):
        to = lax.rem(self.me + k, self.n)
        return pltpu.make_async_remote_copy(
            src_ref=self.outgoing.at[to], dst_ref=self.incoming.at[self.me],
            send_sem=self.sends.at[k], recv_sem=self.arrivals.at[k],
            device_id=(to,), device_id_type=MESH)
    def start(self):
        def body(k, carry):
            self.copy(k).start()
            return carry
        lax.fori_loop(1, self.n, body, 0)
        self.incoming[self.me] = self.outgoing[self.me]
    def wait(self):
        def body(k, carry):
            self.copy(k).wait()
            return carry
        lax.fori_loop(1, self.n, body, 0)

def each_slab(z, body):
    if z.cpd % 8 == 0:
        lax.fori_loop(0, z.n, body, 0)
    else:
        for k in range(z.n):
            body(k, 0)

def slabs_from_rows(z, flipped, outgoing):
    def body(k, carry):
        at = k * z.cpd
        if z.cpd % 8 == 0:
            at = pl.multiple_of(at, 8)
        slab = flipped[pl.ds(at, z.cpad), :]
        outgoing[k] = jnp.concatenate([slab[:, :LANES], slab[:, LANES:]], axis=0).astype(outgoing.dtype)
        return carry
    each_slab(z, body)

def rows_from_slabs(z, incoming, flipped):
    def body(k, carry):
        at = k * z.cpd
        if z.cpd % 8 == 0:
            at = pl.multiple_of(at, 8)
        slab = incoming[k].astype(jnp.float32)
        flipped[pl.ds(at, z.cpad), :] = jnp.concatenate([slab[:z.cpad], slab[z.cpad:]], axis=1)
        return carry
    each_slab(z, body)

def widen_slabs(z, incoming, wide):
    def body(j, carry):
        wide[pl.ds(pl.multiple_of(j * 2 * z.cpad, 8), 2 * z.cpad), :] = incoming[j].astype(jnp.float32)
        return carry
    lax.fori_loop(0, z.n, body, 0)

def narrow_slabs(z, wide, outgoing):
    def body(j, carry):
        outgoing[j] = wide[pl.ds(pl.multiple_of(j * 2 * z.cpad, 8), 2 * z.cpad), :].astype(outgoing.dtype)
        return carry
    lax.fori_loop(0, z.n, body, 0)

def channel_blocks(z, wide, c):
    lane = lax.broadcasted_iota(jnp.int32, (z.nb, LANES), 1)
    low = lane < LANES // 2
    out = []
    for t in range(2):
        even = wide[pl.ds(t * z.cpad + c, z.nb, 4 * z.cpad), :]
        odd = wide[pl.ds((2 + t) * z.cpad + c, z.nb, 4 * z.cpad), :]
        out.append(jnp.where(low, even, pltpu.roll(odd, LANES // 2, 1)))
        out.append(jnp.where(low, pltpu.roll(even, LANES // 2, 1), odd))
    return out

def put_channel_blocks(z, wide, c, blocks):
    lane = lax.broadcasted_iota(jnp.int32, (z.nb, LANES), 1)
    low = lane < LANES // 2
    for t in range(2):
        a, b = blocks[2 * t], blocks[2 * t + 1]
        wide[pl.ds(t * z.cpad + c, z.nb, 4 * z.cpad), :] = jnp.where(low, a, pltpu.roll(b, LANES // 2, 1))
        wide[pl.ds((2 + t) * z.cpad + c, z.nb, 4 * z.cpad), :] = jnp.where(low, pltpu.roll(a, LANES // 2, 1), b)

def panel_rows(z, c, k):
    return pl.ds(pl.multiple_of((c * z.panels + k) * LANES, LANES), LANES)


def convolve_forward(z, wide, pool, kept, spread):
    each = z.panel // LANES
    def body(c, carry):
        blocks = channel_blocks(z, wide, c)
        x = jnp.concatenate(blocks, axis=0).astype(jnp.bfloat16)
        kept[c] = x
        spread[...] = jnp.zeros(spread.shape, jnp.float32)
        for k in range(z.panels):
            product = dot(x, pool[panel_rows(z, c, k), :], 1, 0)
            for i in range(each):
                d = k * each + i
                for r in range(4):
                    spread[r, d:d + z.nb, :] += product[r * z.nb:(r + 1) * z.nb, i * LANES:(i + 1) * LANES]
        put_channel_blocks(z, wide, c, [spread[r, 0:z.nb, :] for r in range(4)])
        return carry
    lax.fori_loop(0, z.cpd, body, 0)


def convolve_back_channel(z, c, wide, panel_of, kept, spread, advanced, back, fold, grad_taps):
    blocks = channel_blocks(z, wide, c)
    for r in range(4):
        spread[r, 0:z.nb, :] = blocks[r]
    each = z.panel // LANES
    source = kept[c].astype(jnp.float32).T.astype(jnp.bfloat16)
    for k in range(z.panels):
        for i in range(each):
            d = k * each + i
            advanced[:, i * LANES:(i + 1) * LANES] = jnp.concatenate(
                [spread[r, d:d + z.nb, :] for r in range(4)], axis=0).astype(jnp.bfloat16)
        panel = panel_of(c, k)
        product = dot(advanced[...], panel[...], 1, 1)
        back[...] = product if k == 0 else back[...] + product
        fold_panel(z, k, dot(source, advanced[...], 1, 0), fold)
    put_channel_blocks(z, wide, c, [back[r * z.nb:(r + 1) * z.nb, :] for r in range(4)])
    grad_taps[pl.ds(c, 1), :] = fold_rows(z, fold)


class Names:
    def __init__(self, names, values):
        vars(self).update(zip(names, values))


def keep_shapes(z):
    return dict(
        own_filter=(z.cpad, z.filt), own_decay=(z.cpad, LANES), embed_pad=(z.erows, z.filt),
        bias_one=(z.filt, LANES), bias_two=(z.filt, LANES), taps=(z.cpad, z.length),
    )


def sum_shapes(z):
    return dict(
        decay=(z.cpad, LANES), filter=(z.cpad, z.filt), inner=(z.filt, z.filt), inner_bias=(z.filt, LANES),
        embed=(z.erows, z.filt), embed_bias=(z.filt, LANES),
    )


F32, BF16 = jnp.float32, jnp.bfloat16
BLOCKS = 8
WIDE = 256


class Row:
    FIRST_GAIN, FIRST_SHIFT, INPUT_BIAS, SHORT_KERNEL, SHORT_BIAS = 0, 1, 2, 5, 14
    DECAY, FILTER_BIAS, OUTPUT_BIAS, SECOND_GAIN, SECOND_SHIFT, UP_BIAS, DOWN_BIAS = 17, 18, 19, 20, 21, 22, 26
    EMBED_BIAS, INNER_BIAS = 27, 28
    FILTER, NETWORK, TOTAL = 32, 96, 128


def normalize(x):
    center = x - jnp.mean(x, axis=-1, keepdims=True)
    inverse = lax.rsqrt(jnp.mean(center * center, axis=-1, keepdims=True) + EPSILON)
    return center * inverse, inverse


def normalize_back(gradient, gain, unit, inverse):
    q = gradient * gain
    return (q - jnp.mean(q, axis=-1, keepdims=True) - unit * jnp.mean(q * unit, axis=-1, keepdims=True)) * inverse


def as_row(column):
    size = column.shape[0]
    row, lane = (lax.broadcasted_iota(jnp.int32, (size, size), i) for i in range(2))
    return dot(column, jnp.where(row == lane, 1.0, 0.0).astype(F32), 0, 0, HIGHEST)[0:1, :]


def total(x):
    return jnp.sum(x, axis=0, keepdims=True)


def row_masks(z, me, lengths, keep_one, keep_two):
    for r in range(z.rows):
        position = me * z.local + lax.broadcasted_iota(jnp.int32, (z.local, LANES), 0)
        first = position == 0
        second = position == 1
        end = 0
        for j in range(lengths.shape[1] - 1):
            end = end + lengths[r, j]
            first = first | (position == end)
            second = second | (position == end + 1)
        keep_one[r * z.local:(r + 1) * z.local, :] = jnp.where(first, 0.0, 1.0)
        keep_two[r * z.local:(r + 1) * z.local, :] = jnp.where(first | second, 0.0, 1.0)


def lagged(z, values, halo, t, columns):
    row = lax.broadcasted_iota(jnp.int32, (LANES, 1), 0)
    one, two = pltpu.roll(values, 1, 0), pltpu.roll(values, 2, 0)
    for u in range(2):
        r = 2 * t + u
        older, newer = halo[2 * r:2 * r + 1, columns], halo[2 * r + 1:2 * r + 2, columns]
        one = jnp.where(row == u * z.local, newer, one)
        two = jnp.where(row == u * z.local, older, jnp.where(row == u * z.local + 1, newer, two))
    return one, two


def halves(t):
    return slice(t * LANES, (t + 1) * LANES)


class Flow:
    def __init__(self, reduction):
        self.reduction = reduction
        self.steps = len(reduction.plan)
        self.at = -1
    def advance(self):
        s, n, r = self.at, self.steps, self.reduction
        if s < 0:
            r.give(0)
        elif s < n - 1:
            r.take(s)
            r.give(s + 1)
        elif s == n - 1:
            r.take(s)
            r.share(s)
        elif s < 2 * n - 1:
            r.collect(2 * n - 1 - s)
            r.share(2 * n - 2 - s)
        elif s == 2 * n - 1:
            r.collect(0)
        self.at += 1
    @property
    def done(self):
        return self.at >= 2 * self.steps


def block_kernel(z, order, *refs):
    inputs, outs, scratch, fetched, keep_names, sum_names = order
    v = Names(inputs + outs + scratch, refs)
    me = lax.axis_index("seq")
    n = z.n
    d = z.width
    p = Names(fetched, [getattr(v, "v_" + name) for name in fetched])
    def fetch(name):
        source, target = getattr(v, name), getattr(p, name)
        if len(source.shape) == 1:
            target = target.at[0]
        return pltpu.make_async_copy(source, target, v.loads.at[fetched.index(name)])
    late = ("input_weight", "output_weight", "cotangent")
    soon = [name for name in fetched if name not in late]
    for name in soon + list(late):
        fetch(name).start()
    def weight_block(j, slot):
        at = pl.multiple_of(j * z.block, LANES)
        return (
            pltpu.make_async_copy(v.up_weight.at[:, pl.ds(at, z.block)], v.up_slots.at[slot], v.stream.at[0, slot]),
            pltpu.make_async_copy(v.down_weight.at[pl.ds(at, z.block), :], v.down_slots.at[slot], v.stream.at[1, slot]),
        )
    for copy in weight_block(0, 0):
        copy.start()
    barrier = pltpu.get_barrier_semaphore()
    def greet(k, carry):
        pl.semaphore_signal(barrier, inc=1, device_id=(lax.rem(me + k, n),), device_id_type=MESH)
        return carry
    lax.fori_loop(1, n, greet, 0)
    small = v.r_small
    small[0:Row.FILTER, :] = jnp.zeros((Row.FILTER, d), F32)
    small[Row.NETWORK:Row.TOTAL, :] = jnp.zeros((Row.TOTAL - Row.NETWORK, d), F32)
    row_masks(z, me, v.doc_lengths, v.keep_one, v.keep_two)

    for name in soon:
        fetch(name).wait()
    tokens = p.tokens
    for t in range(z.tiles):
        unit, inverse = normalize(tokens[halves(t), :].astype(F32))
        v.unit_one[halves(t), :] = unit
        v.inverse_one[halves(t), :] = jnp.broadcast_to(inverse, (LANES, LANES))
        v.normed[halves(t), :] = (unit * p.first_gain[...] + p.first_shift[...]).astype(BF16)
    fetch("input_weight").wait()
    part = 3 * d // 6
    def project(j, carry):
        here = pl.ds(pl.multiple_of(j * part, LANES), part)
        values = (dot(v.normed[...], p.input_weight[:, here], 1, 0) + p.input_bias[:, here]).astype(BF16)
        v.projected[:, here] = values
        rounded = values.astype(F32)
        for r in range(z.rows):
            last = (r + 1) * z.local
            v.rim_out[2 * r:2 * r + 2, here] = rounded[last - 2:last, :]
        return carry
    lax.fori_loop(0, 6, project, 0)
    pl.semaphore_wait(barrier, n - 1)
    ahead, behind = lax.rem(me + 1, n), lax.rem(me + n - 1, n)
    rim = pltpu.make_async_remote_copy(
        src_ref=v.rim_out, dst_ref=v.rim_in, send_sem=v.rims.at[0], recv_sem=v.rims.at[1],
        device_id=(ahead,), device_id_type=MESH)
    rim.start()
    keep = Names(keep_names, [getattr(v, "k_" + name) for name in keep_names])
    chunks = z.length // CHUNK
    early = chunks // 2
    filter_setup(z, me, p, keep)
    filter_forward(z, p, keep, 0, early)
    rim.wait()

    def short(j, carry):
        inner = pl.ds(pl.multiple_of(j * WIDE, LANES), WIDE)
        for t in range(z.tiles):
            k1, k2 = v.keep_one[halves(t), 0:1], v.keep_two[halves(t), 0:1]
            streams = []
            for s in range(3):
                here = pl.ds(pl.multiple_of(s * d + j * WIDE, LANES), WIDE)
                values = v.projected[halves(t), here].astype(F32)
                one, two = lagged(z, values, v.rim_in, t, here)
                taps = p.short_kernel
                out = (taps[0:1, here] * values + taps[1:2, here] * (k1 * one) + taps[2:3, here] * (k2 * two)
                       + p.short_bias[:, here])
                (v.gate_zero, v.gate_one, v.value_part)[s][halves(t), inner] = out
                streams.append(out)
            v.flipped[inner, halves(t)] = (streams[1] * streams[2]).T
        return carry
    lax.fori_loop(0, d // WIDE, short, 0)
    v.flipped[d:, :] = jnp.zeros((8, z.tokens), F32)

    def exchange(i):
        return Exchange(v.slabs_out.at[i % 2], v.slabs_in.at[i % 2], v.sends.at[i], v.arrivals.at[i], me, n)
    slabs_from_rows(z, v.flipped, v.slabs_out.at[0])
    first = exchange(0)
    first.start()
    filter_forward(z, p, keep, early, chunks)
    build_toeplitz(z, keep.taps, v.pool)
    first.wait()
    widen_slabs(z, v.slabs_in.at[0], v.wide)
    save = pltpu.make_async_copy(v.pool, v.toeplitz_saved, v.saves.at[0])
    save.start()
    convolve_forward(z, v.wide, v.pool, v.kept, v.spread)
    save.wait()
    narrow_slabs(z, v.wide, v.slabs_out.at[1])
    second = exchange(1)
    second.start()
    fetch("output_weight").wait()
    fetch("cotangent").wait()
    cotangent = p.cotangent
    small[Row.DOWN_BIAS:Row.DOWN_BIAS + 1, :] = total(cotangent[...].astype(F32))
    second.wait()
    rows_from_slabs(z, v.slabs_in.at[1], v.flipped)

    def gate(j, carry):
        inner = pl.ds(pl.multiple_of(j * WIDE, LANES), WIDE)
        for t in range(z.tiles):
            gated = v.value_part[halves(t), inner] * v.gate_one[halves(t), inner]
            conv = v.flipped[inner, halves(t)].T + p.filter_bias[:, inner] * gated
            v.conv[halves(t), inner] = conv
            v.mixed[halves(t), inner] = (conv * v.gate_zero[halves(t), inner]).astype(BF16)
        return carry
    lax.fori_loop(0, d // WIDE, gate, 0)
    for t in range(z.tiles):
        branch = dot(v.mixed[halves(t), :], p.output_weight[...], 1, 0) + p.output_bias[...]
        residual = tokens[halves(t), :].astype(F32) + branch
        unit, inverse = normalize(residual)
        v.unit_two[halves(t), :] = unit
        v.inverse_two[halves(t), :] = jnp.broadcast_to(inverse, (LANES, LANES))
        v.normed_two[halves(t), :] = (unit * p.second_gain[...] + p.second_shift[...]).astype(BF16)
        v.residual[halves(t), :] = residual + p.down_bias[...]
    v.grad_normed[...] = jnp.zeros((z.tokens, d), F32)

    arrays = [v.r_down.at[i] for i in range(4)] + [v.r_up.at[i] for i in range(4)] + [v.r_out] + [v.r_inner.at[i] for i in range(3)] + [v.r_small]
    flows = []
    for i, (array, plan) in enumerate(zip(arrays, z.plans)):
        reduction = Reduction(array, plan, part_inboxes(z, v, i), v.part_sends.at[i], v.part_arrivals.at[i], v.part_free.at[i], me)
        flows.append(Flow(reduction))
    def run(parts):
        for i in parts:
            if not flows[i].done:
                flows[i].advance()

    def mlp(j, carry):
        slot = lax.rem(j, 2)
        for copy in weight_block(j, slot):
            copy.wait()
        @pl.when(j + 1 < BLOCKS)
        def _():
            for copy in weight_block(j + 1, 1 - slot):
                copy.start()
        up, down = v.up_slots[slot], v.down_slots[slot]
        here = pl.ds(pl.multiple_of(j * z.block, LANES), z.block)
        x = dot(v.normed_two[...], up, 1, 0) + p.up_bias[:, here]
        grad_hidden = dot(cotangent[...], down, 1, 1)
        root = math.sqrt(2.0 / math.pi)
        square = x * x
        curve = jnp.tanh(root * (x + 0.044715 * (square * x)))
        half = 0.5 * (1.0 + curve)
        hidden = (x * half).astype(BF16)
        slope = half + 0.5 * x * (1.0 - curve * curve) * (root * (1.0 + 3.0 * 0.044715 * square))
        grad_pre = (grad_hidden * slope).astype(BF16)
        v.residual[...] += dot(hidden, down, 1, 0)
        v.grad_normed[...] += dot(grad_pre, up, 1, 1)
        part, half_part = lax.div(j, 2), lax.rem(j, 2)
        there = pl.ds(pl.multiple_of(half_part * z.block, LANES), z.block)
        v.r_down[part, there, :] = dot(hidden, cotangent[...], 0, 0).astype(BF16)
        v.r_up[part, :, there] = dot(v.normed_two[...], grad_pre, 0, 0).astype(BF16)
        v.up_sums[:, here] = total(grad_pre.astype(F32))
        return carry
    for i in range(4):
        lax.fori_loop(2 * i, 2 * i + 2, mlp, 0)
        if i:
            run(Schedule.MLP[i - 1])
        run((i, 4 + i))
    wide_rows = v.up_sums.shape[1] // d
    for i in range(wide_rows):
        small[Row.UP_BIAS + i:Row.UP_BIAS + i + 1, :] = v.up_sums[:, i * d:(i + 1) * d]
    v.output[...] = v.residual[...].astype(BF16)

    gain_sum, shift_sum, bias_sum = 0.0, 0.0, 0.0
    for t in range(z.tiles):
        gradient = v.grad_normed[halves(t), :]
        unit = v.unit_two[halves(t), :]
        gain_sum = gain_sum + total(gradient * unit)
        shift_sum = shift_sum + total(gradient)
        value = cotangent[halves(t), :].astype(F32) + normalize_back(gradient, p.second_gain[...], unit, v.inverse_two[halves(t), 0:1])
        v.residual[halves(t), :] = value
        branch = value.astype(BF16)
        v.grad_branch[halves(t), :] = branch
        bias_sum = bias_sum + total(branch.astype(F32))
    small[Row.SECOND_GAIN:Row.SECOND_GAIN + 1, :] = gain_sum
    small[Row.SECOND_SHIFT:Row.SECOND_SHIFT + 1, :] = shift_sum
    small[Row.OUTPUT_BIAS:Row.OUTPUT_BIAS + 1, :] = bias_sum
    grad_conv, grad_gate_zero = v.unit_two, v.grad_normed
    def mix_back(j, carry):
        inner = pl.ds(pl.multiple_of(j * WIDE, LANES), WIDE)
        sums = jnp.zeros((1, WIDE), F32)
        for t in range(z.tiles):
            grad_mixed = dot(v.grad_branch[halves(t), :], p.output_weight[inner, :], 1, 1)
            back = grad_mixed * v.gate_zero[halves(t), inner]
            grad_conv[halves(t), inner] = back
            grad_gate_zero[halves(t), inner] = grad_mixed * v.conv[halves(t), inner]
            gated = v.value_part[halves(t), inner] * v.gate_one[halves(t), inner]
            sums = sums + total(back * gated)
            v.flipped[inner, halves(t)] = back.T
        small[Row.FILTER_BIAS:Row.FILTER_BIAS + 1, inner] = sums
        return carry
    lax.fori_loop(0, d // WIDE, mix_back, 0)
    slabs_from_rows(z, v.flipped, v.slabs_out.at[0])
    third = exchange(2)
    third.start()
    run(Schedule.THREE)
    def load_panel(i):
        saved = v.toeplitz_saved.at[pl.ds(pl.multiple_of(i * LANES, LANES), LANES), :]
        slot = lax.rem(i, 2)
        return pltpu.make_async_copy(saved, v.toeplitz_slots.at[slot], v.stream.at[2, slot])
    load_panel(0).start()
    def panel_of(c, k):
        i = c * z.panels + k
        load_panel(i).wait()
        @pl.when(i + 1 < z.cpd * z.panels)
        def _():
            load_panel(i + 1).start()
        return v.toeplitz_slots.at[lax.rem(i, 2)]
    def out_grad(j, carry):
        inner = pl.ds(pl.multiple_of(j * WIDE, LANES), WIDE)
        v.r_out[:, inner] = dot(v.mixed[...], v.grad_branch[:, inner], 0, 0).astype(BF16)
        return carry
    lax.fori_loop(0, d // WIDE, out_grad, 0)
    run((8,))
    run(Schedule.WAIT_THREE)
    third.wait()
    widen_slabs(z, v.slabs_in.at[0], v.wide)
    v.spread[...] = jnp.zeros(v.spread.shape, F32)
    v.grad_taps[...] = jnp.zeros(v.grad_taps.shape, F32)
    pieces = len(Schedule.PIECES)
    bounds = [z.cpd * i // pieces for i in range(pieces + 1)]
    def back_channel(c, carry):
        convolve_back_channel(z, c, v.wide, panel_of, v.kept, v.spread, v.advanced, v.back, v.fold, v.grad_taps)
        return carry
    for i in range(pieces):
        lax.fori_loop(bounds[i], bounds[i + 1], back_channel, 0)
        run(Schedule.PIECES[i])
    narrow_slabs(z, v.wide, v.slabs_out.at[1])
    fourth = exchange(3)
    fourth.start()
    run(Schedule.SENT)
    sums = Names(sum_names, [getattr(v, "s_" + name) for name in sum_names])
    filter_backward(z, p, keep, v.grad_taps, sums)
    select = own_selection(z, me)
    small[Row.FILTER:Row.NETWORK, :] = dot(sums.filter[...], select, 0, 0, HIGHEST)
    small[Row.DECAY:Row.DECAY + 1, :] = dot(sums.decay[...], select, 0, 0, HIGHEST)[0:1, :]
    half = z.filt // 2
    small[Row.NETWORK:Row.NETWORK + half, 0:z.filt] = sums.inner[0:half, :]
    small[Row.NETWORK:Row.NETWORK + half, LANES:LANES + z.filt] = sums.inner[half:, :]
    small[Row.NETWORK:Row.NETWORK + half, 2 * LANES:2 * LANES + z.filt] = sums.embed[0:half, :]
    small[Row.NETWORK:Row.NETWORK + z.erows - half, 3 * LANES:3 * LANES + z.filt] = sums.embed[half:, :]
    small[Row.EMBED_BIAS:Row.EMBED_BIAS + 1, 0:z.filt] = as_row(sums.embed_bias[...])
    small[Row.INNER_BIAS:Row.INNER_BIAS + 1, 0:z.filt] = as_row(sums.inner_bias[...])
    run(Schedule.FILTER)
    run(Schedule.WAIT_FOUR)
    fourth.wait()
    rows_from_slabs(z, v.slabs_in.at[1], v.flipped)

    def gate_back(j, carry):
        inner = pl.ds(pl.multiple_of(j * WIDE, LANES), WIDE)
        for t in range(z.tiles):
            grad_gated = v.flipped[inner, halves(t)].T + p.filter_bias[:, inner] * grad_conv[halves(t), inner]
            first_part = grad_gated * v.value_part[halves(t), inner]
            second_part = grad_gated * v.gate_one[halves(t), inner]
            v.gate_one[halves(t), inner] = first_part
            v.value_part[halves(t), inner] = second_part
            for s, value in enumerate((grad_gate_zero[halves(t), inner], first_part, second_part)):
                here = pl.ds(pl.multiple_of(s * d + j * WIDE, LANES), WIDE)
                taps = p.short_kernel
                for u in range(2):
                    r = 2 * t + u
                    lo = u * z.local
                    head = value[lo:lo + 8, :]
                    one = (taps[1:2, here] * v.keep_one[r * z.local:r * z.local + 8, 0:1]) * head
                    two = (taps[2:3, here] * v.keep_two[r * z.local:r * z.local + 8, 0:1]) * head
                    v.rim_back_out[2 * r:2 * r + 1, here] = two[0:1]
                    v.rim_back_out[2 * r + 1:2 * r + 2, here] = one[0:1] + two[1:2]
        return carry
    lax.fori_loop(0, d // WIDE, gate_back, 0)
    rim_back = pltpu.make_async_remote_copy(
        src_ref=v.rim_back_out, dst_ref=v.rim_back_in, send_sem=v.rims.at[2], recv_sem=v.rims.at[3],
        device_id=(behind,), device_id_type=MESH)
    rim_back.start()
    run(Schedule.RIM)
    grad_streams = (grad_gate_zero, v.gate_one, v.value_part)
    def short_sums(j, carry):
        inner = pl.ds(pl.multiple_of(j * WIDE, LANES), WIDE)
        for s in range(3):
            here = pl.ds(pl.multiple_of(s * d + j * WIDE, LANES), WIDE)
            acc = [jnp.zeros((1, WIDE), F32)] * 4
            for t in range(z.tiles):
                k1, k2 = v.keep_one[halves(t), 0:1], v.keep_two[halves(t), 0:1]
                values = v.projected[halves(t), here].astype(F32)
                one, two = lagged(z, values, v.rim_in, t, here)
                value = grad_streams[s][halves(t), inner]
                acc[0] = acc[0] + total(value * values)
                acc[1] = acc[1] + total(value * (k1 * one))
                acc[2] = acc[2] + total(value * (k2 * two))
                acc[3] = acc[3] + total(value)
            for i in range(3):
                small[Row.SHORT_KERNEL + 3 * i + s:Row.SHORT_KERNEL + 3 * i + s + 1, inner] = acc[i]
            small[Row.SHORT_BIAS + s:Row.SHORT_BIAS + s + 1, inner] = acc[3]
        return carry
    lax.fori_loop(0, d // WIDE, short_sums, 0)
    run(Schedule.SHORT)
    rim_back.wait()
    def spread_back(j, carry):
        inner = pl.ds(pl.multiple_of(j * WIDE, LANES), WIDE)
        row = lax.broadcasted_iota(jnp.int32, (LANES, 1), 0)
        for s in range(3):
            here = pl.ds(pl.multiple_of(s * d + j * WIDE, LANES), WIDE)
            taps = p.short_kernel
            sums = jnp.zeros((1, WIDE), F32)
            for t in range(z.tiles):
                k1, k2 = v.keep_one[halves(t), 0:1], v.keep_two[halves(t), 0:1]
                value = grad_streams[s][halves(t), inner]
                one = pltpu.roll((taps[1:2, here] * k1) * value, LANES - 1, 0)
                two = pltpu.roll((taps[2:3, here] * k2) * value, LANES - 2, 0)
                later = one + two
                for u in range(2):
                    r = 2 * t + u
                    last = (u + 1) * z.local - 1
                    far, near = v.rim_back_in[2 * r:2 * r + 1, here], v.rim_back_in[2 * r + 1:2 * r + 2, here]
                    later = jnp.where(row == last, near, jnp.where(row == last - 1, one + far, later))
                low = (taps[0:1, here] * value + later).astype(BF16)
                v.projected[halves(t), here] = low
                sums = sums + total(low.astype(F32))
            small[Row.INPUT_BIAS + s:Row.INPUT_BIAS + s + 1, inner] = sums
        return carry
    lax.fori_loop(0, d // WIDE, spread_back, 0)
    run(Schedule.SPREAD)
    for k in range(3):
        v.r_inner[k] = dot(v.normed[...], v.projected[:, k * d:(k + 1) * d], 0, 0).astype(BF16)
        run((9 + k,))
    run(Schedule.NORMAL)
    v.conv[...] = jnp.zeros((z.tokens, d), F32)
    def norm_grad(j, carry):
        here = pl.ds(pl.multiple_of(j * part, LANES), part)
        v.conv[...] += dot(v.projected[:, here], p.input_weight[:, here], 1, 1)
        return carry
    lax.fori_loop(0, 6, norm_grad, 0)
    gain_sum, shift_sum = 0.0, 0.0
    for t in range(z.tiles):
        gradient = v.conv[halves(t), :]
        unit = v.unit_one[halves(t), :]
        gain_sum = gain_sum + total(gradient * unit)
        shift_sum = shift_sum + total(gradient)
        value = v.residual[halves(t), :] + normalize_back(gradient, p.first_gain[...], unit, v.inverse_one[halves(t), 0:1])
        v.grad_tokens[halves(t), :] = value.astype(BF16)
    small[Row.FIRST_GAIN:Row.FIRST_GAIN + 1, :] = gain_sum
    small[Row.FIRST_SHIFT:Row.FIRST_SHIFT + 1, :] = shift_sum
    run((12,))

    run(Schedule.TAIL)
    while not all(flow.done for flow in flows):
        run(range(len(flows)))


class Schedule:
    ORDERS = (
        (0, 3, 1, 2, 4),
        (0, 2, 1, 3, 4),
        (0, 1, 3, 2, 4),
        (0, 2, 1, 3, 4),
        (0, 2, 1, 3, 4),
        (0, 1, 3, 2, 4),
        (0, 3, 1, 2, 4),
        (0, 1, 2, 3, 4),
        (0, 1, 3, 2, 4),
        (0, 3, 2, 1, 4),
        (0, 2, 1, 3, 4),
        (0, 1, 2, 3, 4),
        (0, 2, 1, 3, 4),
    )
    MLP = (
        (0, 4,),
        (),
        (5,),
    )
    THREE = (1, 2, 6, 0, 4, 3, 7, 5,)
    WAIT_THREE = (8,)
    SENT = (7, 0, 5, 1, 4, 2, 6, 8,)
    FILTER = (7, 3, 0,)
    WAIT_FOUR = (5, 1, 2,)
    RIM = (6, 4, 0, 8, 7, 3,)
    SHORT = (5, 4, 1, 2,)
    SPREAD = ()
    NORMAL = (9, 5, 4,)
    TAIL = (
        10, 11, 0, 5, 4, 2, 12, 0, 6, 2, 8, 9, 10, 7, 11, 3, 12, 6, 1, 10, 9, 8, 3, 12,
        1, 10, 11, 9, 7, 3, 6, 12, 1, 10, 11, 9, 7, 12, 3, 10, 11, 9, 12, 10, 8, 1, 11, 12,
        6, 1, 7, 9, 8, 7, 11, 3, 10, 3, 12, 9, 6, 11, 6, 8, 8, 9, 10, 9, 12, 11, 10, 12,
        11,
    )
    PIECES = (
        (1, 2,),
        (6, 0,),
        (5, 3, 4, 0, 2,),
        (5, 4,),
        (7, 2, 0, 5,),
        (4, 2, 8,),
        (),
        (),
    )


def part_shapes(z):
    d = z.width
    return dict(down=((4, d, d), BF16), up=((4, d, d), BF16), out=((d, d), BF16), inner=((3, d, d), BF16), small=((Row.TOTAL, d), F32))


def part_plans(z):
    bits = [1 << i for i in range(z.n.bit_length() - 1)]
    plans = []
    for i, order in enumerate(Schedule.ORDERS):
        ordered = [bits[k] for k in order] + bits[len(order):] if len(bits) >= len(order) else bits
        rows = Row.TOTAL if i == len(Schedule.ORDERS) - 1 else z.width
        plans.append(halving_plan(rows, z.width, ordered, 8))
    return plans


def part_inboxes(z, v, i):
    d = z.width
    if i < 8:
        box = v.pool.at[pl.ds((i // 2) * d, d), pl.ds((i % 2) * d, d)]
    elif i < 12:
        box = v.boxes.at[i - 8]
    else:
        box = v.small_box
    views, row, column = [], 0, 0
    for _, _, rows, columns in z.plans[i]:
        views.append(box.at[pl.ds(row, rows), pl.ds(column, columns)])
        if columns == d:
            row += rows
        else:
            column += columns
            if column == d:
                row, column = row + rows, 0
    return views


def block(z, inputs, collective_id=0):
    d, f = z.width, z.hidden
    shapes = part_shapes(z)
    keep = keep_shapes(z)
    sums = sum_shapes(z)
    names, specs = [], []
    any_space = pl.BlockSpec(memory_space=pl.ANY)
    for name in inputs:
        names.append(name)
        specs.append(pl.BlockSpec(memory_space=pltpu.SMEM) if name == "doc_lengths" else any_space)
    outs = dict(output=((z.tokens, d), BF16), grad_tokens=((z.tokens, d), BF16))
    for name in shapes:
        outs["r_" + name] = shapes[name]
    pool = (z.cpd * z.panels * LANES, z.panel)
    saved = "toeplitz_saved"
    outs[saved] = (pool, BF16)
    scratch = {}
    fetched = tuple(name for name in inputs if name not in ("doc_lengths", "up_weight", "down_weight"))
    for name in fetched:
        shape = inputs[name].shape
        scratch["v_" + name] = pltpu.VMEM(shape if len(shape) > 1 else (1,) + shape, inputs[name].dtype)
    t = z.tokens
    buffers = dict(
        unit_one=((t, d), F32), inverse_one=((t, LANES), F32), normed=((t, d), BF16), projected=((t, 3 * d), BF16),
        rim_out=((8, 3 * d), F32), rim_in=((8, 3 * d), F32), rim_back_out=((8, 3 * d), F32), rim_back_in=((8, 3 * d), F32),
        keep_one=((t, LANES), F32), keep_two=((t, LANES), F32),
        gate_zero=((t, d), F32), gate_one=((t, d), F32), value_part=((t, d), F32),
        flipped=((d + 8, t), F32), slabs_out=((2, z.n, 2 * z.cpad, LANES), BF16), slabs_in=((2, z.n, 2 * z.cpad, LANES), BF16),
        wide=((z.n * 2 * z.cpad, LANES), F32), spread=((4, 2 * z.nb, LANES), F32), kept=((z.cpd, 4 * z.nb, LANES), BF16),
        pool=(pool, BF16),
        conv=((t, d), F32), mixed=((t, d), BF16), unit_two=((t, d), F32), inverse_two=((t, LANES), F32),
        normed_two=((t, d), BF16), residual=((t, d), F32), grad_normed=((t, d), F32),
        up_slots=((2, d, z.block), BF16), down_slots=((2, z.block, d), BF16), up_sums=((1, f), F32),
        grad_branch=((t, d), BF16), toeplitz_slots=((2, LANES, z.panel), BF16), back=((4 * z.nb, LANES), F32), fold=((8, z.length), F32),
        advanced=((4 * z.nb, z.panel), BF16), grad_taps=((z.cpad, z.length), F32),
    )
    for name, (shape, kind) in buffers.items():
        scratch[name] = pltpu.VMEM(shape, kind)
    for name in keep:
        scratch["k_" + name] = pltpu.VMEM(keep[name], F32)
    for name in sums:
        scratch["s_" + name] = pltpu.VMEM(sums[name], F32)
    steps, count = len(z.plans[0]), len(z.plans)
    scratch.update(
        boxes=pltpu.VMEM((4, d, d), BF16), small_box=pltpu.VMEM((Row.TOTAL + 8, d), F32),
        part_sends=pltpu.SemaphoreType.DMA((count, 2 * steps)), part_arrivals=pltpu.SemaphoreType.DMA((count, 2 * steps)),
        part_free=pltpu.SemaphoreType.REGULAR((count, steps)),
        loads=pltpu.SemaphoreType.DMA((len(fetched),)), stream=pltpu.SemaphoreType.DMA((3, 2)),
        saves=pltpu.SemaphoreType.DMA((1,)), rims=pltpu.SemaphoreType.DMA((4,)),
        sends=pltpu.SemaphoreType.DMA((4, z.n)), arrivals=pltpu.SemaphoreType.DMA((4, z.n)),
    )
    order = (tuple(names), tuple(outs), tuple(scratch), fetched, tuple(keep), tuple(sums))
    results = pl.pallas_call(
        functools.partial(block_kernel, z, order),
        out_shape=[jax.ShapeDtypeStruct(*outs[name]) if name == saved else pltpu.VMEM(*outs[name]) for name in outs],
        in_specs=specs,
        out_specs=[any_space if name == saved else pl.BlockSpec(memory_space=pltpu.VMEM) for name in outs],
        scratch_shapes=list(scratch.values()),
        compiler_params=pltpu.CompilerParams(collective_id=collective_id, has_side_effects=True, vmem_limit_bytes=47 << 20),
        name="hyena_block",
    )(*inputs.values())
    return dict(zip(outs, results))


def finish_layout(z):
    d, f = z.width, z.hidden
    return dict(
        grad_down_weight=((f, d), [("down", i, i * d, 0) for i in range(4)]),
        grad_up_weight=((d, f), [("up", i, 0, i * d) for i in range(4)]),
        grad_output_weight=((d, d), [("out", None, 0, 0)]),
        grad_input_weight=((d, 3 * d), [("inner", i, 0, i * d) for i in range(3)]),
    )


def small_layout(z):
    d, half = z.width, z.filt // 2
    def line(row, count=1):
        return (count * d,), [(row + i, 0, 1, d, 0, i * d) for i in range(count)]
    def short(row):
        return (z.filt,), [(row, 0, 1, z.filt, 0, 0)]
    return dict(
        grad_first_gain=line(Row.FIRST_GAIN), grad_first_shift=line(Row.FIRST_SHIFT), grad_input_bias=line(Row.INPUT_BIAS, 3),
        grad_short_kernel=((3, 3 * d), [(Row.SHORT_KERNEL + 3 * i + s, 0, 1, d, i, s * d) for i in range(3) for s in range(3)]),
        grad_short_bias=line(Row.SHORT_BIAS, 3),
        grad_embed_weight=((z.emb, z.filt), [
            (Row.NETWORK, 2 * LANES, half, z.filt, 0, 0), (Row.NETWORK, 3 * LANES, z.emb - half, z.filt, half, 0)]),
        grad_embed_bias=short(Row.EMBED_BIAS),
        grad_inner_weight=((z.filt, z.filt), [
            (Row.NETWORK, 0, half, z.filt, 0, 0), (Row.NETWORK, LANES, half, z.filt, half, 0)]),
        grad_inner_bias=short(Row.INNER_BIAS),
        grad_filter_weight=((z.filt, d), [(Row.FILTER, 0, z.filt, d, 0, 0)]),
        grad_decay_rates=line(Row.DECAY), grad_filter_bias=line(Row.FILTER_BIAS), grad_output_bias=line(Row.OUTPUT_BIAS),
        grad_second_gain=line(Row.SECOND_GAIN), grad_second_shift=line(Row.SECOND_SHIFT),
        grad_up_bias=line(Row.UP_BIAS, z.hidden // d), grad_down_bias=line(Row.DOWN_BIAS),
    )


RUN = 384


def finish_kernel(z, order, pieces, *refs):
    weights, little, names = order
    v = Names(names, refs)
    stores = []
    landed = []
    for i, (part, index, name, row, column, at, rows, columns) in enumerate(pieces):
        source = getattr(v, "r_" + part)
        landed.append(source if index is None else source.at[index])
        wide, out = getattr(v, "w_" + name), getattr(v, name)
        there = (pl.ds(row, rows), pl.ds(column, columns))
        stores.append(pltpu.make_async_copy(wide.at[there], out.at[there], v.stores.at[i]))
    others = [
        pltpu.make_async_copy(v.block_output, v.output, v.others.at[0]),
        pltpu.make_async_copy(v.block_grad_tokens, v.grad_tokens, v.others.at[1]),
    ]
    for copy in others:
        copy.start()
    for i, (part, index, name, row, column, at, rows, columns) in enumerate(pieces):
        getattr(v, "w_" + name)[row:row + rows, column:column + columns] = landed[i][at:at + rows, :].astype(F32)
        stores[i].start()
    for name, (shape, moves) in small_layout(z).items():
        out = getattr(v, name)
        for row, column, rows, columns, to_row, to_column in moves:
            value = v.r_small[row:row + rows, column:column + columns]
            if len(shape) == 1:
                out[to_column:to_column + columns] = value.reshape(columns)
            else:
                out[to_row:to_row + rows, to_column:to_column + columns] = value
    for copy in stores + others:
        copy.wait()


def finish(z, results):
    layout, little = finish_layout(z), small_layout(z)
    shapes = part_shapes(z)
    pieces = []
    for name in layout:
        for part, index, row, column in layout[name][1]:
            rows, columns = shapes[part][0][-2:]
            for at in range(0, rows, RUN):
                pieces.append((part, index, name, row + at, column, at, min(RUN, rows - at), columns))
    any_space, vmem = pl.BlockSpec(memory_space=pl.ANY), pl.BlockSpec(memory_space=pltpu.VMEM)
    arguments = dict(("r_" + part, results["r_" + part]) for part in shapes)
    arguments.update(block_output=results["output"], block_grad_tokens=results["grad_tokens"])
    arguments = dict((name, pltpu.with_memory_space_constraint(value, pltpu.VMEM)) for name, value in arguments.items())
    outs = dict((name, jax.ShapeDtypeStruct(layout[name][0], F32)) for name in layout)
    token_shape = jax.ShapeDtypeStruct((z.tokens, z.width), BF16)
    outs.update(output=token_shape, grad_tokens=token_shape)
    outs.update((name, jax.ShapeDtypeStruct(little[name][0], F32)) for name in little)
    scratch = dict(("w_" + name, pltpu.VMEM(layout[name][0], F32)) for name in layout)
    scratch.update(
        stores=pltpu.SemaphoreType.DMA((len(pieces),)), others=pltpu.SemaphoreType.DMA((2,))
    )
    names = tuple(arguments) + tuple(outs) + tuple(scratch)
    outputs = pl.pallas_call(
        functools.partial(finish_kernel, z, (tuple(layout), tuple(little), names), pieces),
        out_shape=list(outs.values()),
        in_specs=[vmem] * len(arguments),
        out_specs=[any_space] * (len(layout) + 2) + [vmem] * len(little),
        scratch_shapes=list(scratch.values()),
        compiler_params=pltpu.CompilerParams(vmem_limit_bytes=30 << 20),
        name="widen_gradients",
    )(*arguments.values())
    return Names(outs, outputs)


def shards(
    n, tokens, doc_lengths, first_gain, first_shift, input_weight, input_bias, short_kernel, short_bias, embed_weight, embed_bias,
    inner_weight, inner_bias, filter_weight, decay_rates, filter_bias, output_weight, output_bias, second_gain, second_shift,
    up_weight, up_bias, down_weight, down_bias, cotangent,
):
    rows, local, width = tokens.shape
    z = Sizes(n, rows, local, width, *embed_weight.shape, up_weight.shape[1])
    z.plans = part_plans(z)
    inputs = dict(
        tokens=tokens.reshape(rows * local, width), doc_lengths=doc_lengths, first_gain=first_gain, first_shift=first_shift,
        input_weight=input_weight, input_bias=input_bias, short_kernel=short_kernel, short_bias=short_bias, embed_weight=embed_weight,
        embed_bias=embed_bias, inner_weight=inner_weight, inner_bias=inner_bias, filter_weight=filter_weight, decay_rates=decay_rates,
        filter_bias=filter_bias, output_weight=output_weight, output_bias=output_bias, second_gain=second_gain,
        second_shift=second_shift, up_weight=up_weight, up_bias=up_bias, down_weight=down_weight, down_bias=down_bias,
        cotangent=cotangent.reshape(rows * local, width),
    )
    o = finish(z, block(z, inputs))
    return (
        o.output.reshape(tokens.shape), o.grad_tokens.reshape(tokens.shape), o.grad_first_gain, o.grad_first_shift, o.grad_input_weight,
        o.grad_input_bias, o.grad_short_kernel, o.grad_short_bias, o.grad_embed_weight, o.grad_embed_bias, o.grad_inner_weight,
        o.grad_inner_bias, o.grad_filter_weight, o.grad_decay_rates, o.grad_filter_bias, o.grad_output_weight, o.grad_output_bias,
        o.grad_second_gain, o.grad_second_shift, o.grad_up_weight, o.grad_up_bias, o.grad_down_weight, o.grad_down_bias,
    )


def solution(mesh):
    split, whole = P(None, "seq", None), P()
    return jax.shard_map(
        functools.partial(shards, mesh.shape["seq"]),
        mesh=mesh,
        in_specs=(split,) + (whole,) * 22 + (split,),
        out_specs=(split, split) + (whole,) * 21,
        check_vma=False,
    )
```
